512 devices in a mesh: box: 64 (over y, z), angle: 8 (over x, core).
Axes of the slice: x: 4, y: 8, z: 8, core: 2. Of those that a mesh axis runs over, the one named last changes fastest.
Arguments:
- child_field: bfloat16 [4096, 2, 64, 128], P('box', None, 'angle'), may hold values from -6 to 6
- child_list: int32 [4096, 8], P('box'), may hold values from -1 to 4095, as said below
- child_op: int32 [4096, 8], P('box'), may hold values from 0 to 39
- child_home: int32 [4096], replicated, may hold values from 0 to 4095, as said below
- child_ops: bfloat16 [40, 2, 64, 128], P(None, None, 'angle'), may hold values from -2 to 2
- parent_list: int32 [1024, 8], P('box'), may hold values from -1 to 1023, as said below
- parent_op: int32 [1024, 8], P('box'), may hold values from 0 to 39
- parent_home: int32 [1024], replicated, may hold values from 0 to 1023, as said below
- parent_ops: bfloat16 [40, 2, 128, 256], P(None, None, 'angle'), may hold values from -2 to 2
Outputs:
- child_out: bfloat16 [4096, 2, 64, 128], P('box', None, 'angle')
The draws below stay inside these ranges and needn't reach their ends.
Inputs may be any that keep to these rules, and one draw needn't show every extreme that they name: `child_list`: entries are child box ids, or -1 for an empty slot. Among the list rows held by one index of box, at most 8 entries name boxes whose row child_home lies on one index of box (row // 64); some pair of indices reaches 8 in every draw. Entries may repeat. A permutation: child box i is held in row child_home[i]. `parent_list`: entries are parent box ids, or -1 for an empty slot. Among the list rows held by one index of box, at most 2 entries name boxes whose row parent_home lies on one index of box (row // 16); some pair of indices reaches 2 in every draw. Entries may repeat. A permutation: parent box i is held in row parent_home[i].
All inputs are finite; a program needn't handle non-finite values.
Results may differ from the reference program's by a relative error of at most 0.0017.
The reference program's roundings to bfloat16 on the way (of `stretched`, `parent_field`, `parent_far`, `turned`, `narrowed` and `child_term`) count: a program that leaves them out, or rounds other values in their place, can miss the bound.
Values may be sent and summed in bfloat16 or wider, within the bound.
No kernel may reach another device: no remote copies, remote signals or barrier semaphores. Data moves between devices by JAX's collectives and lax.ppermute only.
A program may use at most 64 MiB of HBM per device.

```python
import math
import jax
import jax.numpy as jnp
from jax import lax

CT = 64
SUBBOX_HEADINGS = 128
PT = 128
PP = 256
KIDS = 4
NOPS1 = 40
NOPS2 = 40
L1 = 8
L2 = 8
CB = 64
PB = 16
CHILDREN = 4096
PARENTS = 1024


def home_table(key, salt_value, total_rows):
    return jax.random.permutation(jax.random.fold_in(key, salt_value), total_rows).astype(jnp.int32)


def build_lists(key, salt_value, total_rows, rows_device, list_slots):
    home_rows = home_table(key, salt_value, total_rows)
    owners = total_rows // rows_device
    per_device = rows_device * list_slots
    capacity = per_device // owners
    inverse = jnp.argsort(home_rows).astype(jnp.int32)
    base_key = jax.random.fold_in(key, salt_value + 100)
    level_key, count_key, chosen_key, shuffle_key, corner_key = jax.random.split(base_key, 5)
    loading = jax.random.randint(level_key, (owners, 1), 3, 5)
    ceiling = loading * capacity // 4
    counts = jax.random.randint(count_key, (owners, owners), ceiling // 2, ceiling + 1)
    corner = jax.random.randint(corner_key, (2,), 0, owners)
    rows_grid = lax.broadcasted_iota(jnp.int32, (owners, owners), 0)
    cols_grid = lax.broadcasted_iota(jnp.int32, (owners, owners), 1)
    counts = jnp.where((rows_grid == corner[0]) & (cols_grid == corner[1]), capacity, counts)
    slot_index = jnp.arange(per_device, dtype=jnp.int32)
    owner_of = slot_index // capacity
    filled = (slot_index % capacity)[None, :] < counts[:, owner_of]
    chosen = jax.random.randint(chosen_key, (owners, per_device), 0, rows_device)
    box_ids = inverse[owner_of[None, :] * rows_device + chosen]
    entries = jnp.where(filled, box_ids, -1)
    scores = jax.random.randint(shuffle_key, (owners, per_device), 0, 1 << 16) * per_device + slot_index[None, :]
    shuffle = jnp.argsort(scores, axis=1)
    entries = jnp.take_along_axis(entries, shuffle, axis=1)
    return entries.reshape(owners * rows_device, list_slots).astype(jnp.int32)


def draw_child_field(key, part):
    field_key = jax.random.fold_in(key, 7)
    noise_key, amp_key, wave_key, phase_key = jax.random.split(field_key, 4)
    full_shape = (CHILDREN, 2, CT, SUBBOX_HEADINGS)
    stochastic_jitter = jnp.clip(jax.random.normal(noise_key, full_shape, jnp.float32), -3.5, 3.5)
    radiated_magnitude = jax.random.uniform(amp_key, (CHILDREN, 2, 1, 1), jnp.float32, -2.4, 2.4)
    oscillation_multiplier = jax.random.randint(wave_key, (CHILDREN, 2, 1, 1), 0, 4).astype(jnp.float32)
    cyclic_offset = jax.random.uniform(phase_key, (CHILDREN, 2, 1, 1), jnp.float32, -math.pi, math.pi)
    polar = (jnp.arange(CT, dtype=jnp.float32) + 0.5) * (math.pi / CT)
    bounding_profile = (jnp.sin(polar) ** 4)[None, None, :, None]
    heading_radians = jnp.arange(SUBBOX_HEADINGS, dtype=jnp.float32)[None, None, None, :]
    toggling_parity = (1 - 2 * (jnp.arange(SUBBOX_HEADINGS, dtype=jnp.int32) % 2)).astype(jnp.float32)[None, None, None, :]
    oscillating_tone = toggling_parity * jnp.cos(2.0 * math.pi / SUBBOX_HEADINGS * oscillation_multiplier * heading_radians + cyclic_offset)
    return (stochastic_jitter + radiated_magnitude * bounding_profile * oscillating_tone).astype(jnp.bfloat16)


def draw_child_home(key, part):
    return home_table(key, 1, CHILDREN)


def draw_child_list(key, part):
    return build_lists(key, 1, CHILDREN, CB, L1)


def draw_parent_home(key, part):
    return home_table(key, 2, PARENTS)


def draw_parent_list(key, part):
    return build_lists(key, 2, PARENTS, PB, L2)


def plant(array, rng, least, largest):
    longest = array.shape.index(max(array.shape))
    spots = []
    for shift in (0, 1):
        where = [jax.random.randint(jax.random.fold_in(rng, axis), (), 0, length) for axis, length in enumerate(array.shape)]
        where[longest] = (where[longest] + shift) % array.shape[longest]
        spots.append(tuple(where))
    return array.at[spots[0]].set(least).at[spots[1]].set(largest)


def levels(stream_key, dims, shards, smallest, high):
    def one(dim, shards_of):
        draws = jax.random.uniform(jax.random.fold_in(jax.random.fold_in(stream_key, 6), dim), (shards_of,), jnp.float32, smallest / len(shards), high / len(shards))
        return jnp.repeat(jnp.exp(draws), dims[dim] // shards_of).reshape((-1,) + (1,) * (len(dims) - dim - 1))

    factor_of = one(*shards[0])
    for cut in shards[1:]:
        factor_of = factor_of * one(*cut)
    return factor_of


def normal_values(rng, shape, spread, reach, cuts=(), held_as=jnp.bfloat16):
    values = spread * jax.random.normal(rng, shape, jnp.float32)
    if cuts:
        values = values * levels(rng, shape, cuts, -0.22, 0.18)
    return jnp.clip(values, -reach, reach).astype(held_as)


def setup_inputs(seed: int = 0) -> dict:
    seeds = jax.random.split(jax.random.key(seed), 10)
    return {
        "child_field": draw_child_field(jax.random.fold_in(seeds[9], 71), 0),
        "child_list": draw_child_list(jax.random.fold_in(seeds[9], 71), 0),
        "child_op": plant(jax.random.randint(seeds[2], (CHILDREN, L1), 0, NOPS1), jax.random.fold_in(seeds[2], 1), 0, NOPS1 - 1).astype(jnp.int32),
        "child_home": draw_child_home(jax.random.fold_in(seeds[9], 71), 0),
        "child_ops": normal_values(seeds[4], (NOPS1, 2, CT, SUBBOX_HEADINGS), L1 ** -0.5, 2.0, ((2, 8),)),
        "parent_list": draw_parent_list(jax.random.fold_in(seeds[9], 71), 0),
        "parent_op": plant(jax.random.randint(seeds[6], (PARENTS, L2), 0, NOPS2), jax.random.fold_in(seeds[6], 1), 0, NOPS2 - 1).astype(jnp.int32),
        "parent_home": draw_parent_home(jax.random.fold_in(seeds[9], 71), 0),
        "parent_ops": normal_values(seeds[8], (NOPS2, 2, PT, PP), L2 ** -0.5, 2.0, ((2, 8),)),
    }


WAVE_NUMBER = 6.0


def fourier_table(fine_count, coarse_count, offset):
    fine_pos = (jnp.arange(fine_count, dtype=jnp.float32) + offset) / fine_count
    coarse_pos = (jnp.arange(coarse_count, dtype=jnp.float32) + offset) / coarse_count
    distance = fine_pos[:, None] - coarse_pos[None, :]
    harmonic = jnp.arange(1, coarse_count // 2, dtype=jnp.float32)
    cosines = jnp.cos((2.0 * math.pi) * harmonic[None, None, :] * distance[:, :, None])
    summed = 1.0 + 2.0 * jnp.sum(cosines, axis=2) + jnp.cos(math.pi * coarse_count * distance)
    return summed / coarse_count


def shift_parts(polar_rows):
    polar_angle = math.pi * (polar_rows.astype(jnp.float32) + 0.5) / PT
    heading_radians = (2.0 * math.pi / PP) * jnp.arange(PP, dtype=jnp.float32)
    kid_index = jnp.arange(KIDS, dtype=jnp.int32)
    side_x = (2 * (kid_index % 2) - 1).astype(jnp.float32)
    side_y = (2 * ((kid_index // 2) % 2) - 1).astype(jnp.float32)
    across = side_x[:, None] * jnp.cos(heading_radians)[None, :] + side_y[:, None] * jnp.sin(heading_radians)[None, :]
    phase_arg = WAVE_NUMBER * jnp.sin(polar_angle)[None, :, None] * across[:, None, :]
    return jnp.cos(phase_arg), jnp.sin(phase_arg)


def lift_sum(widened, cos_part, sin_part):
    real_part = jnp.sum(cos_part * widened[..., 0, :, :] - sin_part * widened[..., 1, :, :], axis=-3)
    imag_part = jnp.sum(cos_part * widened[..., 1, :, :] + sin_part * widened[..., 0, :, :], axis=-3)
    return jnp.stack([real_part, imag_part], axis=-3).astype(jnp.bfloat16)


def lower_turn(parents, cos_part, sin_part):
    real_in = jnp.expand_dims(parents[..., 0, :, :].astype(jnp.float32), -3)
    imag_in = jnp.expand_dims(parents[..., 1, :, :].astype(jnp.float32), -3)
    real_out = cos_part * real_in + sin_part * imag_in
    imag_out = cos_part * imag_in - sin_part * real_in
    return jnp.stack([real_out, imag_out], axis=-3).astype(jnp.bfloat16)


def far_sum(patterns, far_lists, op_index, home_rows, op_table, block_rows):
    blocks = far_lists.shape[0] // block_rows
    slot_count = far_lists.shape[1]

    def per_block(block_pair):
        box_ids, op_rows = block_pair
        usable = box_ids >= 0
        source = patterns[home_rows[jnp.where(usable, box_ids, 0)]].astype(jnp.float32)
        translator = op_table[op_rows].astype(jnp.float32)
        weight = usable.astype(jnp.float32)[:, :, None, None]
        real_part = jnp.sum(weight * (translator[:, :, 0] * source[:, :, 0] - translator[:, :, 1] * source[:, :, 1]), axis=1)
        imag_part = jnp.sum(weight * (translator[:, :, 0] * source[:, :, 1] + translator[:, :, 1] * source[:, :, 0]), axis=1)
        return jnp.stack([real_part, imag_part], axis=1)

    summed = lax.map(per_block, (far_lists.reshape(blocks, block_rows, slot_count), op_index.reshape(blocks, block_rows, slot_count)))
    return summed.reshape((far_lists.shape[0],) + patterns.shape[1:])


def reference(child_field, child_list, child_op, child_home, child_ops, parent_list, parent_op, parent_home, parent_ops):
    child_far = far_sum(child_field, child_list, child_op, child_home, child_ops, CB)
    theta_up = fourier_table(PT, CT, 0.5).astype(jnp.bfloat16)
    phi_up = fourier_table(PP, SUBBOX_HEADINGS, 0.0).T.astype(jnp.bfloat16)
    theta_down = (fourier_table(PT, CT, 0.5).T * (CT / PT)).astype(jnp.bfloat16)
    phi_down = (fourier_table(PP, SUBBOX_HEADINGS, 0.0) * (SUBBOX_HEADINGS / PP)).astype(jnp.bfloat16)
    cos_part, sin_part = shift_parts(jnp.arange(PT, dtype=jnp.int32))
    blocks = PARENTS // PB
    grouped = child_field.reshape(blocks, PB, KIDS, 2, CT, SUBBOX_HEADINGS)

    def lift_block(kid_block):
        stretched = jnp.einsum("ut,qkctp->qkcup", theta_up.astype(jnp.float32), kid_block.astype(jnp.float32), precision=lax.Precision.HIGHEST).astype(jnp.bfloat16)
        widened = jnp.einsum("qkcup,pv->qkcuv", stretched.astype(jnp.float32), phi_up.astype(jnp.float32), precision=lax.Precision.HIGHEST)
        return lift_sum(widened, cos_part, sin_part)

    parent_field = lax.map(lift_block, grouped).reshape(PARENTS, 2, PT, PP)
    parent_far = far_sum(parent_field, parent_list, parent_op, parent_home, parent_ops, PB).astype(jnp.bfloat16)

    def lower_block(parents):
        turned = lower_turn(parents, cos_part, sin_part)
        narrowed = jnp.einsum("qkcuv,vp->qkcup", turned.astype(jnp.float32), phi_down.astype(jnp.float32), precision=lax.Precision.HIGHEST).astype(jnp.bfloat16)
        terms = jnp.einsum("tu,qkcup->qkctp", theta_down.astype(jnp.float32), narrowed.astype(jnp.float32), precision=lax.Precision.HIGHEST)
        return terms.astype(jnp.bfloat16)

    child_term = lax.map(lower_block, parent_far.reshape(blocks, PB, 2, PT, PP)).reshape(CHILDREN, 2, CT, SUBBOX_HEADINGS)
    child_term = lax.optimization_barrier(child_term)
    return (child_far + child_term.astype(jnp.float32)).astype(jnp.bfloat16)
```

```python
import functools
import math

import jax
import jax.numpy as jnp
import numpy as np
from jax import lax
from jax.experimental import pallas as pl
from jax.experimental.pallas import tpu as pltpu
from jax.sharding import PartitionSpec as P

CT = 64
SUBBOX_HEADINGS = 128
PT = 128
PP = 256
KIDS = 4
WAVE_NUMBER = 6.0
SIDE = 8
BOTH = ("box", "angle")
F32, BF16, I32 = jnp.float32, jnp.bfloat16, jnp.int32
VM = pltpu.VMEM
ANY = pl.ANY


def fourier_table(fine_count, coarse_count, offset):
    f32 = np.float32
    fine = (np.arange(fine_count, dtype=f32) + f32(offset)) / f32(fine_count)
    coarse = (np.arange(coarse_count, dtype=f32) + f32(offset)) / f32(coarse_count)
    x = fine[:, None] - coarse[None, :]
    harmonic = np.arange(1, coarse_count // 2, dtype=f32)
    cosines = np.cos(f32(2.0 * math.pi) * harmonic * x[:, :, None])
    summed = f32(1.0) + f32(2.0) * cosines.sum(2, dtype=np.float64) + np.cos(f32(math.pi * coarse_count) * x)
    return (summed / coarse_count).astype(f32)


def shift_tables():
    f32 = np.float32
    polar = (f32(math.pi) * (np.arange(PT, dtype=f32) + f32(0.5)) / f32(PT)).astype(f32)
    heading = (f32(2.0 * math.pi / PP) * np.arange(PP, dtype=f32)).astype(f32)
    cos_h, sin_h = np.cos(heading), np.sin(heading)
    across = np.stack([-cos_h - sin_h, cos_h - sin_h])
    arg = (f32(WAVE_NUMBER) * np.sin(polar))[None, :, None] * across[:, None, :]
    return np.cos(arg).astype(f32), np.sin(arg).astype(f32)


def bmm(a, b):
    return lax.dot_general(a, b, (((1,), (0,)), ((), ())), preferred_element_type=F32)


def iota(shape, dim):
    return lax.broadcasted_iota(I32, shape, dim)


def plan_level(ids_ref, op_ref, home_ref, core, mine, rows_device, cap, empty_op, code_ref):
    slots, rows = ids_ref.shape
    home = home_ref[...]
    owner = home // rows_device
    table = jnp.concatenate([owner, home - owner * rows_device], axis=0).astype(F32).astype(BF16)
    highs = home.shape[0]
    before = (iota((rows, rows), 0) < iota((rows, rows), 1)).astype(F32).astype(BF16)
    carry = jnp.zeros((SIDE, 1), F32)
    wanted = jnp.zeros((2 * SIDE, cap), F32)
    for j in range(slots):
        ids = ids_ref[pl.ds(j, 1), :]
        usable = ids >= 0
        safe = jnp.maximum(ids, 0)
        high, low = safe >> 7, safe & 127
        low_hot = (iota((128, rows), 0) == low).astype(F32).astype(BF16)
        picked = bmm(table, low_hot)
        high_hot = (iota((highs, rows), 0) == high).astype(F32)
        own = jnp.sum(picked[:highs] * high_hot, axis=0, keepdims=True).astype(I32)
        loc = jnp.sum(picked[highs:] * high_hot, axis=0, keepdims=True)
        along_y, along_z = own >> 3, own & 7
        column = jnp.where(core == 0, along_z, along_y)
        place = (jnp.where(core == 0, along_y, along_z) - mine) & 7
        hot = jnp.where((iota((SIDE, rows), 0) == column) & usable, 1.0, 0.0)
        hot_b = hot.astype(BF16)
        prefix = bmm(hot_b, before) + carry
        carry = carry + jnp.sum(hot, axis=1, keepdims=True)
        rank = jnp.sum(hot * prefix, axis=0, keepdims=True).astype(I32)
        position = column * cap + rank
        code_ref[pl.ds(j, 1), pl.ds(0, rows)] = jnp.where(
            usable, position * 64 + op_ref[pl.ds(j, 1), :], empty_op
        )
        rank_hot = (iota((cap, rows), 0) == rank).astype(F32).astype(BF16)
        both = jnp.concatenate([hot * place.astype(F32), hot * loc], axis=0).astype(BF16)
        wanted = wanted + lax.dot_general(
            both, rank_hot, (((1,), (1,)), ((), ())), preferred_element_type=F32
        )
    return (wanted[:SIDE] * rows_device + wanted[SIDE:]).astype(I32)


def plan_body(where, cl, co, ch, plist, po, ph, want_ref, ccode_ref, pcode_ref):
    core, mine = where[0], where[1]
    want_ref[...] = jnp.zeros(want_ref.shape, I32)
    want_ref[:, pl.ds(0, 64)] = plan_level(cl, co, ch, core, mine, 64, 64, 40, ccode_ref)
    want_ref[:, pl.ds(64, 16)] = plan_level(plist, po, ph, core, mine, 16, 16, 40, pcode_ref)


def plan(where, child_list, child_op, child_home, parent_list, parent_op, parent_home):
    args = (
        where,
        child_list.T,
        child_op.T,
        child_home.reshape(-1, 128),
        parent_list.T,
        parent_op.T,
        parent_home.reshape(-1, 128),
    )
    return pl.pallas_call(
        plan_body,
        out_shape=(
            jax.ShapeDtypeStruct((SIDE, 128), I32),
            jax.ShapeDtypeStruct((8, 64), I32),
            jax.ShapeDtypeStruct((8, 16), I32),
        ),
        in_specs=[pl.BlockSpec(memory_space=pltpu.SMEM)] + [pl.BlockSpec(memory_space=VM)] * 6,
        out_specs=(pl.BlockSpec(memory_space=VM),) * 3,
        name="plan",
    )(*args)


def up_body(field, theta, phi, cos_t, sin_t, out, wide):
    for r in range(8):
        for c in range(2):
            rows = jnp.concatenate([field[s, r, c] for s in range(8)], axis=0)
            stretched = bmm(theta[...], rows).astype(BF16)
            wide[r * 2 + c] = bmm(stretched, phi[...])
    for q in range(2):
        for u in range(PT // 8):
            at = pl.ds(u * 8, 8)
            w = [[wide[(q * 4 + k) * 2 + c, at, :] for c in range(2)] for k in range(4)]
            real = jnp.zeros((8, PP), F32)
            imag = jnp.zeros((8, PP), F32)
            for t, (k, m) in enumerate(((0, 3), (1, 2))):
                cs, sn = cos_t[t, at, :], sin_t[t, at, :]
                real = real + cs * (w[k][0] + w[m][0]) - sn * (w[k][1] - w[m][1])
                imag = imag + cs * (w[k][1] + w[m][1]) + sn * (w[k][0] - w[m][0])
            for c, part in enumerate((real, imag)):
                part = part.astype(BF16)
                for v in range(2):
                    out[u // 2, q, c * 4 + (u % 2) * 2 + v] = part[:, v * 128 : (v + 1) * 128]


def lift(field, theta, phi, cos_t, sin_t):
    return pl.pallas_call(
        up_body,
        out_shape=jax.ShapeDtypeStruct((8, 2, 8, 8, 128), BF16),
        in_specs=[pl.BlockSpec(memory_space=VM)] * 5,
        out_specs=pl.BlockSpec(memory_space=VM),
        scratch_shapes=[pltpu.VMEM((16, PT, PP), F32)],
        name="lift",
    )(field, theta, phi, cos_t, sin_t)


def select_body(first, rows, tiles, asked, *refs):
    blocks, out, pool, sems = refs[:8], refs[8], refs[9], refs[10]
    count = rows * tiles
    copies = [
        pltpu.make_async_copy(b.at[pl.ds(first[1], count)], pool.at[pl.ds(i * count, count)], sems.at[i])
        for i, b in enumerate(blocks)
    ]
    for copy in copies:
        copy.start()
    for copy in copies:
        copy.wait()
    per_peer = out.shape[1]

    def step(h, carry):
        for k in range(per_peer):
            row = asked[h, first[0] + k]
            at = pl.multiple_of(row * tiles, tiles)
            out[h, k] = pool[pl.ds(at, tiles)]
        return carry

    lax.fori_loop(0, SIDE, step, 0)


def select(asked, blocks, first, rows, tiles, per_peer):
    return pl.pallas_call(
        functools.partial(select_body, first, rows, tiles),
        out_shape=jax.ShapeDtypeStruct((SIDE, per_peer, tiles, 8, 128), BF16),
        in_specs=[pl.BlockSpec(memory_space=pltpu.SMEM)] + [pl.BlockSpec(memory_space=ANY)] * 8,
        out_specs=pl.BlockSpec(memory_space=VM),
        scratch_shapes=[pltpu.VMEM((8 * rows * tiles, 8, 128), BF16), pltpu.SemaphoreType.DMA((8,))],
        name="select",
    )(asked, *blocks)


def parent_far_body(code, recv, ops_hbm, out, ops, sem):
    copy = pltpu.make_async_copy(ops_hbm, ops.at[pl.ds(0, 40)], sem)
    copy.start()
    ops[40] = jnp.zeros(ops.shape[1:], BF16)
    copy.wait()

    def row(r, carry):
        real = [jnp.zeros((8, 128), F32) for _ in range(4)]
        imag = [jnp.zeros((8, 128), F32) for _ in range(4)]
        for j in range(8):
            both = code[j, r]
            at, op = both >> 6, both & 63
            for t in range(4):
                u, v = t // 2, t % 2
                a = ops[op, 0, u * 8 : u * 8 + 8, v * 128 : v * 128 + 128].astype(F32)
                b = ops[op, 1, u * 8 : u * 8 + 8, v * 128 : v * 128 + 128].astype(F32)
                c = recv[at, t].astype(F32)
                d = recv[at, 4 + t].astype(F32)
                real[t] = real[t] + (a * c - b * d)
                imag[t] = imag[t] + (a * d + b * c)
        for t in range(4):
            out[r, t] = real[t].astype(BF16)
            out[r, 4 + t] = imag[t].astype(BF16)
        return carry

    lax.fori_loop(0, 16, row, 0)


def far_parents(code, recv, ops):
    return pl.pallas_call(
        parent_far_body,
        out_shape=jax.ShapeDtypeStruct((16, 8, 8, 128), BF16),
        in_specs=[
            pl.BlockSpec(memory_space=pltpu.SMEM),
            pl.BlockSpec(memory_space=VM),
            pl.BlockSpec(memory_space=ANY),
        ],
        out_specs=pl.BlockSpec(memory_space=VM),
        scratch_shapes=[pltpu.VMEM((41, 2, 16, PP), BF16), pltpu.SemaphoreType.DMA],
        name="far_parents",
    )(code, recv, ops)


def child_far_body(code, recv, ops_hbm, term, out, ops, sem):
    copy = pltpu.make_async_copy(ops_hbm, ops.at[pl.ds(0, 40)], sem)
    copy.start()
    ops[40] = jnp.zeros(ops.shape[1:], BF16)
    copy.wait()

    def row(r, carry):
        real = jnp.zeros((8, 128), F32)
        imag = jnp.zeros((8, 128), F32)
        for j in range(8):
            both = code[j, r]
            at, op = both >> 6, both & 63
            a, b = ops[op, 0].astype(F32), ops[op, 1].astype(F32)
            c, d = recv[at, 0].astype(F32), recv[at, 1].astype(F32)
            real = real + (a * c - b * d)
            imag = imag + (a * d + b * c)
        out[r, 0] = (real + term[r, 0].astype(F32)).astype(BF16)
        out[r, 1] = (imag + term[r, 1].astype(F32)).astype(BF16)
        return carry

    lax.fori_loop(0, 64, row, 0, unroll=2)


def far_children(code, recv, ops, term):
    return pl.pallas_call(
        child_far_body,
        out_shape=jax.ShapeDtypeStruct((64, 2, 8, 128), BF16),
        in_specs=[
            pl.BlockSpec(memory_space=pltpu.SMEM),
            pl.BlockSpec(memory_space=VM),
            pl.BlockSpec(memory_space=ANY),
            pl.BlockSpec(memory_space=VM),
        ],
        out_specs=pl.BlockSpec(memory_space=VM),
        scratch_shapes=[pltpu.VMEM((41, 2, 8, 128), BF16), pltpu.SemaphoreType.DMA],
        name="far_children",
    )(code, recv, ops, term)


def down_body(far, theta, phi, cos_t, sin_t, out, turned):
    for q in range(2):
        for u in range(PT // 8):
            at = pl.ds(u * 8, 8)
            re, im = (
                jnp.concatenate(
                    [far[u // 2, q, c * 4 + (u % 2) * 2 + v].astype(F32) for v in range(2)], axis=1
                )
                for c in range(2)
            )
            for t, (k, m) in enumerate(((0, 3), (1, 2))):
                cs, sn = cos_t[t, at, :], sin_t[t, at, :]
                cr, si, ci, sr = cs * re, sn * im, cs * im, sn * re
                turned[(q * 4 + k) * 2, at, :] = (cr + si).astype(BF16)
                turned[(q * 4 + k) * 2 + 1, at, :] = (ci - sr).astype(BF16)
                turned[(q * 4 + m) * 2, at, :] = (cr - si).astype(BF16)
                turned[(q * 4 + m) * 2 + 1, at, :] = (ci + sr).astype(BF16)
    for r in range(8):
        for c in range(2):
            narrowed = bmm(turned[r * 2 + c], phi[...]).astype(BF16)
            term = bmm(theta[...], narrowed).astype(BF16)
            for s in range(8):
                out[s, r, c] = term[s * 8 : s * 8 + 8, :]


def lower(far, theta, phi, cos_t, sin_t):
    return pl.pallas_call(
        down_body,
        out_shape=jax.ShapeDtypeStruct((8, 8, 2, 8, 128), BF16),
        in_specs=[pl.BlockSpec(memory_space=VM)] * 5,
        out_specs=pl.BlockSpec(memory_space=VM),
        scratch_shapes=[pltpu.VMEM((16, PT, PP), BF16)],
        name="lower",
    )(far, theta, phi, cos_t, sin_t)


def groups(straight):
    found = []
    for angle in range(8):
        for o in range(SIDE):
            line = [(o, i) if (angle % 2) == straight else (i, o) for i in range(SIDE)]
            found.append([(y * SIDE + z) * 8 + angle for y, z in line])
    return found


SPREAD, TRADE = groups(1), groups(0)


def hop(x, step):
    pairs = [(g[i], g[(i + step) % SIDE]) for g in SPREAD for i in range(SIDE)]
    return lax.ppermute(x, BOTH, pairs)


def swap(x, axis, **kw):
    return lax.all_to_all(x, axis, split_axis=0, concat_axis=0, tiled=True, **kw)


def local(
    child_field,
    child_list,
    child_op,
    child_home,
    child_ops,
    parent_list,
    parent_op,
    parent_home,
    parent_ops,
):
    theta_up = jnp.asarray(fourier_table(PT, CT, 0.5)).astype(BF16)
    phi_up = jnp.asarray(np.ascontiguousarray(fourier_table(PP, SUBBOX_HEADINGS, 0.0).T)).astype(BF16)
    theta_down = jnp.asarray(np.ascontiguousarray(fourier_table(PT, CT, 0.5).T) * np.float32(CT / PT)).astype(BF16)
    phi_down = jnp.asarray(
        fourier_table(PP, SUBBOX_HEADINGS, 0.0) * np.float32(SUBBOX_HEADINGS / PP)
    ).astype(BF16)
    cos_np, sin_np = shift_tables()
    cos_t, sin_t = jnp.asarray(cos_np), jnp.asarray(sin_np)

    box, angle = lax.axis_index("box"), lax.axis_index("angle")
    core = angle % 2
    mine = jnp.where(core == 0, box // SIDE, box % SIDE)
    where = jnp.stack([core, mine]).astype(I32)

    wanted, child_code, parent_code = plan(
        where, child_list, child_op, child_home, parent_list, parent_op, parent_home
    )
    asked = swap(wanted.reshape(SIDE, 1, 128), BOTH, axis_index_groups=TRADE).reshape(SIDE, 128)

    whole = swap(child_field, "angle").reshape(8, 8, 2, 8, 128)
    parents = swap(lift(whole, theta_up, phi_up, cos_t, sin_t), "angle")
    own = jnp.concatenate([child_field.reshape(128, 8, 128), parents.reshape(128, 8, 128)])
    forth, back = [own], [own]
    for step in range(4):
        forth.append(hop(forth[-1], 1))
        if step < 3:
            back.append(hop(back[-1], -1))
    blocks = back + [forth[8 - p] for p in range(4, 8)]

    parents_out = select(asked, blocks, (64, 128), 16, 8, 16)
    children_out = select(asked, blocks, (0, 0), 64, 2, 64)
    parents_in = swap(parents_out, BOTH, axis_index_groups=TRADE)
    children_in = swap(children_out, BOTH, axis_index_groups=TRADE)
    parent_far = far_parents(parent_code, parents_in.reshape(128, 8, 8, 128), parent_ops)
    turned = swap(parent_far, "angle").reshape(8, 2, 8, 8, 128)
    terms = swap(lower(turned, theta_down, phi_down, cos_t, sin_t), "angle")
    return far_children(
        child_code, children_in.reshape(512, 2, 8, 128), child_ops, terms.reshape(64, 2, 8, 128)
    )


def solution(mesh):
    return jax.shard_map(
        local,
        mesh=mesh,
        in_specs=(
            P("box", None, "angle", None),
            P("box", None),
            P("box", None),
            P(),
            P(None, None, "angle", None),
            P("box", None),
            P("box", None),
            P(),
            P(None, None, "angle", None),
        ),
        out_specs=P("box", None, "angle", None),
        check_vma=False,
    )
```

```python
import functools
import math

import jax
import jax.numpy as jnp
import numpy as np
from jax import lax
from jax.experimental import pallas as pl
from jax.experimental.pallas import tpu as pltpu
from jax.sharding import PartitionSpec as P

CT = 64
SUBBOX_HEADINGS = 128
PT = 128
PP = 256
KIDS = 4
WAVE_NUMBER = 6.0
SIDE = 8
BOTH = ("box", "angle")
F32, BF16, I32 = jnp.float32, jnp.bfloat16, jnp.int32
VM = pltpu.VMEM
ANY = pl.ANY
GRANT = 12 << 20


def fourier_table(fine_count, coarse_count, offset):
    f32 = np.float32
    fine = (np.arange(fine_count, dtype=f32) + f32(offset)) / f32(fine_count)
    coarse = (np.arange(coarse_count, dtype=f32) + f32(offset)) / f32(coarse_count)
    x = fine[:, None] - coarse[None, :]
    harmonic = np.arange(1, coarse_count // 2, dtype=f32)
    cosines = np.cos(f32(2.0 * math.pi) * harmonic * x[:, :, None])
    summed = f32(1.0) + f32(2.0) * cosines.sum(2, dtype=np.float64) + np.cos(f32(math.pi * coarse_count) * x)
    return (summed / coarse_count).astype(f32)


def shift_tables():
    f32 = np.float32
    polar = (f32(math.pi) * (np.arange(PT, dtype=f32) + f32(0.5)) / f32(PT)).astype(f32)
    heading = (f32(2.0 * math.pi / PP) * np.arange(PP, dtype=f32)).astype(f32)
    cos_h, sin_h = np.cos(heading), np.sin(heading)
    across = np.stack([-cos_h - sin_h, cos_h - sin_h])
    arg = (f32(WAVE_NUMBER) * np.sin(polar))[None, :, None] * across[:, None, :]
    return np.cos(arg).astype(f32), np.sin(arg).astype(f32)


def bmm(a, b):
    return lax.dot_general(a, b, (((1,), (0,)), ((), ())), preferred_element_type=F32)


def iota(shape, dim):
    return lax.broadcasted_iota(I32, shape, dim)


def plan_level(ids_ref, op_ref, home_ref, core, mine, rows_device, cap, empty_op, code_ref):
    slots, rows = ids_ref.shape
    home = home_ref[...]
    owner = home // rows_device
    table = jnp.concatenate([owner, home - owner * rows_device], axis=0).astype(F32).astype(BF16)
    highs = home.shape[0]
    before = (iota((rows, rows), 0) < iota((rows, rows), 1)).astype(F32).astype(BF16)
    carry = jnp.zeros((SIDE, 1), F32)
    wanted = jnp.zeros((2 * SIDE, cap), F32)
    for j in range(slots):
        ids = ids_ref[pl.ds(j, 1), :]
        usable = ids >= 0
        safe = jnp.maximum(ids, 0)
        high, low = safe >> 7, safe & 127
        low_hot = (iota((128, rows), 0) == low).astype(F32).astype(BF16)
        picked = bmm(table, low_hot)
        high_hot = (iota((highs, rows), 0) == high).astype(F32)
        own = jnp.sum(picked[:highs] * high_hot, axis=0, keepdims=True).astype(I32)
        loc = jnp.sum(picked[highs:] * high_hot, axis=0, keepdims=True)
        along_y, along_z = own >> 3, own & 7
        column = jnp.where(core == 0, along_z, along_y)
        place = (jnp.where(core == 0, along_y, along_z) - mine) & 7
        hot = jnp.where((iota((SIDE, rows), 0) == column) & usable, 1.0, 0.0)
        hot_b = hot.astype(BF16)
        prefix = bmm(hot_b, before) + carry
        carry = carry + jnp.sum(hot, axis=1, keepdims=True)
        rank = jnp.sum(hot * prefix, axis=0, keepdims=True).astype(I32)
        position = column * cap + rank
        code_ref[pl.ds(j, 1), pl.ds(0, rows)] = jnp.where(
            usable, position * 64 + op_ref[pl.ds(j, 1), :], empty_op
        )
        rank_hot = (iota((cap, rows), 0) == rank).astype(F32).astype(BF16)
        both = jnp.concatenate([hot * place.astype(F32), hot * loc], axis=0).astype(BF16)
        wanted = wanted + lax.dot_general(
            both, rank_hot, (((1,), (1,)), ((), ())), preferred_element_type=F32
        )
    return (wanted[:SIDE] * rows_device + wanted[SIDE:]).astype(I32)


def plan_body(where, cl, co, ch, plist, po, ph, want_ref, ccode_ref, pcode_ref):
    core, mine = where[0], where[1]
    want_ref[...] = jnp.zeros(want_ref.shape, I32)
    want_ref[:, pl.ds(0, 64)] = plan_level(cl, co, ch, core, mine, 64, 64, 40, ccode_ref)
    want_ref[:, pl.ds(64, 16)] = plan_level(plist, po, ph, core, mine, 16, 16, 40, pcode_ref)


def plan(where, child_list, child_op, child_home, parent_list, parent_op, parent_home):
    args = (
        where,
        child_list.T,
        child_op.T,
        child_home.reshape(-1, 128),
        parent_list.T,
        parent_op.T,
        parent_home.reshape(-1, 128),
    )
    return pl.pallas_call(
        plan_body,
        out_shape=(
            jax.ShapeDtypeStruct((SIDE, 128), I32),
            jax.ShapeDtypeStruct((8, 64), I32),
            jax.ShapeDtypeStruct((8, 16), I32),
        ),
        in_specs=[pl.BlockSpec(memory_space=pltpu.SMEM)] + [pl.BlockSpec(memory_space=VM)] * 6,
        out_specs=(pl.BlockSpec(memory_space=VM),) * 3,
        compiler_params=pltpu.CompilerParams(vmem_limit_bytes=GRANT),
        name="plan",
    )(*args)


def up_body(field, theta, phi, cos_t, sin_t, out, wide):
    for r in range(8):
        for c in range(2):
            rows = jnp.concatenate([field[s, r, c] for s in range(8)], axis=0)
            stretched = bmm(theta[...], rows).astype(BF16)
            wide[r * 2 + c] = bmm(stretched, phi[...])
    for q in range(2):
        for u in range(PT // 8):
            at = pl.ds(u * 8, 8)
            w = [[wide[(q * 4 + k) * 2 + c, at, :] for c in range(2)] for k in range(4)]
            real = jnp.zeros((8, PP), F32)
            imag = jnp.zeros((8, PP), F32)
            for t, (k, m) in enumerate(((0, 3), (1, 2))):
                cs, sn = cos_t[t, at, :], sin_t[t, at, :]
                real = real + cs * (w[k][0] + w[m][0]) - sn * (w[k][1] - w[m][1])
                imag = imag + cs * (w[k][1] + w[m][1]) + sn * (w[k][0] - w[m][0])
            for c, part in enumerate((real, imag)):
                part = part.astype(BF16)
                for v in range(2):
                    out[u // 2, q, c * 4 + (u % 2) * 2 + v] = part[:, v * 128 : (v + 1) * 128]


def lift(field, theta, phi, cos_t, sin_t):
    return pl.pallas_call(
        up_body,
        out_shape=jax.ShapeDtypeStruct((8, 2, 8, 8, 128), BF16),
        in_specs=[pl.BlockSpec(memory_space=VM)] * 5,
        out_specs=pl.BlockSpec(memory_space=VM),
        scratch_shapes=[pltpu.VMEM((16, PT, PP), F32)],
        compiler_params=pltpu.CompilerParams(vmem_limit_bytes=GRANT),
        name="lift",
    )(field, theta, phi, cos_t, sin_t)


def select_body(first, rows, tiles, asked, *refs):
    blocks, out, pool, sems = refs[:8], refs[8], refs[9], refs[10]
    count = rows * tiles
    copies = [
        pltpu.make_async_copy(b.at[pl.ds(first[1], count)], pool.at[pl.ds(i * count, count)], sems.at[i])
        for i, b in enumerate(blocks)
    ]
    for copy in copies:
        copy.start()
    for copy in copies:
        copy.wait()
    per_peer = out.shape[1]

    def step(h, carry):
        for k in range(per_peer):
            row = asked[h, first[0] + k]
            at = pl.multiple_of(row * tiles, tiles)
            out[h, k] = pool[pl.ds(at, tiles)]
        return carry

    lax.fori_loop(0, SIDE, step, 0)


def select(asked, blocks, first, rows, tiles, per_peer):
    return pl.pallas_call(
        functools.partial(select_body, first, rows, tiles),
        out_shape=jax.ShapeDtypeStruct((SIDE, per_peer, tiles, 8, 128), BF16),
        in_specs=[pl.BlockSpec(memory_space=pltpu.SMEM)] + [pl.BlockSpec(memory_space=ANY)] * 8,
        out_specs=pl.BlockSpec(memory_space=VM),
        scratch_shapes=[pltpu.VMEM((8 * rows * tiles, 8, 128), BF16), pltpu.SemaphoreType.DMA((8,))],
        compiler_params=pltpu.CompilerParams(vmem_limit_bytes=GRANT),
        name="select",
    )(asked, *blocks)


def parent_far_body(angle, code, recv, ops_hbm, keep, send, ops, sem):
    copy = pltpu.make_async_copy(ops_hbm, ops.at[pl.ds(0, 40)], sem)
    copy.start()
    ops[40] = jnp.zeros(ops.shape[1:], BF16)
    copy.wait()

    def pair(i, carry):
        for odd, out in enumerate((keep, send)):
            for q in range(2):
                r = (angle[0] ^ (2 * i + odd)) * 2 + q
                real = [jnp.zeros((8, 128), F32) for _ in range(4)]
                imag = [jnp.zeros((8, 128), F32) for _ in range(4)]
                for j in range(8):
                    both = code[j, r]
                    at, op = both >> 6, both & 63
                    for t in range(4):
                        u, v = t // 2, t % 2
                        a = ops[op, 0, u * 8 : u * 8 + 8, v * 128 : v * 128 + 128].astype(F32)
                        b = ops[op, 1, u * 8 : u * 8 + 8, v * 128 : v * 128 + 128].astype(F32)
                        c = recv[at, t].astype(F32)
                        d = recv[at, 4 + t].astype(F32)
                        real[t] = real[t] + (a * c - b * d)
                        imag[t] = imag[t] + (a * d + b * c)
                for t in range(4):
                    out[i, q, t] = real[t].astype(BF16)
                    out[i, q, 4 + t] = imag[t].astype(BF16)
        return carry

    lax.fori_loop(0, 4, pair, 0)


def far_parents(angle, code, recv, ops):
    return pl.pallas_call(
        parent_far_body,
        out_shape=(jax.ShapeDtypeStruct((4, 2, 8, 8, 128), BF16),) * 2,
        in_specs=[
            pl.BlockSpec(memory_space=pltpu.SMEM),
            pl.BlockSpec(memory_space=pltpu.SMEM),
            pl.BlockSpec(memory_space=VM),
            pl.BlockSpec(memory_space=ANY),
        ],
        out_specs=(pl.BlockSpec(memory_space=VM),) * 2,
        scratch_shapes=[pltpu.VMEM((41, 2, 16, PP), BF16), pltpu.SemaphoreType.DMA],
        cost_estimate=pl.CostEstimate(flops=10_000_000, bytes_accessed=3_500_000, transcendentals=0),
        compiler_params=pltpu.CompilerParams(vmem_limit_bytes=GRANT),
        name="far_parents",
    )(angle, code, recv, ops)


CUBE = ((0, 0), (1, 0), (2, 0), (2, 2), (3, 0), (3, 1), (3, 2), (3, 3))


def cube(keep, send):
    def across(x, bit):
        return lax.ppermute(x, "angle", [(i, i ^ bit) for i in range(8)])

    first = across(send, 1)
    second = across(jnp.concatenate([keep[1:2], keep[3:4], first[1:2], first[3:4]]), 2)
    third = across(jnp.concatenate([keep[2:3], first[2:3], second[1:2], second[3:4]]), 4)
    return keep, first, second, third


def child_far_body(angle, code, recv, ops_hbm, t0, t1, t2, t3, out, ops, sem):
    copy = pltpu.make_async_copy(ops_hbm, ops.at[pl.ds(0, 40)], sem)
    copy.start()
    ops[40] = jnp.zeros(ops.shape[1:], BF16)
    copy.wait()
    terms = (t0, t1, t2, t3)

    for s, (which, place) in enumerate(CUBE):

        def row(k, carry):
            r = (angle[0] ^ s) * 8 + k
            real = jnp.zeros((8, 128), F32)
            imag = jnp.zeros((8, 128), F32)
            for j in range(8):
                both = code[j, r]
                at, op = both >> 6, both & 63
                a, b = ops[op, 0].astype(F32), ops[op, 1].astype(F32)
                c, d = recv[at, 0].astype(F32), recv[at, 1].astype(F32)
                real = real + (a * c - b * d)
                imag = imag + (a * d + b * c)
            out[r, 0] = (real + terms[which][place, k, 0].astype(F32)).astype(BF16)
            out[r, 1] = (imag + terms[which][place, k, 1].astype(F32)).astype(BF16)
            return carry

        lax.fori_loop(0, 8, row, 0, unroll=2)


def far_children(angle, code, recv, ops, terms):
    return pl.pallas_call(
        child_far_body,
        out_shape=jax.ShapeDtypeStruct((64, 2, 8, 128), BF16),
        in_specs=[
            pl.BlockSpec(memory_space=pltpu.SMEM),
            pl.BlockSpec(memory_space=pltpu.SMEM),
            pl.BlockSpec(memory_space=VM),
            pl.BlockSpec(memory_space=ANY),
        ]
        + [pl.BlockSpec(memory_space=VM)] * 4,
        out_specs=pl.BlockSpec(memory_space=VM),
        scratch_shapes=[pltpu.VMEM((41, 2, 8, 128), BF16), pltpu.SemaphoreType.DMA],
        compiler_params=pltpu.CompilerParams(vmem_limit_bytes=GRANT),
        name="far_children",
    )(angle, code, recv, ops, *terms)


def down_body(angle, f0, f1, f2, f3, theta, phi, cos_t, sin_t, keep, send, turned, whole):
    far = (f0, f1, f2, f3)
    for s, (which, place) in enumerate(CUBE):
        at = pl.ds(pl.multiple_of((angle[0] ^ s) * 16, 16), 16)
        cos_s = [cos_t[t, at, :] for t in range(2)]
        sin_s = [sin_t[t, at, :] for t in range(2)]
        for q in range(2):
            re, im = (
                jnp.concatenate(
                    [
                        jnp.concatenate(
                            [far[which][place, q, c * 4 + u * 2 + v].astype(F32) for v in range(2)], axis=1
                        )
                        for u in range(2)
                    ],
                    axis=0,
                )
                for c in range(2)
            )
            for t, (k, m) in enumerate(((0, 3), (1, 2))):
                cs, sn = cos_s[t], sin_s[t]
                cr, si, ci, sr = cs * re, sn * im, cs * im, sn * re
                turned[(q * 4 + k) * 2, at, :] = (cr + si).astype(BF16)
                turned[(q * 4 + k) * 2 + 1, at, :] = (ci - sr).astype(BF16)
                turned[(q * 4 + m) * 2, at, :] = (cr - si).astype(BF16)
                turned[(q * 4 + m) * 2 + 1, at, :] = (ci + sr).astype(BF16)
    for r in range(8):
        for c in range(2):
            narrowed = bmm(turned[r * 2 + c], phi[...]).astype(BF16)
            whole[r * 2 + c] = bmm(theta[...], narrowed)
    for s in range(8):
        at = pl.ds(pl.multiple_of((angle[0] ^ s) * 8, 8), 8)
        for r in range(8):
            for c in range(2):
                (keep, send)[s % 2][s // 2, r, c] = whole[r * 2 + c, at, :].astype(BF16)


def lower(angle, far, theta, phi, cos_t, sin_t):
    return pl.pallas_call(
        down_body,
        out_shape=(jax.ShapeDtypeStruct((4, 8, 2, 8, 128), BF16),) * 2,
        in_specs=[pl.BlockSpec(memory_space=pltpu.SMEM)] + [pl.BlockSpec(memory_space=VM)] * 8,
        out_specs=(pl.BlockSpec(memory_space=VM),) * 2,
        scratch_shapes=[pltpu.VMEM((16, PT, PP), BF16), pltpu.VMEM((16, CT, SUBBOX_HEADINGS), F32)],
        cost_estimate=pl.CostEstimate(flops=300_000_000, bytes_accessed=2_000_000, transcendentals=0),
        compiler_params=pltpu.CompilerParams(vmem_limit_bytes=GRANT),
        name="lower",
    )(angle, *far, theta, phi, cos_t, sin_t)


def groups(straight):
    found = []
    for angle in range(8):
        for o in range(SIDE):
            line = [(o, i) if (angle % 2) == straight else (i, o) for i in range(SIDE)]
            found.append([(y * SIDE + z) * 8 + angle for y, z in line])
    return found


SPREAD, TRADE = groups(1), groups(0)


def hop(x, step):
    pairs = [(g[i], g[(i + step) % SIDE]) for g in SPREAD for i in range(SIDE)]
    return lax.ppermute(x, BOTH, pairs)


def swap(x, axis, **kw):
    return lax.all_to_all(x, axis, split_axis=0, concat_axis=0, tiled=True, **kw)


def local(
    child_field,
    child_list,
    child_op,
    child_home,
    child_ops,
    parent_list,
    parent_op,
    parent_home,
    parent_ops,
):
    theta_up = jnp.asarray(fourier_table(PT, CT, 0.5)).astype(BF16)
    phi_up = jnp.asarray(np.ascontiguousarray(fourier_table(PP, SUBBOX_HEADINGS, 0.0).T)).astype(BF16)
    theta_down = jnp.asarray(np.ascontiguousarray(fourier_table(PT, CT, 0.5).T) * np.float32(CT / PT)).astype(BF16)
    phi_down = jnp.asarray(
        fourier_table(PP, SUBBOX_HEADINGS, 0.0) * np.float32(SUBBOX_HEADINGS / PP)
    ).astype(BF16)
    cos_np, sin_np = shift_tables()
    cos_t, sin_t = jnp.asarray(cos_np), jnp.asarray(sin_np)

    box, angle = lax.axis_index("box"), lax.axis_index("angle")
    core = angle % 2
    mine = jnp.where(core == 0, box // SIDE, box % SIDE)
    where = jnp.stack([core, mine]).astype(I32)

    wanted, child_code, parent_code = plan(
        where, child_list, child_op, child_home, parent_list, parent_op, parent_home
    )
    whole = swap(child_field, "angle").reshape(8, 8, 2, 8, 128)
    parents = swap(lift(whole, theta_up, phi_up, cos_t, sin_t), "angle")
    own = jnp.concatenate([child_field.reshape(128, 8, 128), parents.reshape(128, 8, 128)])
    forth, back = [own], [own]
    for step in range(4):
        if step == 1:
            forth[1], wanted = lax.optimization_barrier((forth[1], wanted))
        forth.append(hop(forth[-1], 1))
        if step < 3:
            back.append(hop(back[-1], -1))
    asked = swap(wanted.reshape(SIDE, 1, 128), BOTH, axis_index_groups=TRADE).reshape(SIDE, 128)
    blocks = back + [forth[8 - p] for p in range(4, 8)]

    parents_out = select(asked, blocks, (64, 128), 16, 8, 16)
    children_out = select(asked, blocks, (0, 0), 64, 2, 64)
    parents_in = swap(parents_out, BOTH, axis_index_groups=TRADE)
    children_in = swap(children_out, BOTH, axis_index_groups=TRADE)
    here = angle.reshape(1).astype(I32)
    far = cube(*far_parents(here, parent_code, parents_in.reshape(128, 8, 8, 128), parent_ops))
    terms = cube(*lower(here, far, theta_down, phi_down, cos_t, sin_t))
    return far_children(here, child_code, children_in.reshape(512, 2, 8, 128), child_ops, terms)


def solution(mesh):
    return jax.shard_map(
        local,
        mesh=mesh,
        in_specs=(
            P("box", None, "angle", None),
            P("box", None),
            P("box", None),
            P(),
            P(None, None, "angle", None),
            P("box", None),
            P("box", None),
            P(),
            P(None, None, "angle", None),
        ),
        out_specs=P("box", None, "angle", None),
        check_vma=False,
    )
```

```python
import functools
import math

import jax
import jax.numpy as jnp
import numpy as np
from jax import lax
from jax.experimental import pallas as pl
from jax.experimental.pallas import tpu as pltpu
from jax.sharding import PartitionSpec as P


CT = 64
SUBBOX_HEADINGS = 128
PT = 128
PP = 256
WAVE_NUMBER = 6.0
SIDE = 8
BOTH = ("box", "angle")
F32, BF16, I32 = jnp.float32, jnp.bfloat16, jnp.int32
VM = pltpu.VMEM
ANY = pl.ANY
GRANT = 12 << 20


def fourier_table(fine_count, coarse_count, offset):
    f32 = np.float32
    fine = (np.arange(fine_count, dtype=f32) + f32(offset)) / f32(fine_count)
    coarse = (np.arange(coarse_count, dtype=f32) + f32(offset)) / f32(coarse_count)
    x = fine[:, None] - coarse[None, :]
    harmonic = np.arange(1, coarse_count // 2, dtype=f32)
    cosines = np.cos(f32(2.0 * math.pi) * harmonic * x[:, :, None])
    summed = f32(1.0) + f32(2.0) * cosines.sum(2, dtype=np.float64) + np.cos(f32(math.pi * coarse_count) * x)
    return (summed / coarse_count).astype(f32)


def shift_tables():
    f32 = np.float32
    polar = (f32(math.pi) * (np.arange(PT, dtype=f32) + f32(0.5)) / f32(PT)).astype(f32)
    heading = (f32(2.0 * math.pi / PP) * np.arange(PP, dtype=f32)).astype(f32)
    cos_h, sin_h = np.cos(heading), np.sin(heading)
    across = np.stack([-cos_h - sin_h, cos_h - sin_h])
    arg = (f32(WAVE_NUMBER) * np.sin(polar))[None, :, None] * across[:, None, :]
    return np.cos(arg).astype(f32), np.sin(arg).astype(f32)


def bmm(a, b):
    return lax.dot_general(a, b, (((1,), (0,)), ((), ())), preferred_element_type=F32)


def iota(shape, dim):
    return lax.broadcasted_iota(I32, shape, dim)


def plan_level(ids_ref, op_ref, home_ref, core, mine, rows_device, cap, empty_op, code_ref):
    slots, rows = ids_ref.shape
    home = home_ref[...]
    owner = home // rows_device
    table = jnp.concatenate([owner, home - owner * rows_device], axis=0).astype(F32).astype(BF16)
    highs = home.shape[0]
    before = (iota((rows, rows), 0) < iota((rows, rows), 1)).astype(F32).astype(BF16)
    carry = jnp.zeros((SIDE, 1), F32)
    wanted = jnp.zeros((2 * SIDE, cap), F32)
    for j in range(slots):
        ids = ids_ref[pl.ds(j, 1), :]
        usable = ids >= 0
        safe = jnp.maximum(ids, 0)
        high, low = safe >> 7, safe & 127
        low_hot = (iota((128, rows), 0) == low).astype(F32).astype(BF16)
        picked = bmm(table, low_hot)
        high_hot = (iota((highs, rows), 0) == high).astype(F32)
        own = jnp.sum(picked[:highs] * high_hot, axis=0, keepdims=True).astype(I32)
        loc = jnp.sum(picked[highs:] * high_hot, axis=0, keepdims=True)
        along_y, along_z = own >> 3, own & 7
        column = jnp.where(core == 0, along_z, along_y)
        place = (jnp.where(core == 0, along_y, along_z) - mine) & 7
        hot = jnp.where((iota((SIDE, rows), 0) == column) & usable, 1.0, 0.0)
        hot_b = hot.astype(BF16)
        prefix = bmm(hot_b, before) + carry
        carry = carry + jnp.sum(hot, axis=1, keepdims=True)
        rank = jnp.sum(hot * prefix, axis=0, keepdims=True).astype(I32)
        position = column * cap + rank
        code_ref[pl.ds(j, 1), pl.ds(0, rows)] = jnp.where(
            usable, position * 64 + op_ref[pl.ds(j, 1), :], empty_op
        )
        rank_hot = (iota((cap, rows), 0) == rank).astype(F32).astype(BF16)
        both = jnp.concatenate([hot * place.astype(F32), hot * loc], axis=0).astype(BF16)
        wanted = wanted + lax.dot_general(
            both, rank_hot, (((1,), (1,)), ((), ())), preferred_element_type=F32
        )
    return (wanted[:SIDE] * rows_device + wanted[SIDE:]).astype(I32)


def plan_body(where, cl, co, ch, plist, po, ph, want_ref, ccode_ref, pcode_ref):
    core, mine = where[0], where[1]
    want_ref[...] = jnp.zeros(want_ref.shape, I32)
    want_ref[:, pl.ds(0, 64)] = plan_level(cl, co, ch, core, mine, 64, 64, 40, ccode_ref)
    want_ref[:, pl.ds(64, 16)] = plan_level(plist, po, ph, core, mine, 16, 16, 40, pcode_ref)


def plan(where, child_list, child_op, child_home, parent_list, parent_op, parent_home):
    args = (
        where,
        child_list.T,
        child_op.T,
        child_home.reshape(-1, 128),
        parent_list.T,
        parent_op.T,
        parent_home.reshape(-1, 128),
    )
    return pl.pallas_call(
        plan_body,
        out_shape=(
            jax.ShapeDtypeStruct((SIDE, 128), I32),
            jax.ShapeDtypeStruct((8, 64), I32),
            jax.ShapeDtypeStruct((8, 16), I32),
        ),
        in_specs=[pl.BlockSpec(memory_space=pltpu.SMEM)] + [pl.BlockSpec(memory_space=VM)] * 6,
        out_specs=(pl.BlockSpec(memory_space=VM),) * 3,
        compiler_params=pltpu.CompilerParams(vmem_limit_bytes=GRANT),
        name="plan",
    )(*args)


def up_body(field, theta_h, phi_h, cos_h, sin_h, out, theta, phi, cos_t, sin_t, wide, sems):
    copies = fetch((theta_h, phi_h, cos_h, sin_h), (theta, phi, cos_t, sin_t), sems)
    copies[0].wait()
    copies[1].wait()
    for r in range(8):
        for c in range(2):
            rows = jnp.concatenate([field[s, r, c] for s in range(8)], axis=0)
            stretched = bmm(theta[...], rows).astype(BF16)
            wide[r * 2 + c] = bmm(stretched, phi[...])
    copies[2].wait()
    copies[3].wait()
    for q in range(2):
        for u in range(PT // 8):
            at = pl.ds(u * 8, 8)
            w = [[wide[(q * 4 + k) * 2 + c, at, :] for c in range(2)] for k in range(4)]
            real = jnp.zeros((8, PP), F32)
            imag = jnp.zeros((8, PP), F32)
            for t, (k, m) in enumerate(((0, 3), (1, 2))):
                cs, sn = cos_t[t, at, :], sin_t[t, at, :]
                real = real + cs * (w[k][0] + w[m][0]) - sn * (w[k][1] - w[m][1])
                imag = imag + cs * (w[k][1] + w[m][1]) + sn * (w[k][0] - w[m][0])
            for c, part in enumerate((real, imag)):
                part = part.astype(BF16)
                for v in range(2):
                    out[u // 2, q, c * 4 + (u % 2) * 2 + v] = part[:, v * 128 : (v + 1) * 128]


def fetch(sources, targets, sems):
    copies = [pltpu.make_async_copy(a, b, sems.at[i]) for i, (a, b) in enumerate(zip(sources, targets))]
    for copy in copies:
        copy.start()
    return copies


def lift(field, tables):
    return pl.pallas_call(
        up_body,
        out_shape=jax.ShapeDtypeStruct((8, 2, 8, 8, 128), BF16),
        in_specs=[pl.BlockSpec(memory_space=VM)] + [pl.BlockSpec(memory_space=pltpu.HBM)] * 4,
        out_specs=pl.BlockSpec(memory_space=VM),
        scratch_shapes=[pltpu.VMEM(t.shape, t.dtype) for t in tables]
        + [pltpu.VMEM((16, PT, PP), F32), pltpu.SemaphoreType.DMA((4,))],
        compiler_params=pltpu.CompilerParams(vmem_limit_bytes=GRANT),
        name="lift",
    )(field, *tables)


def select_body(first, asked, *refs):
    blocks, out, pool, buf, sems, out_sems = refs[:8], *refs[8:]
    for copy in fetch(blocks, [pool.at[i] for i in range(8)], sems):
        copy.wait()
    _, per_peer, tiles = buf.shape[:3]
    rows = pool.shape[1] // tiles
    shift = rows.bit_length() - 1

    def copy_out(h):
        return pltpu.make_async_copy(buf.at[h], out.at[h], out_sems.at[h])

    def step(h, carry):
        for k in range(per_peer):
            row = asked[h, first + k]
            at = pl.multiple_of((row & (rows - 1)) * tiles, tiles)
            buf[h, k] = pool[row >> shift, pl.ds(at, tiles)]
        copy_out(h).start()
        return carry

    lax.fori_loop(0, SIDE, step, 0)
    for h in range(SIDE):
        copy_out(h).wait()


def select(asked, blocks, first, tiles, per_peer):
    shape = (SIDE, per_peer, tiles, 8, 128)
    return pl.pallas_call(
        functools.partial(select_body, first),
        out_shape=jax.ShapeDtypeStruct(shape, BF16),
        in_specs=[pl.BlockSpec(memory_space=pltpu.SMEM)] + [pl.BlockSpec(memory_space=ANY)] * 8,
        out_specs=pl.BlockSpec(memory_space=pltpu.HBM),
        scratch_shapes=[
            pltpu.VMEM((8, 128, 8, 128), BF16),
            pltpu.VMEM(shape, BF16),
            pltpu.SemaphoreType.DMA((8,)),
            pltpu.SemaphoreType.DMA((8,)),
        ],
        compiler_params=pltpu.CompilerParams(vmem_limit_bytes=GRANT),
        cost_estimate=pl.CostEstimate(flops=0, bytes_accessed=4_000_000, transcendentals=0),
    )(asked, *blocks)


def parent_far_body(angle, code, recv, ops_hbm, keep, send, ops, sem):
    copy = pltpu.make_async_copy(ops_hbm, ops.at[pl.ds(0, 40)], sem)
    copy.start()
    ops[40] = jnp.zeros(ops.shape[1:], BF16)
    copy.wait()

    def pair(i, carry):
        for odd, out in enumerate((keep, send)):
            for q in range(2):
                r = (angle[0] ^ (2 * i + odd)) * 2 + q
                real = [jnp.zeros((8, 128), F32) for _ in range(4)]
                imag = [jnp.zeros((8, 128), F32) for _ in range(4)]
                for j in range(8):
                    both = code[j, r]
                    at, op = both >> 6, both & 63
                    for t in range(4):
                        u, v = t // 2, t % 2
                        a = ops[op, 0, u * 8 : u * 8 + 8, v * 128 : v * 128 + 128].astype(F32)
                        b = ops[op, 1, u * 8 : u * 8 + 8, v * 128 : v * 128 + 128].astype(F32)
                        c = recv[at, t].astype(F32)
                        d = recv[at, 4 + t].astype(F32)
                        real[t] = real[t] + (a * c - b * d)
                        imag[t] = imag[t] + (a * d + b * c)
                for t in range(4):
                    out[i, q, t] = real[t].astype(BF16)
                    out[i, q, 4 + t] = imag[t].astype(BF16)
        return carry

    lax.fori_loop(0, 4, pair, 0)


def far_parents(angle, code, recv, ops):
    return pl.pallas_call(
        parent_far_body,
        out_shape=(jax.ShapeDtypeStruct((4, 2, 8, 8, 128), BF16),) * 2,
        in_specs=[
            pl.BlockSpec(memory_space=pltpu.SMEM),
            pl.BlockSpec(memory_space=pltpu.SMEM),
            pl.BlockSpec(memory_space=VM),
            pl.BlockSpec(memory_space=ANY),
        ],
        out_specs=(pl.BlockSpec(memory_space=VM),) * 2,
        scratch_shapes=[pltpu.VMEM((41, 2, 16, PP), BF16), pltpu.SemaphoreType.DMA],
        cost_estimate=pl.CostEstimate(flops=10_000_000, bytes_accessed=3_500_000, transcendentals=0),
        compiler_params=pltpu.CompilerParams(vmem_limit_bytes=GRANT),
        name="far_parents",
    )(angle, code, recv, ops)


CAME = ((0, 0), (1, 0), (2, 0), (2, 1), (3, 0), (3, 1), (4, 0), (4, 1))


def trade(keep, send):
    def across(x, bit):
        return lax.ppermute(x, "angle", [(i, i ^ bit) for i in range(8)])

    other = across(send, 1)
    return keep, other, *(across(jnp.concatenate([keep[i : i + 1], other[i : i + 1]]), 2 * i) for i in (1, 2, 3))


def child_far_body(angle, code, recv, ops_hbm, t0, t1, t2, t3, t4, out, ops, sem):
    copy = pltpu.make_async_copy(ops_hbm, ops.at[pl.ds(0, 40)], sem)
    copy.start()
    ops[40] = jnp.zeros(ops.shape[1:], BF16)
    copy.wait()
    terms = (t0, t1, t2, t3, t4)

    for s, (which, place) in enumerate(CAME):

        def row(k, carry):
            r = (angle[0] ^ s) * 8 + k
            real = jnp.zeros((8, 128), F32)
            imag = jnp.zeros((8, 128), F32)
            for j in range(8):
                both = code[j, r]
                at, op = both >> 6, both & 63
                a, b = ops[op, 0].astype(F32), ops[op, 1].astype(F32)
                c, d = recv[at, 0].astype(F32), recv[at, 1].astype(F32)
                real = real + (a * c - b * d)
                imag = imag + (a * d + b * c)
            out[r, 0] = (real + terms[which][place, k, 0].astype(F32)).astype(BF16)
            out[r, 1] = (imag + terms[which][place, k, 1].astype(F32)).astype(BF16)
            return carry

        lax.fori_loop(0, 8, row, 0, unroll=2)


def far_children(angle, code, recv, ops, terms):
    return pl.pallas_call(
        child_far_body,
        out_shape=jax.ShapeDtypeStruct((64, 2, 8, 128), BF16),
        in_specs=[
            pl.BlockSpec(memory_space=pltpu.SMEM),
            pl.BlockSpec(memory_space=pltpu.SMEM),
            pl.BlockSpec(memory_space=VM),
            pl.BlockSpec(memory_space=ANY),
        ]
        + [pl.BlockSpec(memory_space=VM)] * 5,
        out_specs=pl.BlockSpec(memory_space=VM),
        scratch_shapes=[pltpu.VMEM((41, 2, 8, 128), BF16), pltpu.SemaphoreType.DMA],
        compiler_params=pltpu.CompilerParams(vmem_limit_bytes=GRANT),
        name="far_children",
    )(angle, code, recv, ops, *terms)


def down_body(angle, f0, f1, f2, f3, f4, theta_h, phi_h, cos_h, sin_h, keep, send, theta, phi, cos_t, sin_t, turned, whole, sems):
    far = (f0, f1, f2, f3, f4)
    for copy in fetch((theta_h, phi_h, cos_h, sin_h), (theta, phi, cos_t, sin_t), sems):
        copy.wait()
    for s, (which, place) in enumerate(CAME):
        at = pl.ds(pl.multiple_of((angle[0] ^ s) * 16, 16), 16)
        cos_s = [cos_t[t, at, :] for t in range(2)]
        sin_s = [sin_t[t, at, :] for t in range(2)]
        for q in range(2):
            re, im = (
                jnp.concatenate(
                    [
                        jnp.concatenate(
                            [far[which][place, q, c * 4 + u * 2 + v].astype(F32) for v in range(2)], axis=1
                        )
                        for u in range(2)
                    ],
                    axis=0,
                )
                for c in range(2)
            )
            for t, (k, m) in enumerate(((0, 3), (1, 2))):
                cs, sn = cos_s[t], sin_s[t]
                cr, si, ci, sr = cs * re, sn * im, cs * im, sn * re
                turned[(q * 4 + k) * 2, at, :] = (cr + si).astype(BF16)
                turned[(q * 4 + k) * 2 + 1, at, :] = (ci - sr).astype(BF16)
                turned[(q * 4 + m) * 2, at, :] = (cr - si).astype(BF16)
                turned[(q * 4 + m) * 2 + 1, at, :] = (ci + sr).astype(BF16)
    for r in range(8):
        for c in range(2):
            narrowed = bmm(turned[r * 2 + c], phi[...]).astype(BF16)
            whole[r * 2 + c] = bmm(theta[...], narrowed)
    for s in range(8):
        at = pl.ds(pl.multiple_of((angle[0] ^ s) * 8, 8), 8)
        for r in range(8):
            for c in range(2):
                (keep, send)[s % 2][s // 2, r, c] = whole[r * 2 + c, at, :].astype(BF16)


def lower(angle, far, tables):
    return pl.pallas_call(
        down_body,
        out_shape=(jax.ShapeDtypeStruct((4, 8, 2, 8, 128), BF16),) * 2,
        in_specs=[pl.BlockSpec(memory_space=pltpu.SMEM)]
        + [pl.BlockSpec(memory_space=VM)] * 5
        + [pl.BlockSpec(memory_space=pltpu.HBM)] * 4,
        out_specs=(pl.BlockSpec(memory_space=VM),) * 2,
        scratch_shapes=[pltpu.VMEM(t.shape, t.dtype) for t in tables]
        + [
            pltpu.VMEM((16, PT, PP), BF16),
            pltpu.VMEM((16, CT, SUBBOX_HEADINGS), F32),
            pltpu.SemaphoreType.DMA((4,)),
        ],
        cost_estimate=pl.CostEstimate(flops=300_000_000, bytes_accessed=2_000_000, transcendentals=0),
        compiler_params=pltpu.CompilerParams(vmem_limit_bytes=GRANT),
        name="lower",
    )(angle, *far, *tables)


def groups(straight):
    found = []
    for angle in range(8):
        for o in range(SIDE):
            line = [(o, i) if (angle % 2) == straight else (i, o) for i in range(SIDE)]
            found.append([(y * SIDE + z) * 8 + angle for y, z in line])
    return found


SPREAD, TRADE = groups(1), groups(0)


def hop(x, step):
    pairs = [(g[i], g[(i + step) % SIDE]) for g in SPREAD for i in range(SIDE)]
    return lax.ppermute(x, BOTH, pairs)


def ring(own):
    forth, back = [own], [own]
    for step in range(4):
        forth.append(hop(forth[-1], 1))
        if step < 3:
            back.append(hop(back[-1], -1))
    return back + [forth[8 - p] for p in range(4, 8)]


def swap(x, axis, **kw):
    return lax.all_to_all(x, axis, split_axis=0, concat_axis=0, tiled=True, **kw)


def local(
    child_field,
    child_list,
    child_op,
    child_home,
    child_ops,
    parent_list,
    parent_op,
    parent_home,
    parent_ops,
):
    theta_up = jnp.asarray(fourier_table(PT, CT, 0.5)).astype(BF16)
    phi_up = jnp.asarray(np.ascontiguousarray(fourier_table(PP, SUBBOX_HEADINGS, 0.0).T)).astype(BF16)
    theta_down = jnp.asarray(np.ascontiguousarray(fourier_table(PT, CT, 0.5).T) * np.float32(CT / PT)).astype(BF16)
    phi_down = jnp.asarray(
        fourier_table(PP, SUBBOX_HEADINGS, 0.0) * np.float32(SUBBOX_HEADINGS / PP)
    ).astype(BF16)
    cos_np, sin_np = shift_tables()
    cos_t, sin_t = jnp.asarray(cos_np), jnp.asarray(sin_np)

    box, angle = lax.axis_index("box"), lax.axis_index("angle")
    core = angle % 2
    mine = jnp.where(core == 0, box // SIDE, box % SIDE)
    where = jnp.stack([core, mine]).astype(I32)

    whole = swap(child_field, "angle").reshape(8, 8, 2, 8, 128)
    wanted, child_code, parent_code = plan(where, child_list, child_op, child_home, parent_list, parent_op, parent_home)
    parents = swap(lift(whole, (theta_up, phi_up, cos_t, sin_t)), "angle").reshape(128, 8, 128)
    parent_blocks = ring(parents)
    asked = swap(wanted.reshape(SIDE, 1, 128), BOTH, axis_index_groups=TRADE).reshape(SIDE, 128)
    parents_out = select(asked, parent_blocks, 64, 8, 16)
    field, parents_out = lax.optimization_barrier((child_field, parents_out))
    parents_in = swap(parents_out, BOTH, axis_index_groups=TRADE)
    child_blocks = ring(field.reshape(128, 8, 128))
    children_out = select(asked, child_blocks, 0, 2, 64)
    here = angle.reshape(1).astype(I32)
    sums = far_parents(here, parent_code, parents_in.reshape(128, 8, 8, 128), parent_ops)
    children_out, sums = lax.optimization_barrier((children_out, sums))
    children_in = swap(children_out, BOTH, axis_index_groups=TRADE)
    far = trade(*sums)
    terms = trade(*lower(here, far, (theta_down, phi_down, cos_t, sin_t)))
    return far_children(here, child_code, children_in.reshape(512, 2, 8, 128), child_ops, terms)


def solution(mesh):
    return jax.shard_map(
        local,
        mesh=mesh,
        in_specs=(
            P("box", None, "angle", None),
            P("box", None),
            P("box", None),
            P(),
            P(None, None, "angle", None),
            P("box", None),
            P("box", None),
            P(),
            P(None, None, "angle", None),
        ),
        out_specs=P("box", None, "angle", None),
        check_vma=False,
    )
```

```python
import math

import jax
import jax.numpy as jnp
import numpy as np
from jax import lax
from jax.experimental import pallas as pl
from jax.experimental.pallas import tpu as pltpu
from jax.sharding import PartitionSpec as P


CT = 64
SUBBOX_HEADINGS = 128
PT = 128
PP = 256
WAVE_NUMBER = 6.0
SIDE = 8
BOTH = ("box", "angle")
F32, BF16, I32 = jnp.float32, jnp.bfloat16, jnp.int32
VM = pltpu.VMEM
ANY = pl.ANY
GRANT = 12 << 20


def fourier_table(fine_count, coarse_count, offset):
    f32 = np.float32
    fine = (np.arange(fine_count, dtype=f32) + f32(offset)) / f32(fine_count)
    coarse = (np.arange(coarse_count, dtype=f32) + f32(offset)) / f32(coarse_count)
    x = fine[:, None] - coarse[None, :]
    harmonic = np.arange(1, coarse_count // 2, dtype=f32)
    cosines = np.cos(f32(2.0 * math.pi) * harmonic * x[:, :, None])
    summed = f32(1.0) + f32(2.0) * cosines.sum(2, dtype=np.float64) + np.cos(f32(math.pi * coarse_count) * x)
    return (summed / coarse_count).astype(f32)


def shift_tables():
    f32 = np.float32
    polar = (f32(math.pi) * (np.arange(PT, dtype=f32) + f32(0.5)) / f32(PT)).astype(f32)
    heading = (f32(2.0 * math.pi / PP) * np.arange(PP, dtype=f32)).astype(f32)
    cos_h, sin_h = np.cos(heading), np.sin(heading)
    across = np.stack([-cos_h - sin_h, cos_h - sin_h])
    arg = (f32(WAVE_NUMBER) * np.sin(polar))[None, :, None] * across[:, None, :]
    return np.cos(arg).astype(f32), np.sin(arg).astype(f32)


def bmm(a, b):
    return lax.dot_general(a, b, (((1,), (0,)), ((), ())), preferred_element_type=F32)


def iota(shape, dim):
    return lax.broadcasted_iota(I32, shape, dim)


def plan_level(ids_ref, op_ref, home_ref, core, mine, other, rows_device, cap, empty_op, code_ref):
    slots, rows = ids_ref.shape
    home = home_ref[...]
    owner = home // rows_device
    table = jnp.concatenate([owner, home - owner * rows_device], axis=0).astype(F32).astype(BF16)
    highs = home.shape[0]
    before = (iota((rows, rows), 0) < iota((rows, rows), 1)).astype(F32).astype(BF16)
    carry = jnp.zeros((SIDE, 1), F32)
    wanted = jnp.zeros((2 * SIDE, cap), F32)
    for j in range(slots):
        ids = ids_ref[pl.ds(j, 1), :]
        usable = ids >= 0
        safe = jnp.maximum(ids, 0)
        high, low = safe >> 7, safe & 127
        low_hot = (iota((128, rows), 0) == low).astype(F32).astype(BF16)
        picked = bmm(table, low_hot)
        high_hot = (iota((highs, rows), 0) == high).astype(F32)
        own = jnp.sum(picked[:highs] * high_hot, axis=0, keepdims=True).astype(I32)
        loc = jnp.sum(picked[highs:] * high_hot, axis=0, keepdims=True)
        along_y, along_z = own >> 3, own & 7
        column = jnp.where(core == 0, along_z, along_y)
        place = (jnp.where(core == 0, along_y, along_z) - mine) & 7
        hot = jnp.where((iota((SIDE, rows), 0) == column) & usable, 1.0, 0.0)
        hot_b = hot.astype(BF16)
        prefix = bmm(hot_b, before) + carry
        carry = carry + jnp.sum(hot, axis=1, keepdims=True)
        rank = jnp.sum(hot * prefix, axis=0, keepdims=True).astype(I32)
        lane = column if other is None else (other - column) & 7
        position = lane * cap + rank
        code_ref[pl.ds(j, 1), pl.ds(0, rows)] = jnp.where(
            usable, position * 64 + op_ref[pl.ds(j, 1), :], empty_op
        )
        rank_hot = (iota((cap, rows), 0) == rank).astype(F32).astype(BF16)
        both = jnp.concatenate([hot * place.astype(F32), hot * loc], axis=0).astype(BF16)
        wanted = wanted + lax.dot_general(
            both, rank_hot, (((1,), (1,)), ((), ())), preferred_element_type=F32
        )
    return (wanted[:SIDE] * rows_device + wanted[SIDE:]).astype(I32)


def plan_body(where, cl, co, ch, plist, po, ph, want_ref, ccode_ref, pcode_ref):
    core, mine, other = where[0], where[1], where[2]
    want_ref[...] = jnp.zeros(want_ref.shape, I32)
    want_ref[:, pl.ds(0, 64)] = plan_level(cl, co, ch, core, mine, other, 64, 64, 40, ccode_ref)
    want_ref[:, pl.ds(64, 16)] = plan_level(plist, po, ph, core, mine, None, 16, 16, 40, pcode_ref)


def plan(where, child_list, child_op, child_home, parent_list, parent_op, parent_home):
    args = (
        where,
        child_list.T,
        child_op.T,
        child_home.reshape(-1, 128),
        parent_list.T,
        parent_op.T,
        parent_home.reshape(-1, 128),
    )
    return pl.pallas_call(
        plan_body,
        out_shape=(
            jax.ShapeDtypeStruct((SIDE, 128), I32),
            jax.ShapeDtypeStruct((8, 64), I32),
            jax.ShapeDtypeStruct((8, 16), I32),
        ),
        in_specs=[pl.BlockSpec(memory_space=pltpu.SMEM)] + [pl.BlockSpec(memory_space=VM)] * 6,
        out_specs=(pl.BlockSpec(memory_space=VM),) * 3,
        compiler_params=pltpu.CompilerParams(vmem_limit_bytes=GRANT),
        name="plan",
    )(*args)


def up_body(field, theta_h, phi_h, cos_h, sin_h, out, theta, phi, cos_t, sin_t, wide, sems):
    copies = fetch((theta_h, phi_h, cos_h, sin_h), (theta, phi, cos_t, sin_t), sems)
    copies[0].wait()
    copies[1].wait()
    for r in range(8):
        for c in range(2):
            rows = jnp.concatenate([field[s, r, c] for s in range(8)], axis=0)
            stretched = bmm(theta[...], rows).astype(BF16)
            wide[r * 2 + c] = bmm(stretched, phi[...])
    copies[2].wait()
    copies[3].wait()
    for q in range(2):
        for u in range(PT // 8):
            at = pl.ds(u * 8, 8)
            w = [[wide[(q * 4 + k) * 2 + c, at, :] for c in range(2)] for k in range(4)]
            real = jnp.zeros((8, PP), F32)
            imag = jnp.zeros((8, PP), F32)
            for t, (k, m) in enumerate(((0, 3), (1, 2))):
                cs, sn = cos_t[t, at, :], sin_t[t, at, :]
                real = real + cs * (w[k][0] + w[m][0]) - sn * (w[k][1] - w[m][1])
                imag = imag + cs * (w[k][1] + w[m][1]) + sn * (w[k][0] - w[m][0])
            for c, part in enumerate((real, imag)):
                part = part.astype(BF16)
                for v in range(2):
                    out[u // 2, q, c * 4 + (u % 2) * 2 + v] = part[:, v * 128 : (v + 1) * 128]


def fetch(sources, targets, sems):
    copies = [pltpu.make_async_copy(a, b, sems.at[i]) for i, (a, b) in enumerate(zip(sources, targets))]
    for copy in copies:
        copy.start()
    return copies


def lift(field, tables):
    return pl.pallas_call(
        up_body,
        out_shape=jax.ShapeDtypeStruct((8, 2, 8, 8, 128), BF16),
        in_specs=[pl.BlockSpec(memory_space=VM)] + [pl.BlockSpec(memory_space=pltpu.HBM)] * 4,
        out_specs=pl.BlockSpec(memory_space=VM),
        scratch_shapes=[pltpu.VMEM(t.shape, t.dtype) for t in tables]
        + [pltpu.VMEM((16, PT, PP), F32), pltpu.SemaphoreType.DMA((4,))],
        compiler_params=pltpu.CompilerParams(vmem_limit_bytes=GRANT),
        name="lift",
    )(field, *tables)


def select_body(where, asked, *refs):
    blocks, parents, children = refs[:8], refs[8], refs[9:17]
    pool, parent_buf, child_buf, sems, parent_sems, child_sems = refs[17:]
    copies = [
        pltpu.make_async_copy(
            b.at[pl.ds(128 * half, 128)], pool.at[half, i], sems.at[half, i]
        )
        for half in (1, 0)
        for i, b in enumerate(blocks)
    ]
    for copy in copies:
        copy.start()

    def child_out(d):
        return pltpu.make_async_copy(child_buf.at[d], children[d], child_sems.at[d])

    def parent_out(h):
        return pltpu.make_async_copy(parent_buf.at[h], parents.at[h], parent_sems.at[h])

    for copy in copies[:8]:
        copy.wait()

    def peer(h, carry):
        for k in range(16):
            row = asked[h, 64 + k]
            at = pl.multiple_of((row & 15) * 8, 8)
            parent_buf[h, k] = pool[1, row >> 4, pl.ds(at, 8)]
        parent_out(h).start()
        return carry

    lax.fori_loop(0, SIDE, peer, 0)
    for copy in copies[8:]:
        copy.wait()
    for d in range(SIDE):
        h = (where[2] + d) & 7

        def some(i, carry):
            for j in range(16):
                k = i * 16 + j
                row = asked[h, k]
                at = pl.multiple_of((row & 63) * 2, 2)
                child_buf[d, k] = pool[0, row >> 6, pl.ds(at, 2)]
            return carry

        lax.fori_loop(0, 4, some, 0)
        child_out(d).start()
    for h in range(SIDE):
        parent_out(h).wait()
    for d in range(SIDE):
        child_out(d).wait()


def select(where, asked, blocks):
    hbm = pl.BlockSpec(memory_space=pltpu.HBM)
    return pl.pallas_call(
        select_body,
        out_shape=(pltpu.HBM((SIDE, 16, 8, 8, 128), BF16),) + (pltpu.HBM((64, 2, 8, 128), BF16),) * SIDE,
        in_specs=[pl.BlockSpec(memory_space=pltpu.SMEM)] * 2 + [pl.BlockSpec(memory_space=ANY)] * 8,
        out_specs=(hbm,) * 9,
        scratch_shapes=[
            pltpu.VMEM((2, 8, 128, 8, 128), BF16),
            pltpu.VMEM((SIDE, 16, 8, 8, 128), BF16),
            pltpu.VMEM((SIDE, 64, 2, 8, 128), BF16),
            pltpu.SemaphoreType.DMA((2, 8)),
            pltpu.SemaphoreType.DMA((8,)),
            pltpu.SemaphoreType.DMA((8,)),
        ],
        compiler_params=pltpu.CompilerParams(vmem_limit_bytes=GRANT),
        name="select",
    )(where, asked, *blocks)


def parent_far_body(code, recv, ops_hbm, out, ops, sem):
    copy = pltpu.make_async_copy(ops_hbm, ops.at[pl.ds(0, 40)], sem)
    copy.start()
    ops[40] = jnp.zeros(ops.shape[1:], BF16)
    copy.wait()

    def row(r, carry):
        real = [jnp.zeros((8, 128), F32) for _ in range(4)]
        imag = [jnp.zeros((8, 128), F32) for _ in range(4)]
        for j in range(8):
            both = code[j, r]
            at, op = both >> 6, both & 63
            for t in range(4):
                u, v = t // 2, t % 2
                a = ops[op, 0, u * 8 : u * 8 + 8, v * 128 : v * 128 + 128].astype(F32)
                b = ops[op, 1, u * 8 : u * 8 + 8, v * 128 : v * 128 + 128].astype(F32)
                c = recv[at, t].astype(F32)
                d = recv[at, 4 + t].astype(F32)
                real[t] = real[t] + (a * c - b * d)
                imag[t] = imag[t] + (a * d + b * c)
        for t in range(4):
            out[r, t] = real[t].astype(BF16)
            out[r, 4 + t] = imag[t].astype(BF16)
        return carry

    lax.fori_loop(0, 16, row, 0)


def far_parents(code, recv, ops):
    return pl.pallas_call(
        parent_far_body,
        out_shape=jax.ShapeDtypeStruct((16, 8, 8, 128), BF16),
        in_specs=[
            pl.BlockSpec(memory_space=pltpu.SMEM),
            pl.BlockSpec(memory_space=VM),
            pl.BlockSpec(memory_space=ANY),
        ],
        out_specs=pl.BlockSpec(memory_space=VM),
        scratch_shapes=[pltpu.VMEM((41, 2, 16, PP), BF16), pltpu.SemaphoreType.DMA],
        compiler_params=pltpu.CompilerParams(vmem_limit_bytes=GRANT),
        name="far_parents",
    )(code, recv, ops)


def child_far_body(code, *refs):
    blocks, ops_hbm, term, out, recv, ops, sems = refs[:8], *refs[8:]
    copies = fetch((ops_hbm, *blocks), (ops.at[pl.ds(0, 40)], *(recv.at[i] for i in range(8))), sems)
    ops[40] = jnp.zeros(ops.shape[1:], BF16)
    for copy in copies:
        copy.wait()

    def row(r, carry):
        real = jnp.zeros((8, 128), F32)
        imag = jnp.zeros((8, 128), F32)
        for j in range(8):
            both = code[j, r]
            lane, at, op = both >> 12, (both >> 6) & 63, both & 63
            a, b = ops[op, 0].astype(F32), ops[op, 1].astype(F32)
            c, d = recv[lane, at, 0].astype(F32), recv[lane, at, 1].astype(F32)
            real = real + (a * c - b * d)
            imag = imag + (a * d + b * c)
        out[r, 0] = (real + term[r, 0].astype(F32)).astype(BF16)
        out[r, 1] = (imag + term[r, 1].astype(F32)).astype(BF16)
        return carry

    lax.fori_loop(0, 64, row, 0, unroll=2)


def far_children(code, blocks, ops, term):
    return pl.pallas_call(
        child_far_body,
        out_shape=jax.ShapeDtypeStruct((64, 2, 8, 128), BF16),
        in_specs=[pl.BlockSpec(memory_space=pltpu.SMEM)]
        + [pl.BlockSpec(memory_space=ANY)] * 9
        + [pl.BlockSpec(memory_space=VM)],
        out_specs=pl.BlockSpec(memory_space=VM),
        scratch_shapes=[
            pltpu.VMEM((SIDE, 64, 2, 8, 128), BF16),
            pltpu.VMEM((41, 2, 8, 128), BF16),
            pltpu.SemaphoreType.DMA((9,)),
        ],
        compiler_params=pltpu.CompilerParams(vmem_limit_bytes=GRANT),
        name="far_children",
    )(code, *blocks, ops, term)


def down_body(far, theta_h, phi_h, cos_h, sin_h, out, theta, phi, cos_t, sin_t, turned, sems):
    for copy in fetch((theta_h, phi_h, cos_h, sin_h), (theta, phi, cos_t, sin_t), sems):
        copy.wait()
    for q in range(2):
        for u in range(PT // 8):
            at = pl.ds(u * 8, 8)
            re, im = (
                jnp.concatenate(
                    [far[u // 2, q, c * 4 + (u % 2) * 2 + v].astype(F32) for v in range(2)], axis=1
                )
                for c in range(2)
            )
            for t, (k, m) in enumerate(((0, 3), (1, 2))):
                cs, sn = cos_t[t, at, :], sin_t[t, at, :]
                cr, si, ci, sr = cs * re, sn * im, cs * im, sn * re
                turned[(q * 4 + k) * 2, at, :] = (cr + si).astype(BF16)
                turned[(q * 4 + k) * 2 + 1, at, :] = (ci - sr).astype(BF16)
                turned[(q * 4 + m) * 2, at, :] = (cr - si).astype(BF16)
                turned[(q * 4 + m) * 2 + 1, at, :] = (ci + sr).astype(BF16)
    for r in range(8):
        for c in range(2):
            narrowed = bmm(turned[r * 2 + c], phi[...]).astype(BF16)
            term = bmm(theta[...], narrowed).astype(BF16)
            for s in range(8):
                out[s, r, c] = term[s * 8 : s * 8 + 8, :]


def lower(far, tables):
    return pl.pallas_call(
        down_body,
        out_shape=jax.ShapeDtypeStruct((8, 8, 2, 8, 128), BF16),
        in_specs=[pl.BlockSpec(memory_space=VM)] + [pl.BlockSpec(memory_space=pltpu.HBM)] * 4,
        out_specs=pl.BlockSpec(memory_space=VM),
        scratch_shapes=[pltpu.VMEM(t.shape, t.dtype) for t in tables]
        + [pltpu.VMEM((16, PT, PP), BF16), pltpu.SemaphoreType.DMA((4,))],
        compiler_params=pltpu.CompilerParams(vmem_limit_bytes=GRANT),
        name="lower",
    )(far, *tables)


def groups(straight):
    found = []
    for angle in range(8):
        for o in range(SIDE):
            line = [(o, i) if (angle % 2) == straight else (i, o) for i in range(SIDE)]
            found.append([(y * SIDE + z) * 8 + angle for y, z in line])
    return found


SPREAD, TRADE = groups(1), groups(0)


def hop(x, step, lines=SPREAD):
    pairs = [(g[i], g[(i + step) % SIDE]) for g in lines for i in range(SIDE)]
    return lax.ppermute(x, BOTH, pairs)


def swap(x, axis, **kw):
    return lax.all_to_all(x, axis, split_axis=0, concat_axis=0, tiled=True, **kw)


def local(
    child_field,
    child_list,
    child_op,
    child_home,
    child_ops,
    parent_list,
    parent_op,
    parent_home,
    parent_ops,
):
    theta_up = jnp.asarray(fourier_table(PT, CT, 0.5)).astype(BF16)
    phi_up = jnp.asarray(np.ascontiguousarray(fourier_table(PP, SUBBOX_HEADINGS, 0.0).T)).astype(BF16)
    theta_down = jnp.asarray(np.ascontiguousarray(fourier_table(PT, CT, 0.5).T) * np.float32(CT / PT)).astype(BF16)
    phi_down = jnp.asarray(
        fourier_table(PP, SUBBOX_HEADINGS, 0.0) * np.float32(SUBBOX_HEADINGS / PP)
    ).astype(BF16)
    cos_np, sin_np = shift_tables()
    cos_t, sin_t = jnp.asarray(cos_np), jnp.asarray(sin_np)

    box, angle = lax.axis_index("box"), lax.axis_index("angle")
    core = angle % 2
    mine = jnp.where(core == 0, box // SIDE, box % SIDE)
    other = jnp.where(core == 0, box % SIDE, box // SIDE)
    where = jnp.stack([core, mine, other]).astype(I32)

    hold = lambda x: pltpu.with_memory_space_constraint(x, pltpu.HBM)
    whole = swap(child_field, "angle").reshape(8, 8, 2, 8, 128)
    parents = swap(lift(whole, tuple(map(hold, (theta_up, phi_up, cos_t, sin_t)))), "angle")
    wanted, child_code, parent_code = plan(
        where, child_list, child_op, child_home, parent_list, parent_op, parent_home
    )
    own = jnp.concatenate([child_field.reshape(128, 8, 128), parents.reshape(128, 8, 128)])
    forth, back = [own], [own]
    for step in range(4):
        if step == 1:
            forth[1], wanted = lax.optimization_barrier((forth[1], wanted))
        forth.append(hop(forth[-1], 1))
        if step < 3:
            back.append(hop(back[-1], -1))
    blocks = back + [forth[8 - p] for p in range(4, 8)]
    asked = swap(wanted.reshape(SIDE, 1, 128), BOTH, axis_index_groups=TRADE).reshape(SIDE, 128)
    parents_out, *children_out = select(where, asked, blocks)
    parents_in = swap(parents_out, BOTH, axis_index_groups=TRADE)
    children_in = {0: children_out[0]}
    for d in (4, 3, 5, 2, 6, 1, 7):
        children_in[d] = hop(children_out[d], d, TRADE)
    sums = far_parents(parent_code, parents_in.reshape(128, 8, 8, 128), parent_ops)
    turned = swap(sums, "angle").reshape(8, 2, 8, 8, 128)
    terms = swap(lower(turned, tuple(map(hold, (theta_down, phi_down, cos_t, sin_t)))), "angle")
    return far_children(
        child_code, [children_in[d] for d in range(SIDE)], child_ops, terms.reshape(64, 2, 8, 128)
    )


def solution(mesh):
    return jax.shard_map(
        local,
        mesh=mesh,
        in_specs=(
            P("box", None, "angle", None),
            P("box", None),
            P("box", None),
            P(),
            P(None, None, "angle", None),
            P("box", None),
            P("box", None),
            P(),
            P(None, None, "angle", None),
        ),
        out_specs=P("box", None, "angle", None),
        check_vma=False,
    )
```

```python
import math

import jax
import jax.numpy as jnp
import numpy as np
from jax import lax
from jax.experimental import pallas as pl
from jax.experimental.pallas import tpu as pltpu
from jax.sharding import PartitionSpec as P


CT = 64
SUBBOX_HEADINGS = 128
PT = 128
PP = 256
WAVE_NUMBER = 6.0
SIDE = 8
BOTH = ("box", "angle")
F32, BF16, I32 = jnp.float32, jnp.bfloat16, jnp.int32
VM = pltpu.VMEM
ANY = pl.ANY
GRANT = 12 << 20


def fourier_table(fine_count, coarse_count, offset):
    f32 = np.float32
    fine = (np.arange(fine_count, dtype=f32) + f32(offset)) / f32(fine_count)
    coarse = (np.arange(coarse_count, dtype=f32) + f32(offset)) / f32(coarse_count)
    x = fine[:, None] - coarse[None, :]
    harmonic = np.arange(1, coarse_count // 2, dtype=f32)
    cosines = np.cos(f32(2.0 * math.pi) * harmonic * x[:, :, None])
    summed = f32(1.0) + f32(2.0) * cosines.sum(2, dtype=np.float64) + np.cos(f32(math.pi * coarse_count) * x)
    return (summed / coarse_count).astype(f32)


def shift_tables():
    f32 = np.float32
    polar = (f32(math.pi) * (np.arange(PT, dtype=f32) + f32(0.5)) / f32(PT)).astype(f32)
    heading = (f32(2.0 * math.pi / PP) * np.arange(PP, dtype=f32)).astype(f32)
    cos_h, sin_h = np.cos(heading), np.sin(heading)
    across = np.stack([-cos_h - sin_h, cos_h - sin_h])
    arg = (f32(WAVE_NUMBER) * np.sin(polar))[None, :, None] * across[:, None, :]
    return np.cos(arg).astype(f32), np.sin(arg).astype(f32)


def bmm(a, b):
    return lax.dot_general(a, b, (((1,), (0,)), ((), ())), preferred_element_type=F32)


def iota(shape, dim):
    return lax.broadcasted_iota(I32, shape, dim)


def plan_level(ids_ref, op_ref, home_ref, core, mine, other, rows_device, cap, empty_op, code_ref):
    slots, rows = ids_ref.shape
    home = home_ref[...]
    owner = home // rows_device
    table = jnp.concatenate([owner, home - owner * rows_device], axis=0).astype(F32).astype(BF16)
    highs = home.shape[0]
    before = (iota((rows, rows), 0) < iota((rows, rows), 1)).astype(F32).astype(BF16)
    carry = jnp.zeros((SIDE, 1), F32)
    wanted = jnp.zeros((2 * SIDE, cap), F32)
    for j in range(slots):
        ids = ids_ref[pl.ds(j, 1), :]
        usable = ids >= 0
        safe = jnp.maximum(ids, 0)
        high, low = safe >> 7, safe & 127
        low_hot = (iota((128, rows), 0) == low).astype(F32).astype(BF16)
        picked = bmm(table, low_hot)
        high_hot = (iota((highs, rows), 0) == high).astype(F32)
        own = jnp.sum(picked[:highs] * high_hot, axis=0, keepdims=True).astype(I32)
        loc = jnp.sum(picked[highs:] * high_hot, axis=0, keepdims=True)
        along_y, along_z = own >> 3, own & 7
        column = jnp.where(core == 0, along_z, along_y)
        place = (jnp.where(core == 0, along_y, along_z) - mine) & 7
        hot = jnp.where((iota((SIDE, rows), 0) == column) & usable, 1.0, 0.0)
        hot_b = hot.astype(BF16)
        prefix = bmm(hot_b, before) + carry
        carry = carry + jnp.sum(hot, axis=1, keepdims=True)
        rank = jnp.sum(hot * prefix, axis=0, keepdims=True).astype(I32)
        lane = column if other is None else (other - column) & 7
        position = lane * cap + rank
        code_ref[pl.ds(j, 1), pl.ds(0, rows)] = jnp.where(
            usable, position * 64 + op_ref[pl.ds(j, 1), :], empty_op
        )
        rank_hot = (iota((cap, rows), 0) == rank).astype(F32).astype(BF16)
        both = jnp.concatenate([hot * place.astype(F32), hot * loc], axis=0).astype(BF16)
        wanted = wanted + lax.dot_general(
            both, rank_hot, (((1,), (1,)), ((), ())), preferred_element_type=F32
        )
    return (wanted[:SIDE] * rows_device + wanted[SIDE:]).astype(I32)


def plan_body(where, cl, co, ch, plist, po, ph, want_ref, ccode_ref, pcode_ref):
    core, mine, other = where[0], where[1], where[2]
    want_ref[...] = jnp.zeros(want_ref.shape, I32)
    want_ref[:, pl.ds(0, 64)] = plan_level(cl, co, ch, core, mine, other, 64, 64, 40, ccode_ref)
    want_ref[:, pl.ds(64, 16)] = plan_level(plist, po, ph, core, mine, None, 16, 16, 40, pcode_ref)


def plan(where, child_list, child_op, child_home, parent_list, parent_op, parent_home):
    args = (
        where,
        child_list.T,
        child_op.T,
        child_home.reshape(-1, 128),
        parent_list.T,
        parent_op.T,
        parent_home.reshape(-1, 128),
    )
    return pl.pallas_call(
        plan_body,
        out_shape=(
            jax.ShapeDtypeStruct((SIDE, 128), I32),
            pltpu.HBM((8, 64), I32),
            pltpu.HBM((8, 16), I32),
        ),
        in_specs=[pl.BlockSpec(memory_space=pltpu.SMEM)] + [pl.BlockSpec(memory_space=VM)] * 6,
        out_specs=(pl.BlockSpec(memory_space=VM),) * 3,
        compiler_params=pltpu.CompilerParams(vmem_limit_bytes=GRANT),
        name="plan",
    )(*args)


def up_body(field, theta_h, phi_h, cos_h, sin_h, out, theta, phi, cos_t, sin_t, wide, sems):
    copies = fetch((theta_h, phi_h, cos_h, sin_h), (theta, phi, cos_t, sin_t), sems)
    copies[0].wait()
    copies[1].wait()
    for r in range(8):
        for c in range(2):
            rows = jnp.concatenate([field[s, r, c] for s in range(8)], axis=0)
            stretched = bmm(theta[...], rows).astype(BF16)
            wide[r * 2 + c] = bmm(stretched, phi[...])
    copies[2].wait()
    copies[3].wait()
    for q in range(2):
        for u in range(PT // 8):
            at = pl.ds(u * 8, 8)
            w = [[wide[(q * 4 + k) * 2 + c, at, :] for c in range(2)] for k in range(4)]
            real = jnp.zeros((8, PP), F32)
            imag = jnp.zeros((8, PP), F32)
            for t, (k, m) in enumerate(((0, 3), (1, 2))):
                cs, sn = cos_t[t, at, :], sin_t[t, at, :]
                real = real + cs * (w[k][0] + w[m][0]) - sn * (w[k][1] - w[m][1])
                imag = imag + cs * (w[k][1] + w[m][1]) + sn * (w[k][0] - w[m][0])
            for c, part in enumerate((real, imag)):
                part = part.astype(BF16)
                for v in range(2):
                    out[u // 2, q, c * 4 + (u % 2) * 2 + v] = part[:, v * 128 : (v + 1) * 128]


def fetch(sources, targets, sems):
    copies = [pltpu.make_async_copy(a, b, sems.at[i]) for i, (a, b) in enumerate(zip(sources, targets))]
    for copy in copies:
        copy.start()
    return copies


def lift(field, tables):
    return pl.pallas_call(
        up_body,
        out_shape=jax.ShapeDtypeStruct((8, 2, 8, 8, 128), BF16),
        in_specs=[pl.BlockSpec(memory_space=VM)] + [pl.BlockSpec(memory_space=pltpu.HBM)] * 4,
        out_specs=pl.BlockSpec(memory_space=VM),
        scratch_shapes=[pltpu.VMEM(t.shape, t.dtype) for t in tables]
        + [pltpu.VMEM((16, PT, PP), F32), pltpu.SemaphoreType.DMA((4,))],
        compiler_params=pltpu.CompilerParams(vmem_limit_bytes=GRANT),
        name="lift",
    )(field, *tables)


def select_body(where, asked, *refs):
    blocks, parents, children = refs[:8], refs[8], refs[9:17]
    pool, parent_buf, child_buf, sems, parent_sems, child_sems = refs[17:]
    copies = [
        pltpu.make_async_copy(
            b.at[pl.ds(128 * half, 128)], pool.at[half, i], sems.at[half, i]
        )
        for half in (1, 0)
        for i, b in enumerate(blocks)
    ]
    for copy in copies:
        copy.start()

    def child_out(d):
        return pltpu.make_async_copy(child_buf.at[d], children[d], child_sems.at[d])

    def parent_out(h):
        return pltpu.make_async_copy(parent_buf.at[h], parents.at[h], parent_sems.at[h])

    for copy in copies[:8]:
        copy.wait()

    def peer(h, carry):
        for k in range(16):
            row = asked[h, 64 + k]
            at = pl.multiple_of((row & 15) * 8, 8)
            parent_buf[h, k] = pool[1, row >> 4, pl.ds(at, 8)]
        parent_out(h).start()
        return carry

    lax.fori_loop(0, SIDE, peer, 0)
    for copy in copies[8:]:
        copy.wait()
    for d in range(SIDE):
        h = (where[2] + d) & 7

        def some(i, carry):
            for j in range(16):
                k = i * 16 + j
                row = asked[h, k]
                at = pl.multiple_of((row & 63) * 2, 2)
                child_buf[d, k] = pool[0, row >> 6, pl.ds(at, 2)]
            return carry

        lax.fori_loop(0, 4, some, 0)
        child_out(d).start()
    for h in range(SIDE):
        parent_out(h).wait()
    for d in range(SIDE):
        child_out(d).wait()


def select(where, asked, blocks):
    hbm = pl.BlockSpec(memory_space=pltpu.HBM)
    return pl.pallas_call(
        select_body,
        out_shape=(pltpu.HBM((SIDE, 16, 8, 8, 128), BF16),) + (pltpu.HBM((64, 2, 8, 128), BF16),) * SIDE,
        in_specs=[pl.BlockSpec(memory_space=pltpu.SMEM)] * 2 + [pl.BlockSpec(memory_space=ANY)] * 8,
        out_specs=(hbm,) * 9,
        scratch_shapes=[
            pltpu.VMEM((2, 8, 128, 8, 128), BF16),
            pltpu.VMEM((SIDE, 16, 8, 8, 128), BF16),
            pltpu.VMEM((SIDE, 64, 2, 8, 128), BF16),
            pltpu.SemaphoreType.DMA((2, 8)),
            pltpu.SemaphoreType.DMA((8,)),
            pltpu.SemaphoreType.DMA((8,)),
        ],
        compiler_params=pltpu.CompilerParams(vmem_limit_bytes=GRANT),
        name="select",
    )(where, asked, *blocks)


def parent_far_body(code, recv, ops_hbm, out, ops, sem):
    copy = pltpu.make_async_copy(ops_hbm, ops.at[pl.ds(0, 40)], sem)
    copy.start()
    ops[40] = jnp.zeros(ops.shape[1:], BF16)
    copy.wait()

    def row(r, carry):
        real = [jnp.zeros((8, 128), F32) for _ in range(4)]
        imag = [jnp.zeros((8, 128), F32) for _ in range(4)]
        for j in range(8):
            both = code[j, r]
            at, op = both >> 6, both & 63
            for t in range(4):
                u, v = t // 2, t % 2
                a = ops[op, 0, u * 8 : u * 8 + 8, v * 128 : v * 128 + 128].astype(F32)
                b = ops[op, 1, u * 8 : u * 8 + 8, v * 128 : v * 128 + 128].astype(F32)
                c = recv[at, t].astype(F32)
                d = recv[at, 4 + t].astype(F32)
                real[t] = real[t] + (a * c - b * d)
                imag[t] = imag[t] + (a * d + b * c)
        for t in range(4):
            out[r, t] = real[t].astype(BF16)
            out[r, 4 + t] = imag[t].astype(BF16)
        return carry

    lax.fori_loop(0, 16, row, 0)


def far_parents(code, recv, ops):
    return pl.pallas_call(
        parent_far_body,
        out_shape=jax.ShapeDtypeStruct((16, 8, 8, 128), BF16),
        in_specs=[
            pl.BlockSpec(memory_space=pltpu.SMEM),
            pl.BlockSpec(memory_space=VM),
            pl.BlockSpec(memory_space=ANY),
        ],
        out_specs=pl.BlockSpec(memory_space=VM),
        scratch_shapes=[pltpu.VMEM((41, 2, 16, PP), BF16), pltpu.SemaphoreType.DMA],
        compiler_params=pltpu.CompilerParams(vmem_limit_bytes=GRANT),
        name="far_parents",
    )(code, recv, ops)


def child_far_body(code, *refs):
    blocks, ops_hbm, out, recv, ops, sems = refs[:8], *refs[8:]
    copies = fetch((ops_hbm, *blocks), (ops.at[pl.ds(0, 40)], *(recv.at[i] for i in range(8))), sems)
    ops[40] = jnp.zeros(ops.shape[1:], BF16)
    for copy in copies:
        copy.wait()

    def row(r, carry):
        real = jnp.zeros((8, 128), F32)
        imag = jnp.zeros((8, 128), F32)
        for j in range(8):
            both = code[j, r]
            lane, at, op = both >> 12, (both >> 6) & 63, both & 63
            a, b = ops[op, 0].astype(F32), ops[op, 1].astype(F32)
            c, d = recv[lane, at, 0].astype(F32), recv[lane, at, 1].astype(F32)
            real = real + (a * c - b * d)
            imag = imag + (a * d + b * c)
        out[r, 0] = real
        out[r, 1] = imag
        return carry

    lax.fori_loop(0, 64, row, 0, unroll=2)


def far_children(code, blocks, ops):
    return pl.pallas_call(
        child_far_body,
        out_shape=pltpu.HBM((64, 2, 8, 128), F32),
        in_specs=[pl.BlockSpec(memory_space=pltpu.SMEM)] + [pl.BlockSpec(memory_space=ANY)] * 9,
        out_specs=pl.BlockSpec(memory_space=VM),
        scratch_shapes=[
            pltpu.VMEM((SIDE, 64, 2, 8, 128), BF16),
            pltpu.VMEM((41, 2, 8, 128), BF16),
            pltpu.SemaphoreType.DMA((9,)),
        ],
        compiler_params=pltpu.CompilerParams(vmem_limit_bytes=GRANT),
        name="far_children",
    )(code, *blocks, ops)


def down_body(far, theta, phi_h, cos_t, sin_t, out, phi, turned, sem):
    copy = pltpu.make_async_copy(phi_h, phi, sem)
    copy.start()
    for q in range(2):
        for u in range(PT // 8):
            at = pl.ds(u * 8, 8)
            re, im = (
                jnp.concatenate(
                    [far[u // 2, q, c * 4 + (u % 2) * 2 + v].astype(F32) for v in range(2)], axis=1
                )
                for c in range(2)
            )
            for t, (k, m) in enumerate(((0, 3), (1, 2))):
                cs, sn = cos_t[t, at, :], sin_t[t, at, :]
                cr, si, ci, sr = cs * re, sn * im, cs * im, sn * re
                turned[(q * 4 + k) * 2, at, :] = (cr + si).astype(BF16)
                turned[(q * 4 + k) * 2 + 1, at, :] = (ci - sr).astype(BF16)
                turned[(q * 4 + m) * 2, at, :] = (cr - si).astype(BF16)
                turned[(q * 4 + m) * 2 + 1, at, :] = (ci + sr).astype(BF16)
    copy.wait()
    for r in range(8):
        for c in range(2):
            narrowed = bmm(turned[r * 2 + c], phi[...]).astype(BF16)
            term = bmm(theta[...], narrowed).astype(BF16)
            for s in range(8):
                out[s, r, c] = term[s * 8 : s * 8 + 8, :]


def lower(far, tables):
    return pl.pallas_call(
        down_body,
        out_shape=jax.ShapeDtypeStruct((8, 8, 2, 8, 128), BF16),
        in_specs=[pl.BlockSpec(memory_space=ANY if i == 2 else VM) for i in range(5)],
        out_specs=pl.BlockSpec(memory_space=VM),
        scratch_shapes=[
            pltpu.VMEM(tables[1].shape, BF16),
            pltpu.VMEM((16, PT, PP), BF16),
            pltpu.SemaphoreType.DMA,
        ],
        compiler_params=pltpu.CompilerParams(vmem_limit_bytes=GRANT),
        name="lower",
    )(far, *tables)


def groups(straight):
    found = []
    for angle in range(8):
        for o in range(SIDE):
            line = [(o, i) if (angle % 2) == straight else (i, o) for i in range(SIDE)]
            found.append([(y * SIDE + z) * 8 + angle for y, z in line])
    return found


SPREAD, TRADE = groups(1), groups(0)


def hop(x, step, lines=SPREAD):
    pairs = [(g[i], g[(i + step) % SIDE]) for g in lines for i in range(SIDE)]
    return lax.ppermute(x, BOTH, pairs)


def swap(x, axis, **kw):
    return lax.all_to_all(x, axis, split_axis=0, concat_axis=0, tiled=True, **kw)


def local(
    child_field,
    child_list,
    child_op,
    child_home,
    child_ops,
    parent_list,
    parent_op,
    parent_home,
    parent_ops,
):
    theta_up = jnp.asarray(fourier_table(PT, CT, 0.5)).astype(BF16)
    phi_up = jnp.asarray(np.ascontiguousarray(fourier_table(PP, SUBBOX_HEADINGS, 0.0).T)).astype(BF16)
    theta_down = jnp.asarray(np.ascontiguousarray(fourier_table(PT, CT, 0.5).T) * np.float32(CT / PT)).astype(BF16)
    phi_down = jnp.asarray(
        fourier_table(PP, SUBBOX_HEADINGS, 0.0) * np.float32(SUBBOX_HEADINGS / PP)
    ).astype(BF16)
    cos_np, sin_np = shift_tables()
    cos_t, sin_t = jnp.asarray(cos_np), jnp.asarray(sin_np)

    box, angle = lax.axis_index("box"), lax.axis_index("angle")
    core = angle % 2
    mine = jnp.where(core == 0, box // SIDE, box % SIDE)
    other = jnp.where(core == 0, box % SIDE, box // SIDE)
    where = jnp.stack([core, mine, other]).astype(I32)

    hold = lambda x: pltpu.with_memory_space_constraint(x, pltpu.HBM)
    whole = swap(child_field, "angle").reshape(8, 8, 2, 8, 128)
    parents = swap(lift(whole, tuple(map(hold, (theta_up, phi_up, cos_t, sin_t)))), "angle")
    wanted, child_code, parent_code = plan(
        where, child_list, child_op, child_home, parent_list, parent_op, parent_home
    )
    own = jnp.concatenate([child_field.reshape(128, 8, 128), parents.reshape(128, 8, 128)])
    forth, back = [own], [own]
    for step in range(4):
        if step == 1:
            forth[1], wanted = lax.optimization_barrier((forth[1], wanted))
        forth.append(hop(forth[-1], 1))
        if step < 3:
            back.append(hop(back[-1], -1))
    blocks = back + [forth[8 - p] for p in range(4, 8)]
    asked = swap(wanted.reshape(SIDE, 1, 128), BOTH, axis_index_groups=TRADE).reshape(SIDE, 128)
    parents_out, *children_out = select(where, asked, blocks)
    parents_in = swap(parents_out, BOTH, axis_index_groups=TRADE)
    children_in = {0: children_out[0]}
    for d in (4, 3, 5, 2, 6, 1, 7):
        children_in[d] = hop(children_out[d], d, TRADE)
    sums = far_parents(hold(parent_code), parents_in.reshape(128, 8, 8, 128), parent_ops)
    turned = swap(sums, "angle").reshape(8, 2, 8, 8, 128)
    term = lower(turned, (theta_down, hold(phi_down), cos_t, sin_t))
    term = swap(term, "angle").reshape(64, 2, 8, 128)
    child_far = far_children(hold(child_code), [children_in[d] for d in range(SIDE)], child_ops)
    return (child_far + term.astype(F32)).astype(BF16)


def solution(mesh):
    return jax.shard_map(
        local,
        mesh=mesh,
        in_specs=(
            P("box", None, "angle", None),
            P("box", None),
            P("box", None),
            P(),
            P(None, None, "angle", None),
            P("box", None),
            P("box", None),
            P(),
            P(None, None, "angle", None),
        ),
        out_specs=P("box", None, "angle", None),
        check_vma=False,
    )
```

```python
import math

import jax
import jax.numpy as jnp
import numpy as np
from jax import lax
from jax.experimental import pallas as pl
from jax.experimental.pallas import tpu as pltpu
from jax.sharding import PartitionSpec as P


CT = 64
SUBBOX_HEADINGS = 128
PT = 128
PP = 256
WAVE_NUMBER = 6.0
SIDE = 8
ORDER = (4, 3, 5, 2, 6, 1, 7, 0)
BOTH = ("box", "angle")
F32, BF16, I32 = jnp.float32, jnp.bfloat16, jnp.int32
VM = pltpu.VMEM
ANY = pl.ANY
GRANT = 12 << 20


def fourier_table(fine_count, coarse_count, offset):
    f32 = np.float32
    fine = (np.arange(fine_count, dtype=f32) + f32(offset)) / f32(fine_count)
    coarse = (np.arange(coarse_count, dtype=f32) + f32(offset)) / f32(coarse_count)
    x = fine[:, None] - coarse[None, :]
    harmonic = np.arange(1, coarse_count // 2, dtype=f32)
    cosines = np.cos(f32(2.0 * math.pi) * harmonic * x[:, :, None])
    summed = f32(1.0) + f32(2.0) * cosines.sum(2, dtype=np.float64) + np.cos(f32(math.pi * coarse_count) * x)
    return (summed / coarse_count).astype(f32)


def shift_tables():
    f32 = np.float32
    polar = (f32(math.pi) * (np.arange(PT, dtype=f32) + f32(0.5)) / f32(PT)).astype(f32)
    heading = (f32(2.0 * math.pi / PP) * np.arange(PP, dtype=f32)).astype(f32)
    cos_h, sin_h = np.cos(heading), np.sin(heading)
    across = np.stack([-cos_h - sin_h, cos_h - sin_h])
    arg = (f32(WAVE_NUMBER) * np.sin(polar))[None, :, None] * across[:, None, :]
    return np.cos(arg).astype(f32), np.sin(arg).astype(f32)


def bmm(a, b):
    return lax.dot_general(a, b, (((1,), (0,)), ((), ())), preferred_element_type=F32)


def iota(shape, dim):
    return lax.broadcasted_iota(I32, shape, dim)


def plan_level(ids_ref, op_ref, home_ref, core, mine, other, rows_device, cap, empty_op, code_ref):
    slots, rows = ids_ref.shape
    home = home_ref[...]
    owner = home // rows_device
    table = jnp.concatenate([owner, home - owner * rows_device], axis=0).astype(F32).astype(BF16)
    highs = home.shape[0]
    before = (iota((rows, rows), 0) < iota((rows, rows), 1)).astype(F32).astype(BF16)
    carry = jnp.zeros((SIDE, 1), F32)
    wanted = jnp.zeros((2 * SIDE, cap), F32)
    for j in range(slots):
        ids = ids_ref[pl.ds(j, 1), :]
        usable = ids >= 0
        safe = jnp.maximum(ids, 0)
        high, low = safe >> 7, safe & 127
        low_hot = (iota((128, rows), 0) == low).astype(F32).astype(BF16)
        picked = bmm(table, low_hot)
        high_hot = (iota((highs, rows), 0) == high).astype(F32)
        own = jnp.sum(picked[:highs] * high_hot, axis=0, keepdims=True).astype(I32)
        loc = jnp.sum(picked[highs:] * high_hot, axis=0, keepdims=True)
        along_y, along_z = own >> 3, own & 7
        column = jnp.where(core == 0, along_z, along_y)
        place = (jnp.where(core == 0, along_y, along_z) - mine) & 7
        hot = jnp.where((iota((SIDE, rows), 0) == column) & usable, 1.0, 0.0)
        hot_b = hot.astype(BF16)
        prefix = bmm(hot_b, before) + carry
        carry = carry + jnp.sum(hot, axis=1, keepdims=True)
        rank = jnp.sum(hot * prefix, axis=0, keepdims=True).astype(I32)
        lane = column if other is None else (other - column) & 7
        position = lane * cap + rank
        code_ref[pl.ds(j, 1), pl.ds(0, rows)] = jnp.where(
            usable, position * 64 + op_ref[pl.ds(j, 1), :], empty_op
        )
        rank_hot = (iota((cap, rows), 0) == rank).astype(F32).astype(BF16)
        both = jnp.concatenate([hot * place.astype(F32), hot * loc], axis=0).astype(BF16)
        wanted = wanted + lax.dot_general(
            both, rank_hot, (((1,), (1,)), ((), ())), preferred_element_type=F32
        )
    return (wanted[:SIDE] * rows_device + wanted[SIDE:]).astype(I32)


def plan_body(where, cl, co, ch, plist, po, ph, want_ref, ccode_ref, pcode_ref):
    core, mine, other = where[0], where[1], where[2]
    want_ref[...] = jnp.zeros(want_ref.shape, I32)
    want_ref[:, pl.ds(0, 64)] = plan_level(cl, co, ch, core, mine, other, 64, 64, 40, ccode_ref)
    want_ref[:, pl.ds(64, 16)] = plan_level(plist, po, ph, core, mine, None, 16, 16, 40, pcode_ref)


def plan(where, child_list, child_op, child_home, parent_list, parent_op, parent_home):
    args = (
        where,
        child_list.T,
        child_op.T,
        child_home.reshape(-1, 128),
        parent_list.T,
        parent_op.T,
        parent_home.reshape(-1, 128),
    )
    return pl.pallas_call(
        plan_body,
        out_shape=(
            pltpu.HBM((SIDE, 128), I32),
            pltpu.HBM((8, 64), I32),
            pltpu.HBM((8, 16), I32),
        ),
        in_specs=[pl.BlockSpec(memory_space=pltpu.SMEM)] + [pl.BlockSpec(memory_space=VM)] * 6,
        out_specs=(pl.BlockSpec(memory_space=VM),) * 3,
        compiler_params=pltpu.CompilerParams(vmem_limit_bytes=GRANT),
        name="plan",
    )(*args)


def up_body(field, theta_h, phi_h, cos_h, sin_h, out, theta, phi, cos_t, sin_t, wide, sems):
    copies = fetch((theta_h, phi_h, cos_h, sin_h), (theta, phi, cos_t, sin_t), sems)
    copies[0].wait()
    copies[1].wait()
    for r in range(8):
        for c in range(2):
            rows = jnp.concatenate([field[s, r, c] for s in range(8)], axis=0)
            stretched = bmm(theta[...], rows).astype(BF16)
            wide[r * 2 + c] = bmm(stretched, phi[...])
    copies[2].wait()
    copies[3].wait()
    for q in range(2):
        for u in range(PT // 8):
            at = pl.ds(u * 8, 8)
            w = [[wide[(q * 4 + k) * 2 + c, at, :] for c in range(2)] for k in range(4)]
            real = jnp.zeros((8, PP), F32)
            imag = jnp.zeros((8, PP), F32)
            for t, (k, m) in enumerate(((0, 3), (1, 2))):
                cs, sn = cos_t[t, at, :], sin_t[t, at, :]
                real = real + cs * (w[k][0] + w[m][0]) - sn * (w[k][1] - w[m][1])
                imag = imag + cs * (w[k][1] + w[m][1]) + sn * (w[k][0] - w[m][0])
            for c, part in enumerate((real, imag)):
                part = part.astype(BF16)
                for v in range(2):
                    out[u // 2, q, c * 4 + (u % 2) * 2 + v] = part[:, v * 128 : (v + 1) * 128]


def fetch(sources, targets, sems):
    copies = [pltpu.make_async_copy(a, b, sems.at[i]) for i, (a, b) in enumerate(zip(sources, targets))]
    for copy in copies:
        copy.start()
    return copies


def lift(field, tables):
    return pl.pallas_call(
        up_body,
        out_shape=jax.ShapeDtypeStruct((8, 2, 8, 8, 128), BF16),
        in_specs=[pl.BlockSpec(memory_space=VM)] + [pl.BlockSpec(memory_space=pltpu.HBM)] * 4,
        out_specs=pl.BlockSpec(memory_space=VM),
        scratch_shapes=[pltpu.VMEM(t.shape, t.dtype) for t in tables]
        + [pltpu.VMEM((16, PT, PP), F32), pltpu.SemaphoreType.DMA((4,))],
        compiler_params=pltpu.CompilerParams(vmem_limit_bytes=GRANT),
        name="lift",
    )(field, *tables)


def pooled(blocks, first, pool, sems):
    for copy in fetch([b.at[pl.ds(first, 128)] for b in blocks], [pool.at[i] for i in range(8)], sems):
        copy.wait()


def parents_body(asked, *refs):
    blocks, out, pool, buf, sems, out_sems = refs[:8], *refs[8:]
    pooled(blocks, 128, pool, sems)

    def copy_out(h):
        return pltpu.make_async_copy(buf.at[h], out.at[h], out_sems.at[h])

    def peer(h, carry):
        for k in range(16):
            row = asked[h, 64 + k]
            at = pl.multiple_of((row & 15) * 8, 8)
            buf[h, k] = pool[row >> 4, pl.ds(at, 8)]
        copy_out(h).start()
        return carry

    lax.fori_loop(0, SIDE, peer, 0)
    for h in range(SIDE):
        copy_out(h).wait()


def children_body(where, asked, *refs):
    blocks, outs, pool, buf, sems, out_sems = refs[:8], refs[8:16], *refs[16:]
    pooled(blocks, 0, pool, sems)
    for d in ORDER:
        h = (where[2] + d) & 7

        def some(i, carry):
            for j in range(16):
                k = i * 16 + j
                row = asked[h, k]
                at = pl.multiple_of((row & 63) * 2, 2)
                buf[d, k] = pool[row >> 6, pl.ds(at, 2)]
            return carry

        lax.fori_loop(0, 4, some, 0)
        pltpu.make_async_copy(buf.at[d], outs[d], out_sems.at[d]).start()
    for d in ORDER:
        pltpu.make_async_copy(buf.at[d], outs[d], out_sems.at[d]).wait()


def select_call(body, smem, blocks, shape, outs):
    return pl.pallas_call(
        body,
        out_shape=outs,
        in_specs=[pl.BlockSpec(memory_space=pltpu.SMEM)] * len(smem) + [pl.BlockSpec(memory_space=ANY)] * 8,
        out_specs=jax.tree.map(lambda _: pl.BlockSpec(memory_space=pltpu.HBM), outs),
        scratch_shapes=[
            pltpu.VMEM((8, 128, 8, 128), BF16),
            pltpu.VMEM(shape, BF16),
            pltpu.SemaphoreType.DMA((8,)),
            pltpu.SemaphoreType.DMA((8,)),
        ],
        compiler_params=pltpu.CompilerParams(vmem_limit_bytes=GRANT),
        cost_estimate=pl.CostEstimate(flops=0, bytes_accessed=4_000_000, transcendentals=0),
    )(*smem, *blocks)


def select_parents(asked, blocks):
    shape = (SIDE, 16, 8, 8, 128)
    return select_call(parents_body, (asked,), blocks, shape, pltpu.HBM(shape, BF16))


def select_children(where, asked, blocks):
    outs = tuple(pltpu.HBM((64, 2, 8, 128), BF16) for _ in range(SIDE))
    return select_call(children_body, (where, asked), blocks, (SIDE, 64, 2, 8, 128), outs)


def parent_far_body(code, recv, ops_hbm, out, ops, sem):
    copy = pltpu.make_async_copy(ops_hbm, ops.at[pl.ds(0, 40)], sem)
    copy.start()
    ops[40] = jnp.zeros(ops.shape[1:], BF16)
    copy.wait()

    def row(r, carry):
        real = [jnp.zeros((8, 128), F32) for _ in range(4)]
        imag = [jnp.zeros((8, 128), F32) for _ in range(4)]
        for j in range(8):
            both = code[j, r]
            at, op = both >> 6, both & 63
            for t in range(4):
                u, v = t // 2, t % 2
                a = ops[op, 0, u * 8 : u * 8 + 8, v * 128 : v * 128 + 128].astype(F32)
                b = ops[op, 1, u * 8 : u * 8 + 8, v * 128 : v * 128 + 128].astype(F32)
                c = recv[at, t].astype(F32)
                d = recv[at, 4 + t].astype(F32)
                real[t] = real[t] + (a * c - b * d)
                imag[t] = imag[t] + (a * d + b * c)
        for t in range(4):
            out[r, t] = real[t].astype(BF16)
            out[r, 4 + t] = imag[t].astype(BF16)
        return carry

    lax.fori_loop(0, 16, row, 0)


def far_parents(code, recv, ops):
    return pl.pallas_call(
        parent_far_body,
        out_shape=jax.ShapeDtypeStruct((16, 8, 8, 128), BF16),
        in_specs=[
            pl.BlockSpec(memory_space=pltpu.SMEM),
            pl.BlockSpec(memory_space=VM),
            pl.BlockSpec(memory_space=ANY),
        ],
        out_specs=pl.BlockSpec(memory_space=VM),
        scratch_shapes=[pltpu.VMEM((41, 2, 16, PP), BF16), pltpu.SemaphoreType.DMA],
        compiler_params=pltpu.CompilerParams(vmem_limit_bytes=GRANT),
        name="far_parents",
    )(code, recv, ops)


def child_far_body(code, *refs):
    blocks, ops_hbm, out, recv, ops, sems = refs[:8], *refs[8:]
    copies = fetch((ops_hbm, *blocks), (ops.at[pl.ds(0, 40)], *(recv.at[i] for i in range(8))), sems)
    ops[40] = jnp.zeros(ops.shape[1:], BF16)
    for copy in copies:
        copy.wait()

    def row(r, carry):
        real = jnp.zeros((8, 128), F32)
        imag = jnp.zeros((8, 128), F32)
        for j in range(8):
            both = code[j, r]
            lane, at, op = both >> 12, (both >> 6) & 63, both & 63
            a, b = ops[op, 0].astype(F32), ops[op, 1].astype(F32)
            c, d = recv[lane, at, 0].astype(F32), recv[lane, at, 1].astype(F32)
            real = real + (a * c - b * d)
            imag = imag + (a * d + b * c)
        out[r, 0] = real
        out[r, 1] = imag
        return carry

    lax.fori_loop(0, 64, row, 0, unroll=2)


def far_children(code, blocks, ops):
    return pl.pallas_call(
        child_far_body,
        out_shape=pltpu.HBM((64, 2, 8, 128), F32),
        in_specs=[pl.BlockSpec(memory_space=pltpu.SMEM)] + [pl.BlockSpec(memory_space=ANY)] * 9,
        out_specs=pl.BlockSpec(memory_space=VM),
        scratch_shapes=[
            pltpu.VMEM((SIDE, 64, 2, 8, 128), BF16),
            pltpu.VMEM((41, 2, 8, 128), BF16),
            pltpu.SemaphoreType.DMA((9,)),
        ],
        compiler_params=pltpu.CompilerParams(vmem_limit_bytes=GRANT),
        name="far_children",
    )(code, *blocks, ops)


def down_body(far, theta, phi_h, cos_t, sin_t, out, phi, turned, sem):
    copy = pltpu.make_async_copy(phi_h, phi, sem)
    copy.start()
    for s in range(8):
        at = pl.ds(s * 16, 16)
        for q in range(2):
            re, im = (
                jnp.concatenate(
                    [
                        jnp.concatenate([far[s, q, c * 4 + u * 2 + v].astype(F32) for v in range(2)], axis=1)
                        for u in range(2)
                    ],
                    axis=0,
                )
                for c in range(2)
            )
            for t, (k, m) in enumerate(((0, 3), (1, 2))):
                cs, sn = cos_t[t, at, :], sin_t[t, at, :]
                cr, si, ci, sr = cs * re, sn * im, cs * im, sn * re
                turned[(q * 4 + k) * 2, at, :] = (cr + si).astype(BF16)
                turned[(q * 4 + k) * 2 + 1, at, :] = (ci - sr).astype(BF16)
                turned[(q * 4 + m) * 2, at, :] = (cr - si).astype(BF16)
                turned[(q * 4 + m) * 2 + 1, at, :] = (ci + sr).astype(BF16)
    copy.wait()
    for r in range(8):
        for c in range(2):
            narrowed = bmm(turned[r * 2 + c], phi[...]).astype(BF16)
            term = bmm(theta[...], narrowed).astype(BF16)
            for s in range(8):
                out[s, r, c] = term[s * 8 : s * 8 + 8, :]


def lower(far, tables):
    return pl.pallas_call(
        down_body,
        out_shape=jax.ShapeDtypeStruct((8, 8, 2, 8, 128), BF16),
        in_specs=[pl.BlockSpec(memory_space=ANY if i == 2 else VM) for i in range(5)],
        out_specs=pl.BlockSpec(memory_space=VM),
        scratch_shapes=[
            pltpu.VMEM(tables[1].shape, BF16),
            pltpu.VMEM((16, PT, PP), BF16),
            pltpu.SemaphoreType.DMA,
        ],
        compiler_params=pltpu.CompilerParams(vmem_limit_bytes=GRANT),
        name="lower",
    )(far, *tables)


def groups(straight):
    found = []
    for angle in range(8):
        for o in range(SIDE):
            line = [(o, i) if (angle % 2) == straight else (i, o) for i in range(SIDE)]
            found.append([(y * SIDE + z) * 8 + angle for y, z in line])
    return found


SPREAD, TRADE = groups(1), groups(0)


def hop(x, step, lines=SPREAD):
    pairs = [(g[i], g[(i + step) % SIDE]) for g in lines for i in range(SIDE)]
    return lax.ppermute(x, BOTH, pairs)


def swap(x, axis, **kw):
    return lax.all_to_all(x, axis, split_axis=0, concat_axis=0, tiled=True, **kw)


def local(
    child_field,
    child_list,
    child_op,
    child_home,
    child_ops,
    parent_list,
    parent_op,
    parent_home,
    parent_ops,
):
    theta_up = jnp.asarray(fourier_table(PT, CT, 0.5)).astype(BF16)
    phi_up = jnp.asarray(np.ascontiguousarray(fourier_table(PP, SUBBOX_HEADINGS, 0.0).T)).astype(BF16)
    theta_down = jnp.asarray(np.ascontiguousarray(fourier_table(PT, CT, 0.5).T) * np.float32(CT / PT)).astype(BF16)
    phi_down = jnp.asarray(
        fourier_table(PP, SUBBOX_HEADINGS, 0.0) * np.float32(SUBBOX_HEADINGS / PP)
    ).astype(BF16)
    cos_np, sin_np = shift_tables()
    cos_t, sin_t = jnp.asarray(cos_np), jnp.asarray(sin_np)

    box, angle = lax.axis_index("box"), lax.axis_index("angle")
    core = angle % 2
    mine = jnp.where(core == 0, box // SIDE, box % SIDE)
    other = jnp.where(core == 0, box % SIDE, box // SIDE)
    where = jnp.stack([core, mine, other]).astype(I32)

    hold = lambda x: pltpu.with_memory_space_constraint(x, pltpu.HBM)
    whole = swap(child_field, "angle").reshape(8, 8, 2, 8, 128)
    parents = swap(lift(whole, tuple(map(hold, (theta_up, phi_up, cos_t, sin_t)))), "angle")
    wanted, child_code, parent_code = plan(
        where, child_list, child_op, child_home, parent_list, parent_op, parent_home
    )
    own = hold(jnp.concatenate([child_field.reshape(128, 8, 128), parents.reshape(128, 8, 128)]))
    forth, back = [own], [own]
    for step in range(4):
        if step == 1:
            forth[1], wanted = lax.optimization_barrier((forth[1], wanted))
        forth.append(hold(hop(forth[-1], 1)))
        if step < 3:
            back.append(hold(hop(back[-1], -1)))
    blocks = back + [forth[8 - p] for p in range(4, 8)]
    asked = swap(wanted.reshape(SIDE, 1, 128), BOTH, axis_index_groups=TRADE).reshape(SIDE, 128)
    parents_out = select_parents(asked, blocks)
    parents_in = swap(parents_out, BOTH, axis_index_groups=TRADE)
    children_out = select_children(where, hold(asked), blocks)
    children_in = {0: children_out[0]}
    for d in ORDER[:-1]:
        children_in[d] = hop(children_out[d], d, TRADE)
    sums = far_parents(hold(parent_code), parents_in.reshape(128, 8, 8, 128), parent_ops)
    turned = swap(sums, "angle").reshape(8, 2, 8, 8, 128)
    term = lower(turned, (theta_down, hold(phi_down), cos_t, sin_t))
    term = swap(term, "angle").reshape(64, 2, 8, 128)
    child_far = far_children(hold(child_code), [children_in[d] for d in range(SIDE)], child_ops)
    return (child_far + term.astype(F32)).astype(BF16)


def solution(mesh):
    return jax.shard_map(
        local,
        mesh=mesh,
        in_specs=(
            P("box", None, "angle", None),
            P("box", None),
            P("box", None),
            P(),
            P(None, None, "angle", None),
            P("box", None),
            P("box", None),
            P(),
            P(None, None, "angle", None),
        ),
        out_specs=P("box", None, "angle", None),
        check_vma=False,
    )
```

```python
import math

import jax
import jax.numpy as jnp
import numpy as np
from jax import lax
from jax.experimental import pallas as pl
from jax.experimental.pallas import tpu as pltpu
from jax.sharding import PartitionSpec as P


CT = 64
SUBBOX_HEADINGS = 128
PT = 128
PP = 256
WAVE_NUMBER = 6.0
SIDE = 8
BOTH = ("box", "angle")
F32, BF16, I32 = jnp.float32, jnp.bfloat16, jnp.int32
VM = pltpu.VMEM
ANY = pl.ANY
GRANT = 12 << 20


def fourier_table(fine_count, coarse_count, offset):
    f32 = np.float32
    fine = (np.arange(fine_count, dtype=f32) + f32(offset)) / f32(fine_count)
    coarse = (np.arange(coarse_count, dtype=f32) + f32(offset)) / f32(coarse_count)
    x = fine[:, None] - coarse[None, :]
    harmonic = np.arange(1, coarse_count // 2, dtype=f32)
    cosines = np.cos(f32(2.0 * math.pi) * harmonic * x[:, :, None])
    summed = f32(1.0) + f32(2.0) * cosines.sum(2, dtype=np.float64) + np.cos(f32(math.pi * coarse_count) * x)
    return (summed / coarse_count).astype(f32)


def shift_tables():
    f32 = np.float32
    polar = (f32(math.pi) * (np.arange(PT, dtype=f32) + f32(0.5)) / f32(PT)).astype(f32)
    heading = (f32(2.0 * math.pi / PP) * np.arange(PP, dtype=f32)).astype(f32)
    cos_h, sin_h = np.cos(heading), np.sin(heading)
    across = np.stack([-cos_h - sin_h, cos_h - sin_h])
    arg = (f32(WAVE_NUMBER) * np.sin(polar))[None, :, None] * across[:, None, :]
    return np.cos(arg).astype(f32), np.sin(arg).astype(f32)


def bmm(a, b):
    return lax.dot_general(a, b, (((1,), (0,)), ((), ())), preferred_element_type=F32)


def iota(shape, dim):
    return lax.broadcasted_iota(I32, shape, dim)


def plan_level(ids_ref, op_ref, home_ref, core, mine, other, rows_device, cap, empty_op, code_ref):
    slots, rows = ids_ref.shape
    home = home_ref[...]
    owner = home // rows_device
    table = jnp.concatenate([owner, home - owner * rows_device], axis=0).astype(F32).astype(BF16)
    highs = home.shape[0]
    before = (iota((rows, rows), 0) < iota((rows, rows), 1)).astype(F32).astype(BF16)
    carry = jnp.zeros((SIDE, 1), F32)
    wanted = jnp.zeros((2 * SIDE, cap), F32)
    for j in range(slots):
        ids = ids_ref[pl.ds(j, 1), :]
        usable = ids >= 0
        safe = jnp.maximum(ids, 0)
        high, low = safe >> 7, safe & 127
        low_hot = (iota((128, rows), 0) == low).astype(F32).astype(BF16)
        picked = bmm(table, low_hot)
        high_hot = (iota((highs, rows), 0) == high).astype(F32)
        own = jnp.sum(picked[:highs] * high_hot, axis=0, keepdims=True).astype(I32)
        loc = jnp.sum(picked[highs:] * high_hot, axis=0, keepdims=True)
        along_y, along_z = own >> 3, own & 7
        column = jnp.where(core == 0, along_z, along_y)
        place = (jnp.where(core == 0, along_y, along_z) - mine) & 7
        hot = jnp.where((iota((SIDE, rows), 0) == column) & usable, 1.0, 0.0)
        hot_b = hot.astype(BF16)
        prefix = bmm(hot_b, before) + carry
        carry = carry + jnp.sum(hot, axis=1, keepdims=True)
        rank = jnp.sum(hot * prefix, axis=0, keepdims=True).astype(I32)
        lane = column if other is None else (other - column) & 7
        position = lane * cap + rank
        code_ref[pl.ds(j, 1), pl.ds(0, rows)] = jnp.where(
            usable, position * 64 + op_ref[pl.ds(j, 1), :], empty_op
        )
        rank_hot = (iota((cap, rows), 0) == rank).astype(F32).astype(BF16)
        both = jnp.concatenate([hot * place.astype(F32), hot * loc], axis=0).astype(BF16)
        wanted = wanted + lax.dot_general(
            both, rank_hot, (((1,), (1,)), ((), ())), preferred_element_type=F32
        )
    return (wanted[:SIDE] * rows_device + wanted[SIDE:]).astype(I32)


def plan_body(where, cl, co, ch, plist, po, ph, want_ref, ccode_ref, pcode_ref):
    core, mine, other = where[0], where[1], where[2]
    want_ref[...] = jnp.zeros(want_ref.shape, I32)
    want_ref[:, pl.ds(0, 64)] = plan_level(cl, co, ch, core, mine, other, 64, 64, 40, ccode_ref)
    want_ref[:, pl.ds(64, 16)] = plan_level(plist, po, ph, core, mine, None, 16, 16, 40, pcode_ref)


def plan(where, child_list, child_op, child_home, parent_list, parent_op, parent_home):
    args = (
        where,
        child_list.T,
        child_op.T,
        child_home.reshape(-1, 128),
        parent_list.T,
        parent_op.T,
        parent_home.reshape(-1, 128),
    )
    return pl.pallas_call(
        plan_body,
        out_shape=(
            jax.ShapeDtypeStruct((SIDE, 128), I32),
            pltpu.HBM((8, 64), I32),
            pltpu.HBM((8, 16), I32),
        ),
        in_specs=[pl.BlockSpec(memory_space=pltpu.SMEM)] + [pl.BlockSpec(memory_space=VM)] * 6,
        out_specs=(pl.BlockSpec(memory_space=VM),) * 3,
        compiler_params=pltpu.CompilerParams(vmem_limit_bytes=GRANT),
        name="plan",
    )(*args)


def up_body(field, theta_h, phi_h, cos_h, sin_h, out, theta, phi, cos_t, sin_t, wide, sems):
    copies = fetch((theta_h, phi_h, cos_h, sin_h), (theta, phi, cos_t, sin_t), sems)
    copies[0].wait()
    copies[1].wait()
    for r in range(8):
        for c in range(2):
            rows = jnp.concatenate([field[s, r, c] for s in range(8)], axis=0)
            stretched = bmm(theta[...], rows).astype(BF16)
            wide[r * 2 + c] = bmm(stretched, phi[...])
    copies[2].wait()
    copies[3].wait()
    for q in range(2):
        for u in range(PT // 8):
            at = pl.ds(u * 8, 8)
            w = [[wide[(q * 4 + k) * 2 + c, at, :] for c in range(2)] for k in range(4)]
            real = jnp.zeros((8, PP), F32)
            imag = jnp.zeros((8, PP), F32)
            for t, (k, m) in enumerate(((0, 3), (1, 2))):
                cs, sn = cos_t[t, at, :], sin_t[t, at, :]
                real = real + cs * (w[k][0] + w[m][0]) - sn * (w[k][1] - w[m][1])
                imag = imag + cs * (w[k][1] + w[m][1]) + sn * (w[k][0] - w[m][0])
            for c, part in enumerate((real, imag)):
                part = part.astype(BF16)
                for v in range(2):
                    out[u // 2, q, c * 4 + (u % 2) * 2 + v] = part[:, v * 128 : (v + 1) * 128]


def fetch(sources, targets, sems):
    copies = [pltpu.make_async_copy(a, b, sems.at[i]) for i, (a, b) in enumerate(zip(sources, targets))]
    for copy in copies:
        copy.start()
    return copies


def lift(field, tables):
    return pl.pallas_call(
        up_body,
        out_shape=jax.ShapeDtypeStruct((8, 2, 8, 8, 128), BF16),
        in_specs=[pl.BlockSpec(memory_space=VM)] + [pl.BlockSpec(memory_space=pltpu.HBM)] * 4,
        out_specs=pl.BlockSpec(memory_space=VM),
        scratch_shapes=[pltpu.VMEM(t.shape, t.dtype) for t in tables]
        + [pltpu.VMEM((16, PT, PP), F32), pltpu.SemaphoreType.DMA((4,))],
        compiler_params=pltpu.CompilerParams(vmem_limit_bytes=GRANT),
        name="lift",
    )(field, *tables)


def select_body(where, asked, *refs):
    blocks, parents, children = refs[:8], refs[8], refs[9:17]
    pool, parent_buf, child_buf, sems, parent_sems, child_sems = refs[17:]
    copies = [
        pltpu.make_async_copy(
            b.at[pl.ds(128 * half, 128)], pool.at[half, i], sems.at[half, i]
        )
        for half in (1, 0)
        for i, b in enumerate(blocks)
    ]
    for copy in copies:
        copy.start()

    def child_out(d):
        return pltpu.make_async_copy(child_buf.at[d], children[d], child_sems.at[d])

    def parent_out(h):
        return pltpu.make_async_copy(parent_buf.at[h], parents.at[h], parent_sems.at[h])

    for copy in copies[:8]:
        copy.wait()

    def peer(h, carry):
        for k in range(16):
            row = asked[h, 64 + k]
            at = pl.multiple_of((row & 15) * 8, 8)
            parent_buf[h, k] = pool[1, row >> 4, pl.ds(at, 8)]
        parent_out(h).start()
        return carry

    lax.fori_loop(0, SIDE, peer, 0)
    for copy in copies[8:]:
        copy.wait()
    for d in range(SIDE):
        h = (where[2] + d) & 7

        def some(i, carry):
            for j in range(16):
                k = i * 16 + j
                row = asked[h, k]
                at = pl.multiple_of((row & 63) * 2, 2)
                child_buf[d, k] = pool[0, row >> 6, pl.ds(at, 2)]
            return carry

        lax.fori_loop(0, 4, some, 0)
        child_out(d).start()
    for h in range(SIDE):
        parent_out(h).wait()
    for d in range(SIDE):
        child_out(d).wait()


def select(where, asked, blocks):
    hbm = pl.BlockSpec(memory_space=pltpu.HBM)
    return pl.pallas_call(
        select_body,
        out_shape=(pltpu.HBM((SIDE, 16, 8, 8, 128), BF16),) + (pltpu.HBM((64, 2, 8, 128), BF16),) * SIDE,
        in_specs=[pl.BlockSpec(memory_space=pltpu.SMEM)] * 2 + [pl.BlockSpec(memory_space=ANY)] * 8,
        out_specs=(hbm,) * 9,
        scratch_shapes=[
            pltpu.VMEM((2, 8, 128, 8, 128), BF16),
            pltpu.VMEM((SIDE, 16, 8, 8, 128), BF16),
            pltpu.VMEM((SIDE, 64, 2, 8, 128), BF16),
            pltpu.SemaphoreType.DMA((2, 8)),
            pltpu.SemaphoreType.DMA((8,)),
            pltpu.SemaphoreType.DMA((8,)),
        ],
        compiler_params=pltpu.CompilerParams(vmem_limit_bytes=GRANT),
        name="select",
    )(where, asked, *blocks)


def parent_far_body(code, recv, ops_hbm, out, ops, sem):
    copy = pltpu.make_async_copy(ops_hbm, ops.at[pl.ds(0, 40)], sem)
    copy.start()
    ops[40] = jnp.zeros(ops.shape[1:], BF16)
    copy.wait()

    def row(r, carry):
        real = [jnp.zeros((8, 128), F32) for _ in range(4)]
        imag = [jnp.zeros((8, 128), F32) for _ in range(4)]
        for j in range(8):
            both = code[j, r]
            at, op = both >> 6, both & 63
            for t in range(4):
                u, v = t // 2, t % 2
                a = ops[op, 0, u * 8 : u * 8 + 8, v * 128 : v * 128 + 128].astype(F32)
                b = ops[op, 1, u * 8 : u * 8 + 8, v * 128 : v * 128 + 128].astype(F32)
                c = recv[at, t].astype(F32)
                d = recv[at, 4 + t].astype(F32)
                real[t] = real[t] + (a * c - b * d)
                imag[t] = imag[t] + (a * d + b * c)
        for t in range(4):
            out[r, t] = real[t].astype(BF16)
            out[r, 4 + t] = imag[t].astype(BF16)
        return carry

    lax.fori_loop(0, 16, row, 0)


def far_parents(code, recv, ops):
    return pl.pallas_call(
        parent_far_body,
        out_shape=jax.ShapeDtypeStruct((16, 8, 8, 128), BF16),
        in_specs=[
            pl.BlockSpec(memory_space=pltpu.SMEM),
            pl.BlockSpec(memory_space=VM),
            pl.BlockSpec(memory_space=ANY),
        ],
        out_specs=pl.BlockSpec(memory_space=VM),
        scratch_shapes=[pltpu.VMEM((41, 2, 16, PP), BF16), pltpu.SemaphoreType.DMA],
        compiler_params=pltpu.CompilerParams(vmem_limit_bytes=GRANT),
        name="far_parents",
    )(code, recv, ops)


def child_far_body(code, *refs):
    blocks, ops_hbm, out, recv, ops, sems = refs[:8], *refs[8:]
    copies = fetch((ops_hbm, *blocks), (ops.at[pl.ds(0, 40)], *(recv.at[i] for i in range(8))), sems)
    ops[40] = jnp.zeros(ops.shape[1:], BF16)
    for copy in copies:
        copy.wait()

    def row(r, carry):
        real = jnp.zeros((8, 128), F32)
        imag = jnp.zeros((8, 128), F32)
        for j in range(8):
            both = code[j, r]
            lane, at, op = both >> 12, (both >> 6) & 63, both & 63
            a, b = ops[op, 0].astype(F32), ops[op, 1].astype(F32)
            c, d = recv[lane, at, 0].astype(F32), recv[lane, at, 1].astype(F32)
            real = real + (a * c - b * d)
            imag = imag + (a * d + b * c)
        out[r, 0] = real
        out[r, 1] = imag
        return carry

    lax.fori_loop(0, 64, row, 0, unroll=2)


def far_children(code, blocks, ops):
    return pl.pallas_call(
        child_far_body,
        out_shape=pltpu.HBM((64, 2, 8, 128), F32),
        in_specs=[pl.BlockSpec(memory_space=pltpu.SMEM)] + [pl.BlockSpec(memory_space=ANY)] * 9,
        out_specs=pl.BlockSpec(memory_space=VM),
        scratch_shapes=[
            pltpu.VMEM((SIDE, 64, 2, 8, 128), BF16),
            pltpu.VMEM((41, 2, 8, 128), BF16),
            pltpu.SemaphoreType.DMA((9,)),
        ],
        compiler_params=pltpu.CompilerParams(vmem_limit_bytes=GRANT),
        name="far_children",
    )(code, *blocks, ops)


def down_body(far, theta, phi_h, cos_t, sin_t, out, phi, turned, sem):
    copy = pltpu.make_async_copy(phi_h, phi, sem)
    copy.start()
    for q in range(2):
        for u in range(PT // 8):
            at = pl.ds(u * 8, 8)
            re, im = (
                jnp.concatenate(
                    [far[u // 2, q, c * 4 + (u % 2) * 2 + v].astype(F32) for v in range(2)], axis=1
                )
                for c in range(2)
            )
            for t, (k, m) in enumerate(((0, 3), (1, 2))):
                cs, sn = cos_t[t, at, :], sin_t[t, at, :]
                cr, si, ci, sr = cs * re, sn * im, cs * im, sn * re
                turned[(q * 4 + k) * 2, at, :] = (cr + si).astype(BF16)
                turned[(q * 4 + k) * 2 + 1, at, :] = (ci - sr).astype(BF16)
                turned[(q * 4 + m) * 2, at, :] = (cr - si).astype(BF16)
                turned[(q * 4 + m) * 2 + 1, at, :] = (ci + sr).astype(BF16)
    copy.wait()
    for r in range(8):
        for c in range(2):
            narrowed = bmm(turned[r * 2 + c], phi[...]).astype(BF16)
            term = bmm(theta[...], narrowed).astype(BF16)
            for s in range(8):
                out[s, r, c] = term[s * 8 : s * 8 + 8, :]


def lower(far, tables):
    return pl.pallas_call(
        down_body,
        out_shape=jax.ShapeDtypeStruct((8, 8, 2, 8, 128), BF16),
        in_specs=[pl.BlockSpec(memory_space=ANY if i == 2 else VM) for i in range(5)],
        out_specs=pl.BlockSpec(memory_space=VM),
        scratch_shapes=[
            pltpu.VMEM(tables[1].shape, BF16),
            pltpu.VMEM((16, PT, PP), BF16),
            pltpu.SemaphoreType.DMA,
        ],
        compiler_params=pltpu.CompilerParams(vmem_limit_bytes=GRANT),
        name="lower",
    )(far, *tables)


def groups(straight):
    found = []
    for angle in range(8):
        for o in range(SIDE):
            line = [(o, i) if (angle % 2) == straight else (i, o) for i in range(SIDE)]
            found.append([(y * SIDE + z) * 8 + angle for y, z in line])
    return found


SPREAD, TRADE = groups(1), groups(0)


def hop(x, step, lines=SPREAD):
    pairs = [(g[i], g[(i + step) % SIDE]) for g in lines for i in range(SIDE)]
    return lax.ppermute(x, BOTH, pairs)


def swap(x, axis, **kw):
    return lax.all_to_all(x, axis, split_axis=0, concat_axis=0, tiled=True, **kw)


def local(
    child_field,
    child_list,
    child_op,
    child_home,
    child_ops,
    parent_list,
    parent_op,
    parent_home,
    parent_ops,
):
    theta_up = jnp.asarray(fourier_table(PT, CT, 0.5)).astype(BF16)
    phi_up = jnp.asarray(np.ascontiguousarray(fourier_table(PP, SUBBOX_HEADINGS, 0.0).T)).astype(BF16)
    theta_down = jnp.asarray(np.ascontiguousarray(fourier_table(PT, CT, 0.5).T) * np.float32(CT / PT)).astype(BF16)
    phi_down = jnp.asarray(
        fourier_table(PP, SUBBOX_HEADINGS, 0.0) * np.float32(SUBBOX_HEADINGS / PP)
    ).astype(BF16)
    cos_np, sin_np = shift_tables()
    cos_t, sin_t = jnp.asarray(cos_np), jnp.asarray(sin_np)

    box, angle = lax.axis_index("box"), lax.axis_index("angle")
    core = angle % 2
    mine = jnp.where(core == 0, box // SIDE, box % SIDE)
    other = jnp.where(core == 0, box % SIDE, box // SIDE)
    where = jnp.stack([core, mine, other]).astype(I32)

    hold = lambda x: pltpu.with_memory_space_constraint(x, pltpu.HBM)
    whole = swap(child_field, "angle").reshape(8, 8, 2, 8, 128)
    parents = swap(lift(whole, tuple(map(hold, (theta_up, phi_up, cos_t, sin_t)))), "angle")
    wanted, child_code, parent_code = plan(
        where, child_list, child_op, child_home, parent_list, parent_op, parent_home
    )
    own = jnp.concatenate([child_field.reshape(128, 8, 128), parents.reshape(128, 8, 128)])
    up2, down2 = hop(own, 2), hop(own, -2)
    up1, down1 = hop(own, 1), hop(own, -1)
    up2, wanted = lax.optimization_barrier((up2, wanted))
    up4 = hop(up2, 2)
    up3, down3 = hop(up2, 1), hop(down2, -1)
    blocks = [own, down1, down2, down3, up4, up3, up2, up1]
    asked = swap(wanted.reshape(SIDE, 1, 128), BOTH, axis_index_groups=TRADE).reshape(SIDE, 128)
    parents_out, *children_out = select(where, asked, blocks)
    parents_in = swap(parents_out, BOTH, axis_index_groups=TRADE)
    children_in = {0: children_out[0]}
    for d in (4, 3, 5, 2, 6, 1, 7):
        children_in[d] = hop(children_out[d], d, TRADE)
    sums = far_parents(hold(parent_code), parents_in.reshape(128, 8, 8, 128), parent_ops)
    turned = swap(sums, "angle").reshape(8, 2, 8, 8, 128)
    term = lower(turned, (theta_down, hold(phi_down), cos_t, sin_t))
    term = swap(term, "angle").reshape(64, 2, 8, 128)
    child_far = far_children(hold(child_code), [children_in[d] for d in range(SIDE)], child_ops)
    return (child_far + term.astype(F32)).astype(BF16)


def solution(mesh):
    return jax.shard_map(
        local,
        mesh=mesh,
        in_specs=(
            P("box", None, "angle", None),
            P("box", None),
            P("box", None),
            P(),
            P(None, None, "angle", None),
            P("box", None),
            P("box", None),
            P(),
            P(None, None, "angle", None),
        ),
        out_specs=P("box", None, "angle", None),
        check_vma=False,
    )
```

```python
import math

import jax
import jax.numpy as jnp
import numpy as np
from jax import lax
from jax.experimental import pallas as pl
from jax.experimental.pallas import tpu as pltpu
from jax.sharding import PartitionSpec as P


CT = 64
SUBBOX_HEADINGS = 128
PT = 128
PP = 256
WAVE_NUMBER = 6.0
SIDE = 8
BOTH = ("box", "angle")
F32, BF16, I32 = jnp.float32, jnp.bfloat16, jnp.int32
VM = pltpu.VMEM
ANY = pl.ANY
GRANT = 12 << 20


def fourier_table(fine_count, coarse_count, offset):
    f32 = np.float32
    fine = (np.arange(fine_count, dtype=f32) + f32(offset)) / f32(fine_count)
    coarse = (np.arange(coarse_count, dtype=f32) + f32(offset)) / f32(coarse_count)
    x = fine[:, None] - coarse[None, :]
    harmonic = np.arange(1, coarse_count // 2, dtype=f32)
    cosines = np.cos(f32(2.0 * math.pi) * harmonic * x[:, :, None])
    summed = f32(1.0) + f32(2.0) * cosines.sum(2, dtype=np.float64) + np.cos(f32(math.pi * coarse_count) * x)
    return (summed / coarse_count).astype(f32)


def shift_tables():
    f32 = np.float32
    polar = (f32(math.pi) * (np.arange(PT, dtype=f32) + f32(0.5)) / f32(PT)).astype(f32)
    heading = (f32(2.0 * math.pi / PP) * np.arange(PP, dtype=f32)).astype(f32)
    cos_h, sin_h = np.cos(heading), np.sin(heading)
    across = np.stack([-cos_h - sin_h, cos_h - sin_h])
    arg = (f32(WAVE_NUMBER) * np.sin(polar))[None, :, None] * across[:, None, :]
    return np.cos(arg).astype(f32), np.sin(arg).astype(f32)


def hold(x):
    return pltpu.with_memory_space_constraint(x, pltpu.HBM)


def bmm(a, b):
    return lax.dot_general(a, b, (((1,), (0,)), ((), ())), preferred_element_type=F32)


def iota(shape, dim):
    return lax.broadcasted_iota(I32, shape, dim)


def plan_level(ids_ref, op_ref, home_ref, core, mine, other, rows_device, cap, empty_op, code_ref):
    slots, rows = ids_ref.shape
    home = home_ref[...]
    owner = home // rows_device
    table = jnp.concatenate([owner, home - owner * rows_device], axis=0).astype(F32).astype(BF16)
    highs = home.shape[0]
    before = (iota((rows, rows), 0) < iota((rows, rows), 1)).astype(F32).astype(BF16)
    carry = jnp.zeros((SIDE, 1), F32)
    wanted = jnp.zeros((2 * SIDE, cap), F32)
    for j in range(slots):
        ids = ids_ref[pl.ds(j, 1), :]
        usable = ids >= 0
        safe = jnp.maximum(ids, 0)
        high, low = safe >> 7, safe & 127
        low_hot = (iota((128, rows), 0) == low).astype(F32).astype(BF16)
        picked = bmm(table, low_hot)
        high_hot = (iota((highs, rows), 0) == high).astype(F32)
        own = jnp.sum(picked[:highs] * high_hot, axis=0, keepdims=True).astype(I32)
        loc = jnp.sum(picked[highs:] * high_hot, axis=0, keepdims=True)
        along_y, along_z = own >> 3, own & 7
        column = jnp.where(core == 0, along_z, along_y)
        place = (jnp.where(core == 0, along_y, along_z) - mine) & 7
        hot = jnp.where((iota((SIDE, rows), 0) == column) & usable, 1.0, 0.0)
        hot_b = hot.astype(BF16)
        prefix = bmm(hot_b, before) + carry
        carry = carry + jnp.sum(hot, axis=1, keepdims=True)
        rank = jnp.sum(hot * prefix, axis=0, keepdims=True).astype(I32)
        lane = column if other is None else (other - column) & 7
        position = lane * cap + rank
        code_ref[pl.ds(j, 1), pl.ds(0, rows)] = jnp.where(
            usable, position * 64 + op_ref[pl.ds(j, 1), :], empty_op
        )
        rank_hot = (iota((cap, rows), 0) == rank).astype(F32).astype(BF16)
        both = jnp.concatenate([hot * place.astype(F32), hot * loc], axis=0).astype(BF16)
        wanted = wanted + lax.dot_general(
            both, rank_hot, (((1,), (1,)), ((), ())), preferred_element_type=F32
        )
    return (wanted[:SIDE] * rows_device + wanted[SIDE:]).astype(I32)


def plan_body(where, cl, co, ch, plist, po, ph, want_ref, ccode_ref, pcode_ref):
    core, mine, other = where[0], where[1], where[2]
    want_ref[...] = jnp.zeros(want_ref.shape, I32)
    want_ref[:, pl.ds(0, 64)] = plan_level(cl, co, ch, core, mine, other, 64, 64, 40, ccode_ref)
    want_ref[:, pl.ds(64, 16)] = plan_level(plist, po, ph, core, mine, None, 16, 16, 40, pcode_ref)


def plan(where, child_list, child_op, child_home, parent_list, parent_op, parent_home):
    args = (
        where,
        *map(
            hold,
            (
                child_list.T,
                child_op.T,
                child_home.reshape(-1, 128),
                parent_list.T,
                parent_op.T,
                parent_home.reshape(-1, 128),
            ),
        ),
    )
    return pl.pallas_call(
        plan_body,
        out_shape=(
            jax.ShapeDtypeStruct((SIDE, 128), I32),
            pltpu.HBM((8, 64), I32),
            pltpu.HBM((8, 16), I32),
        ),
        in_specs=[pl.BlockSpec(memory_space=pltpu.SMEM)] + [pl.BlockSpec(memory_space=VM)] * 6,
        out_specs=(pl.BlockSpec(memory_space=VM),) * 3,
        compiler_params=pltpu.CompilerParams(vmem_limit_bytes=GRANT),
        name="plan",
    )(*args)


def up_body(field, theta_h, phi_h, cos_h, sin_h, out, theta, phi, cos_t, sin_t, wide, sems):
    copies = fetch((theta_h, phi_h, cos_h, sin_h), (theta, phi, cos_t, sin_t), sems)
    copies[0].wait()
    copies[1].wait()
    for r in range(8):
        for c in range(2):
            rows = jnp.concatenate([field[s, r, c] for s in range(8)], axis=0)
            stretched = bmm(theta[...], rows).astype(BF16)
            wide[r * 2 + c] = bmm(stretched, phi[...])
    copies[2].wait()
    copies[3].wait()
    for q in range(2):
        for u in range(PT // 8):
            at = pl.ds(u * 8, 8)
            w = [[wide[(q * 4 + k) * 2 + c, at, :] for c in range(2)] for k in range(4)]
            real = jnp.zeros((8, PP), F32)
            imag = jnp.zeros((8, PP), F32)
            for t, (k, m) in enumerate(((0, 3), (1, 2))):
                cs, sn = cos_t[t, at, :], sin_t[t, at, :]
                real = real + cs * (w[k][0] + w[m][0]) - sn * (w[k][1] - w[m][1])
                imag = imag + cs * (w[k][1] + w[m][1]) + sn * (w[k][0] - w[m][0])
            for c, part in enumerate((real, imag)):
                part = part.astype(BF16)
                for v in range(2):
                    out[u // 2, q, c * 4 + (u % 2) * 2 + v] = part[:, v * 128 : (v + 1) * 128]


def fetch(sources, targets, sems):
    copies = [pltpu.make_async_copy(a, b, sems.at[i]) for i, (a, b) in enumerate(zip(sources, targets))]
    for copy in copies:
        copy.start()
    return copies


def lift(field, tables):
    return pl.pallas_call(
        up_body,
        out_shape=jax.ShapeDtypeStruct((8, 2, 8, 8, 128), BF16),
        in_specs=[pl.BlockSpec(memory_space=VM)] + [pl.BlockSpec(memory_space=pltpu.HBM)] * 4,
        out_specs=pl.BlockSpec(memory_space=VM),
        scratch_shapes=[pltpu.VMEM(t.shape, t.dtype) for t in tables]
        + [pltpu.VMEM((16, PT, PP), F32), pltpu.SemaphoreType.DMA((4,))],
        compiler_params=pltpu.CompilerParams(vmem_limit_bytes=GRANT),
        name="lift",
    )(field, *tables)


def select_body(where, asked, *refs):
    blocks, parents, children = refs[:8], refs[8], refs[9:17]
    pool, parent_buf, child_buf, sems, parent_sems, child_sems = refs[17:]
    copies = [
        pltpu.make_async_copy(
            b.at[pl.ds(128 * half, 128)], pool.at[half, i], sems.at[half, i]
        )
        for half in (1, 0)
        for i, b in enumerate(blocks)
    ]
    for copy in copies:
        copy.start()

    def child_out(d):
        return pltpu.make_async_copy(child_buf.at[d], children[d], child_sems.at[d])

    def parent_out(h):
        return pltpu.make_async_copy(parent_buf.at[h], parents.at[h], parent_sems.at[h])

    for copy in copies[:8]:
        copy.wait()

    def peer(h, carry):
        for k in range(16):
            row = asked[h, 64 + k]
            at = pl.multiple_of((row & 15) * 8, 8)
            parent_buf[h, k] = pool[1, row >> 4, pl.ds(at, 8)]
        parent_out(h).start()
        return carry

    lax.fori_loop(0, SIDE, peer, 0)
    for copy in copies[8:]:
        copy.wait()
    for d in range(SIDE):
        h = (where[2] + d) & 7

        def some(i, carry):
            for j in range(16):
                k = i * 16 + j
                row = asked[h, k]
                at = pl.multiple_of((row & 63) * 2, 2)
                child_buf[d, k] = pool[0, row >> 6, pl.ds(at, 2)]
            return carry

        lax.fori_loop(0, 4, some, 0)
        child_out(d).start()
    for h in range(SIDE):
        parent_out(h).wait()
    for d in range(SIDE):
        child_out(d).wait()


def select(where, asked, blocks):
    hbm = pl.BlockSpec(memory_space=pltpu.HBM)
    return pl.pallas_call(
        select_body,
        out_shape=(pltpu.HBM((SIDE, 16, 8, 8, 128), BF16),) + (pltpu.HBM((64, 2, 8, 128), BF16),) * SIDE,
        in_specs=[pl.BlockSpec(memory_space=pltpu.SMEM)] * 2 + [pl.BlockSpec(memory_space=ANY)] * 8,
        out_specs=(hbm,) * 9,
        scratch_shapes=[
            pltpu.VMEM((2, 8, 128, 8, 128), BF16),
            pltpu.VMEM((SIDE, 16, 8, 8, 128), BF16),
            pltpu.VMEM((SIDE, 64, 2, 8, 128), BF16),
            pltpu.SemaphoreType.DMA((2, 8)),
            pltpu.SemaphoreType.DMA((8,)),
            pltpu.SemaphoreType.DMA((8,)),
        ],
        compiler_params=pltpu.CompilerParams(vmem_limit_bytes=GRANT),
        name="select",
    )(where, asked, *blocks)


def parent_far_body(code, recv, ops_hbm, out, ops, sem):
    copy = pltpu.make_async_copy(ops_hbm, ops.at[pl.ds(0, 40)], sem)
    copy.start()
    ops[40] = jnp.zeros(ops.shape[1:], BF16)
    copy.wait()

    def row(r, carry):
        real = [jnp.zeros((8, 128), F32) for _ in range(4)]
        imag = [jnp.zeros((8, 128), F32) for _ in range(4)]
        for j in range(8):
            both = code[j, r]
            at, op = both >> 6, both & 63
            for t in range(4):
                u, v = t // 2, t % 2
                a = ops[op, 0, u * 8 : u * 8 + 8, v * 128 : v * 128 + 128].astype(F32)
                b = ops[op, 1, u * 8 : u * 8 + 8, v * 128 : v * 128 + 128].astype(F32)
                c = recv[at, t].astype(F32)
                d = recv[at, 4 + t].astype(F32)
                real[t] = real[t] + (a * c - b * d)
                imag[t] = imag[t] + (a * d + b * c)
        for t in range(4):
            out[r, t] = real[t].astype(BF16)
            out[r, 4 + t] = imag[t].astype(BF16)
        return carry

    lax.fori_loop(0, 16, row, 0)


def far_parents(code, recv, ops):
    return pl.pallas_call(
        parent_far_body,
        out_shape=jax.ShapeDtypeStruct((16, 8, 8, 128), BF16),
        in_specs=[
            pl.BlockSpec(memory_space=pltpu.SMEM),
            pl.BlockSpec(memory_space=VM),
            pl.BlockSpec(memory_space=ANY),
        ],
        out_specs=pl.BlockSpec(memory_space=VM),
        scratch_shapes=[pltpu.VMEM((41, 2, 16, PP), BF16), pltpu.SemaphoreType.DMA],
        compiler_params=pltpu.CompilerParams(vmem_limit_bytes=GRANT),
        name="far_parents",
    )(code, recv, ops)


def child_far_body(code, *refs):
    blocks, ops_hbm, out, recv, ops, sems = refs[:8], *refs[8:]
    copies = fetch((ops_hbm, *blocks), (ops.at[pl.ds(0, 40)], *(recv.at[i] for i in range(8))), sems)
    ops[40] = jnp.zeros(ops.shape[1:], BF16)
    for copy in copies:
        copy.wait()

    def row(r, carry):
        real = jnp.zeros((8, 128), F32)
        imag = jnp.zeros((8, 128), F32)
        for j in range(8):
            both = code[j, r]
            lane, at, op = both >> 12, (both >> 6) & 63, both & 63
            a, b = ops[op, 0].astype(F32), ops[op, 1].astype(F32)
            c, d = recv[lane, at, 0].astype(F32), recv[lane, at, 1].astype(F32)
            real = real + (a * c - b * d)
            imag = imag + (a * d + b * c)
        out[r, 0] = real
        out[r, 1] = imag
        return carry

    lax.fori_loop(0, 64, row, 0, unroll=2)


def far_children(code, blocks, ops):
    return pl.pallas_call(
        child_far_body,
        out_shape=jax.ShapeDtypeStruct((64, 2, 8, 128), F32),
        in_specs=[pl.BlockSpec(memory_space=pltpu.SMEM)] + [pl.BlockSpec(memory_space=ANY)] * 9,
        out_specs=pl.BlockSpec(memory_space=VM),
        scratch_shapes=[
            pltpu.VMEM((SIDE, 64, 2, 8, 128), BF16),
            pltpu.VMEM((41, 2, 8, 128), BF16),
            pltpu.SemaphoreType.DMA((9,)),
        ],
        compiler_params=pltpu.CompilerParams(vmem_limit_bytes=GRANT),
        name="far_children",
    )(code, *blocks, ops)


def down_body(far, theta, phi_h, cos_t, sin_t, out, phi, turned, sem):
    copy = pltpu.make_async_copy(phi_h, phi, sem)
    copy.start()
    for q in range(2):
        for u in range(PT // 8):
            at = pl.ds(u * 8, 8)
            re, im = (
                jnp.concatenate(
                    [far[u // 2, q, c * 4 + (u % 2) * 2 + v].astype(F32) for v in range(2)], axis=1
                )
                for c in range(2)
            )
            for t, (k, m) in enumerate(((0, 3), (1, 2))):
                cs, sn = cos_t[t, at, :], sin_t[t, at, :]
                cr, si, ci, sr = cs * re, sn * im, cs * im, sn * re
                turned[(q * 4 + k) * 2, at, :] = (cr + si).astype(BF16)
                turned[(q * 4 + k) * 2 + 1, at, :] = (ci - sr).astype(BF16)
                turned[(q * 4 + m) * 2, at, :] = (cr - si).astype(BF16)
                turned[(q * 4 + m) * 2 + 1, at, :] = (ci + sr).astype(BF16)
    copy.wait()
    for r in range(8):
        for c in range(2):
            narrowed = bmm(turned[r * 2 + c], phi[...]).astype(BF16)
            term = bmm(theta[...], narrowed).astype(BF16)
            for s in range(8):
                out[s, r, c] = term[s * 8 : s * 8 + 8, :]


def lower(far, tables):
    return pl.pallas_call(
        down_body,
        out_shape=jax.ShapeDtypeStruct((8, 8, 2, 8, 128), BF16),
        in_specs=[pl.BlockSpec(memory_space=ANY if i == 2 else VM) for i in range(5)],
        out_specs=pl.BlockSpec(memory_space=VM),
        scratch_shapes=[
            pltpu.VMEM(tables[1].shape, BF16),
            pltpu.VMEM((16, PT, PP), BF16),
            pltpu.SemaphoreType.DMA,
        ],
        compiler_params=pltpu.CompilerParams(vmem_limit_bytes=GRANT),
        name="lower",
    )(far, *tables)


def groups(straight):
    found = []
    for angle in range(8):
        for o in range(SIDE):
            line = [(o, i) if (angle % 2) == straight else (i, o) for i in range(SIDE)]
            found.append([(y * SIDE + z) * 8 + angle for y, z in line])
    return found


SPREAD, TRADE = groups(1), groups(0)


def hop(x, step, lines=SPREAD):
    pairs = [(g[i], g[(i + step) % SIDE]) for g in lines for i in range(SIDE)]
    return lax.ppermute(x, BOTH, pairs)


def swap(x, axis, **kw):
    return lax.all_to_all(x, axis, split_axis=0, concat_axis=0, tiled=True, **kw)


def local(
    child_field,
    child_list,
    child_op,
    child_home,
    child_ops,
    parent_list,
    parent_op,
    parent_home,
    parent_ops,
):
    theta_up = jnp.asarray(fourier_table(PT, CT, 0.5)).astype(BF16)
    phi_up = jnp.asarray(np.ascontiguousarray(fourier_table(PP, SUBBOX_HEADINGS, 0.0).T)).astype(BF16)
    theta_down = jnp.asarray(np.ascontiguousarray(fourier_table(PT, CT, 0.5).T) * np.float32(CT / PT)).astype(BF16)
    phi_down = jnp.asarray(
        fourier_table(PP, SUBBOX_HEADINGS, 0.0) * np.float32(SUBBOX_HEADINGS / PP)
    ).astype(BF16)
    cos_np, sin_np = shift_tables()
    cos_t, sin_t = jnp.asarray(cos_np), jnp.asarray(sin_np)

    box, angle = lax.axis_index("box"), lax.axis_index("angle")
    core = angle % 2
    mine = jnp.where(core == 0, box // SIDE, box % SIDE)
    other = jnp.where(core == 0, box % SIDE, box // SIDE)
    where = jnp.stack([core, mine, other]).astype(I32)

    whole = swap(child_field, "angle").reshape(8, 8, 2, 8, 128)
    parents = swap(lift(whole, tuple(map(hold, (theta_up, phi_up, cos_t, sin_t)))), "angle")
    wanted, child_code, parent_code = plan(
        where, child_list, child_op, child_home, parent_list, parent_op, parent_home
    )
    own = jnp.concatenate([child_field.reshape(128, 8, 128), parents.reshape(128, 8, 128)])
    up2, down2 = hop(own, 2), hop(own, -2)
    up1, down1 = hop(own, 1), hop(own, -1)
    onward = jnp.where(mine % 2 == 0, up2, down2)
    pairs = [(g[i], g[(i + 2 - 4 * (i % 2)) % SIDE]) for g in SPREAD for i in range(SIDE)]
    up4 = lax.ppermute(onward, BOTH, pairs)
    up3, down3 = hop(up2, 1), hop(down2, -1)
    blocks = [own, down1, down2, down3, up4, up3, up2, up1]
    asked = swap(wanted.reshape(SIDE, 1, 128), BOTH, axis_index_groups=TRADE).reshape(SIDE, 128)
    parents_out, *children_out = select(where, asked, blocks)
    parents_in = swap(parents_out, BOTH, axis_index_groups=TRADE)
    children_in = {0: children_out[0]}
    for d in (4, 3, 5, 2, 6, 1, 7):
        children_in[d] = hop(children_out[d], d, TRADE)
    sums = far_parents(hold(parent_code), parents_in.reshape(128, 8, 8, 128), parent_ops)
    turned = swap(sums, "angle").reshape(8, 2, 8, 8, 128)
    term = lower(turned, (theta_down, hold(phi_down), cos_t, sin_t))
    term = swap(term, "angle").reshape(64, 2, 8, 128)
    child_far = far_children(hold(child_code), [children_in[d] for d in range(SIDE)], child_ops)
    return (child_far + term.astype(F32)).astype(BF16)


def solution(mesh):
    return jax.shard_map(
        local,
        mesh=mesh,
        in_specs=(
            P("box", None, "angle", None),
            P("box", None),
            P("box", None),
            P(),
            P(None, None, "angle", None),
            P("box", None),
            P("box", None),
            P(),
            P(None, None, "angle", None),
        ),
        out_specs=P("box", None, "angle", None),
        check_vma=False,
    )
```

```python
import math

import jax
import jax.numpy as jnp
import numpy as np
from jax import lax
from jax.experimental import pallas as pl
from jax.experimental.pallas import tpu as pltpu
from jax.sharding import PartitionSpec as P


CT = 64
SUBBOX_HEADINGS = 128
PT = 128
PP = 256
WAVE_NUMBER = 6.0
SIDE = 8
BOTH = ("box", "angle")
F32, BF16, I32 = jnp.float32, jnp.bfloat16, jnp.int32
VM = pltpu.VMEM
ANY = pl.ANY
GRANT = 12 << 20


def fourier_table(fine_count, coarse_count, offset):
    f32 = np.float32
    fine = (np.arange(fine_count, dtype=f32) + f32(offset)) / f32(fine_count)
    coarse = (np.arange(coarse_count, dtype=f32) + f32(offset)) / f32(coarse_count)
    x = fine[:, None] - coarse[None, :]
    harmonic = np.arange(1, coarse_count // 2, dtype=f32)
    cosines = np.cos(f32(2.0 * math.pi) * harmonic * x[:, :, None])
    summed = f32(1.0) + f32(2.0) * cosines.sum(2, dtype=np.float64) + np.cos(f32(math.pi * coarse_count) * x)
    return (summed / coarse_count).astype(f32)


def shift_tables():
    f32 = np.float32
    polar = (f32(math.pi) * (np.arange(PT, dtype=f32) + f32(0.5)) / f32(PT)).astype(f32)
    heading = (f32(2.0 * math.pi / PP) * np.arange(PP, dtype=f32)).astype(f32)
    cos_h, sin_h = np.cos(heading), np.sin(heading)
    across = np.stack([-cos_h - sin_h, cos_h - sin_h])
    arg = (f32(WAVE_NUMBER) * np.sin(polar))[None, :, None] * across[:, None, :]
    return np.cos(arg).astype(f32), np.sin(arg).astype(f32)


def hold(x):
    return pltpu.with_memory_space_constraint(x, pltpu.HBM)


def bmm(a, b):
    return lax.dot_general(a, b, (((1,), (0,)), ((), ())), preferred_element_type=F32)


def iota(shape, dim):
    return lax.broadcasted_iota(I32, shape, dim)


def plan_level(ids_ref, op_ref, home_ref, core, mine, other, rows_device, cap, empty_op, code_ref):
    slots, rows = ids_ref.shape
    home = home_ref[...]
    owner = home // rows_device
    table = jnp.concatenate([owner, home - owner * rows_device], axis=0).astype(F32).astype(BF16)
    highs = home.shape[0]
    before = (iota((rows, rows), 0) < iota((rows, rows), 1)).astype(F32).astype(BF16)
    carry = jnp.zeros((SIDE, 1), F32)
    wanted = jnp.zeros((2 * SIDE, cap), F32)
    for j in range(slots):
        ids = ids_ref[pl.ds(j, 1), :]
        usable = ids >= 0
        safe = jnp.maximum(ids, 0)
        high, low = safe >> 7, safe & 127
        low_hot = (iota((128, rows), 0) == low).astype(F32).astype(BF16)
        picked = bmm(table, low_hot)
        high_hot = (iota((highs, rows), 0) == high).astype(F32)
        own = jnp.sum(picked[:highs] * high_hot, axis=0, keepdims=True).astype(I32)
        loc = jnp.sum(picked[highs:] * high_hot, axis=0, keepdims=True)
        along_y, along_z = own >> 3, own & 7
        column = jnp.where(core == 0, along_z, along_y)
        place = (jnp.where(core == 0, along_y, along_z) - mine) & 7
        hot = jnp.where((iota((SIDE, rows), 0) == column) & usable, 1.0, 0.0)
        hot_b = hot.astype(BF16)
        prefix = bmm(hot_b, before) + carry
        carry = carry + jnp.sum(hot, axis=1, keepdims=True)
        rank = jnp.sum(hot * prefix, axis=0, keepdims=True).astype(I32)
        lane = column if other is None else (other - column) & 7
        position = lane * cap + rank
        code_ref[pl.ds(j, 1), pl.ds(0, rows)] = jnp.where(
            usable, position * 64 + op_ref[pl.ds(j, 1), :], empty_op
        )
        rank_hot = (iota((cap, rows), 0) == rank).astype(F32).astype(BF16)
        both = jnp.concatenate([hot * place.astype(F32), hot * loc], axis=0).astype(BF16)
        wanted = wanted + lax.dot_general(
            both, rank_hot, (((1,), (1,)), ((), ())), preferred_element_type=F32
        )
    return (wanted[:SIDE] * rows_device + wanted[SIDE:]).astype(I32)


def plan_body(where, cl, co, ch, plist, po, ph, want_ref, ccode_ref, pcode_ref):
    core, mine, other = where[0], where[1], where[2]
    want_ref[...] = jnp.zeros(want_ref.shape, I32)
    want_ref[:, pl.ds(0, 64)] = plan_level(cl, co, ch, core, mine, other, 64, 64, 40, ccode_ref)
    want_ref[:, pl.ds(64, 16)] = plan_level(plist, po, ph, core, mine, None, 16, 16, 40, pcode_ref)


def plan(where, child_list, child_op, child_home, parent_list, parent_op, parent_home):
    args = (
        where,
        *map(
            hold,
            (
                child_list.T,
                child_op.T,
                child_home.reshape(-1, 128),
                parent_list.T,
                parent_op.T,
                parent_home.reshape(-1, 128),
            ),
        ),
    )
    return pl.pallas_call(
        plan_body,
        out_shape=(
            jax.ShapeDtypeStruct((SIDE, 128), I32),
            pltpu.HBM((8, 64), I32),
            pltpu.HBM((8, 16), I32),
        ),
        in_specs=[pl.BlockSpec(memory_space=pltpu.SMEM)] + [pl.BlockSpec(memory_space=VM)] * 6,
        out_specs=(pl.BlockSpec(memory_space=VM),) * 3,
        compiler_params=pltpu.CompilerParams(vmem_limit_bytes=GRANT),
        name="plan",
    )(*args)


def up_body(field, theta_h, phi_h, cos_h, sin_h, out, theta, phi, cos_t, sin_t, wide, sems):
    copies = fetch((theta_h, phi_h, cos_h, sin_h), (theta, phi, cos_t, sin_t), sems)
    copies[0].wait()
    copies[1].wait()
    for r in range(8):
        for c in range(2):
            rows = jnp.concatenate([field[s, r, c] for s in range(8)], axis=0)
            stretched = bmm(theta[...], rows).astype(BF16)
            wide[r * 2 + c] = bmm(stretched, phi[...])
    copies[2].wait()
    copies[3].wait()
    for q in range(2):
        for u in range(PT // 8):
            at = pl.ds(u * 8, 8)
            w = [[wide[(q * 4 + k) * 2 + c, at, :] for c in range(2)] for k in range(4)]
            real = jnp.zeros((8, PP), F32)
            imag = jnp.zeros((8, PP), F32)
            for t, (k, m) in enumerate(((0, 3), (1, 2))):
                cs, sn = cos_t[t, at, :], sin_t[t, at, :]
                real = real + cs * (w[k][0] + w[m][0]) - sn * (w[k][1] - w[m][1])
                imag = imag + cs * (w[k][1] + w[m][1]) + sn * (w[k][0] - w[m][0])
            for c, part in enumerate((real, imag)):
                part = part.astype(BF16)
                for v in range(2):
                    out[u // 2, q, c * 4 + (u % 2) * 2 + v] = part[:, v * 128 : (v + 1) * 128]


def fetch(sources, targets, sems):
    copies = [pltpu.make_async_copy(a, b, sems.at[i]) for i, (a, b) in enumerate(zip(sources, targets))]
    for copy in copies:
        copy.start()
    return copies


def lift(field, tables):
    return pl.pallas_call(
        up_body,
        out_shape=jax.ShapeDtypeStruct((8, 2, 8, 8, 128), BF16),
        in_specs=[pl.BlockSpec(memory_space=VM)] + [pl.BlockSpec(memory_space=pltpu.HBM)] * 4,
        out_specs=pl.BlockSpec(memory_space=VM),
        scratch_shapes=[pltpu.VMEM(t.shape, t.dtype) for t in tables]
        + [pltpu.VMEM((16, PT, PP), F32), pltpu.SemaphoreType.DMA((4,))],
        compiler_params=pltpu.CompilerParams(vmem_limit_bytes=GRANT),
        name="lift",
    )(field, *tables)


def select_body(where, asked, *refs):
    blocks, parents, children = refs[:8], refs[8], refs[9:17]
    pool, parent_buf, child_buf, sems, parent_sems, child_sems = refs[17:]
    copies = [
        pltpu.make_async_copy(
            b.at[pl.ds(128 * half, 128)], pool.at[half, i], sems.at[half, i]
        )
        for half in (1, 0)
        for i, b in enumerate(blocks)
    ]
    for copy in copies:
        copy.start()

    def child_out(d):
        return pltpu.make_async_copy(child_buf.at[d], children[d], child_sems.at[d])

    def parent_out(h):
        return pltpu.make_async_copy(parent_buf.at[h], parents.at[h], parent_sems.at[h])

    for copy in copies[:8]:
        copy.wait()

    def peer(h, carry):
        for k in range(16):
            row = asked[h, 64 + k]
            at = pl.multiple_of((row & 15) * 8, 8)
            parent_buf[h, k] = pool[1, row >> 4, pl.ds(at, 8)]
        parent_out(h).start()
        return carry

    lax.fori_loop(0, SIDE, peer, 0)
    for copy in copies[8:]:
        copy.wait()
    for d in range(SIDE):
        h = (where[2] + d) & 7

        def some(i, carry):
            for j in range(16):
                k = i * 16 + j
                row = asked[h, k]
                at = pl.multiple_of((row & 63) * 2, 2)
                child_buf[d, k] = pool[0, row >> 6, pl.ds(at, 2)]
            return carry

        lax.fori_loop(0, 4, some, 0)
        child_out(d).start()
    for h in range(SIDE):
        parent_out(h).wait()
    for d in range(SIDE):
        child_out(d).wait()


def select(where, asked, blocks):
    hbm = pl.BlockSpec(memory_space=pltpu.HBM)
    return pl.pallas_call(
        select_body,
        out_shape=(pltpu.HBM((SIDE, 16, 8, 8, 128), BF16),) + (pltpu.HBM((64, 2, 8, 128), BF16),) * SIDE,
        in_specs=[pl.BlockSpec(memory_space=pltpu.SMEM)] * 2 + [pl.BlockSpec(memory_space=ANY)] * 8,
        out_specs=(hbm,) * 9,
        scratch_shapes=[
            pltpu.VMEM((2, 8, 128, 8, 128), BF16),
            pltpu.VMEM((SIDE, 16, 8, 8, 128), BF16),
            pltpu.VMEM((SIDE, 64, 2, 8, 128), BF16),
            pltpu.SemaphoreType.DMA((2, 8)),
            pltpu.SemaphoreType.DMA((8,)),
            pltpu.SemaphoreType.DMA((8,)),
        ],
        compiler_params=pltpu.CompilerParams(vmem_limit_bytes=GRANT),
        name="select",
    )(where, asked, *blocks)


def parent_far_body(code, recv, ops_hbm, out, ops, sem):
    copy = pltpu.make_async_copy(ops_hbm, ops.at[pl.ds(0, 40)], sem)
    copy.start()
    ops[40] = jnp.zeros(ops.shape[1:], BF16)
    copy.wait()

    def row(r, carry):
        real = [jnp.zeros((8, 128), F32) for _ in range(4)]
        imag = [jnp.zeros((8, 128), F32) for _ in range(4)]
        for j in range(8):
            both = code[j, r]
            at, op = both >> 6, both & 63
            for t in range(4):
                u, v = t // 2, t % 2
                a = ops[op, 0, u * 8 : u * 8 + 8, v * 128 : v * 128 + 128].astype(F32)
                b = ops[op, 1, u * 8 : u * 8 + 8, v * 128 : v * 128 + 128].astype(F32)
                c = recv[at, t].astype(F32)
                d = recv[at, 4 + t].astype(F32)
                real[t] = real[t] + (a * c - b * d)
                imag[t] = imag[t] + (a * d + b * c)
        for t in range(4):
            out[r, t] = real[t].astype(BF16)
            out[r, 4 + t] = imag[t].astype(BF16)
        return carry

    lax.fori_loop(0, 16, row, 0)


def far_parents(code, recv, ops):
    return pl.pallas_call(
        parent_far_body,
        out_shape=jax.ShapeDtypeStruct((16, 8, 8, 128), BF16),
        in_specs=[
            pl.BlockSpec(memory_space=pltpu.SMEM),
            pl.BlockSpec(memory_space=VM),
            pl.BlockSpec(memory_space=ANY),
        ],
        out_specs=pl.BlockSpec(memory_space=VM),
        scratch_shapes=[pltpu.VMEM((41, 2, 16, PP), BF16), pltpu.SemaphoreType.DMA],
        compiler_params=pltpu.CompilerParams(vmem_limit_bytes=GRANT),
        name="far_parents",
    )(code, recv, ops)


def child_far_body(code, *refs):
    blocks, ops_hbm, out, recv, ops, sems = refs[:8], *refs[8:]
    copies = fetch((ops_hbm, *blocks), (ops.at[pl.ds(0, 40)], *(recv.at[i] for i in range(8))), sems)
    ops[40] = jnp.zeros(ops.shape[1:], BF16)
    for copy in copies:
        copy.wait()

    def row(r, carry):
        real = jnp.zeros((8, 128), F32)
        imag = jnp.zeros((8, 128), F32)
        for j in range(8):
            both = code[j, r]
            lane, at, op = both >> 12, (both >> 6) & 63, both & 63
            a, b = ops[op, 0].astype(F32), ops[op, 1].astype(F32)
            c, d = recv[lane, at, 0].astype(F32), recv[lane, at, 1].astype(F32)
            real = real + (a * c - b * d)
            imag = imag + (a * d + b * c)
        out[r, 0] = real
        out[r, 1] = imag
        return carry

    lax.fori_loop(0, 64, row, 0, unroll=2)


def far_children(code, blocks, ops):
    return pl.pallas_call(
        child_far_body,
        out_shape=jax.ShapeDtypeStruct((64, 2, 8, 128), F32),
        in_specs=[pl.BlockSpec(memory_space=pltpu.SMEM)] + [pl.BlockSpec(memory_space=ANY)] * 9,
        out_specs=pl.BlockSpec(memory_space=VM),
        scratch_shapes=[
            pltpu.VMEM((SIDE, 64, 2, 8, 128), BF16),
            pltpu.VMEM((41, 2, 8, 128), BF16),
            pltpu.SemaphoreType.DMA((9,)),
        ],
        compiler_params=pltpu.CompilerParams(vmem_limit_bytes=GRANT),
        name="far_children",
    )(code, *blocks, ops)


def down_body(far, theta, phi_h, cos_t, sin_t, out, phi, turned, buf, sem, out_sems):
    copy = pltpu.make_async_copy(phi_h, phi, sem)
    copy.start()
    for q in range(2):
        for u in range(PT // 8):
            at = pl.ds(u * 8, 8)
            re, im = (
                jnp.concatenate(
                    [far[u // 2, q, c * 4 + (u % 2) * 2 + v].astype(F32) for v in range(2)], axis=1
                )
                for c in range(2)
            )
            for t, (k, m) in enumerate(((0, 3), (1, 2))):
                cs, sn = cos_t[t, at, :], sin_t[t, at, :]
                cr, si, ci, sr = cs * re, sn * im, cs * im, sn * re
                turned[(q * 4 + k) * 2, at, :] = (cr + si).astype(BF16)
                turned[(q * 4 + k) * 2 + 1, at, :] = (ci - sr).astype(BF16)
                turned[(q * 4 + m) * 2, at, :] = (cr - si).astype(BF16)
                turned[(q * 4 + m) * 2 + 1, at, :] = (ci + sr).astype(BF16)
    copy.wait()
    pieces = [
        pltpu.make_async_copy(buf.at[r], out.at[pl.ds(0, 8), r], out_sems.at[r]) for r in range(8)
    ]
    for r in range(8):
        for c in range(2):
            narrowed = bmm(turned[r * 2 + c], phi[...]).astype(BF16)
            term = bmm(theta[...], narrowed).astype(BF16)
            for s in range(8):
                buf[r, s, c] = term[s * 8 : s * 8 + 8, :]
        pieces[r].start()
    for piece in pieces:
        piece.wait()


def lower(far, tables):
    return pl.pallas_call(
        down_body,
        out_shape=pltpu.HBM((8, 8, 2, 8, 128), BF16),
        in_specs=[pl.BlockSpec(memory_space=ANY if i == 2 else VM) for i in range(5)],
        out_specs=pl.BlockSpec(memory_space=pltpu.HBM),
        scratch_shapes=[
            pltpu.VMEM(tables[1].shape, BF16),
            pltpu.VMEM((16, PT, PP), BF16),
            pltpu.VMEM((8, 8, 2, 8, 128), BF16),
            pltpu.SemaphoreType.DMA,
            pltpu.SemaphoreType.DMA((8,)),
        ],
        compiler_params=pltpu.CompilerParams(vmem_limit_bytes=GRANT),
        name="lower",
    )(far, *tables)


def groups(straight):
    found = []
    for angle in range(8):
        for o in range(SIDE):
            line = [(o, i) if (angle % 2) == straight else (i, o) for i in range(SIDE)]
            found.append([(y * SIDE + z) * 8 + angle for y, z in line])
    return found


SPREAD, TRADE = groups(1), groups(0)


def hop(x, step, lines=SPREAD):
    pairs = [(g[i], g[(i + step) % SIDE]) for g in lines for i in range(SIDE)]
    return lax.ppermute(x, BOTH, pairs)


def swap(x, axis, **kw):
    return lax.all_to_all(x, axis, split_axis=0, concat_axis=0, tiled=True, **kw)


def local(
    child_field,
    child_list,
    child_op,
    child_home,
    child_ops,
    parent_list,
    parent_op,
    parent_home,
    parent_ops,
):
    theta_up = jnp.asarray(fourier_table(PT, CT, 0.5)).astype(BF16)
    phi_up = jnp.asarray(np.ascontiguousarray(fourier_table(PP, SUBBOX_HEADINGS, 0.0).T)).astype(BF16)
    theta_down = jnp.asarray(np.ascontiguousarray(fourier_table(PT, CT, 0.5).T) * np.float32(CT / PT)).astype(BF16)
    phi_down = jnp.asarray(
        fourier_table(PP, SUBBOX_HEADINGS, 0.0) * np.float32(SUBBOX_HEADINGS / PP)
    ).astype(BF16)
    cos_np, sin_np = shift_tables()
    cos_t, sin_t = jnp.asarray(cos_np), jnp.asarray(sin_np)

    box, angle = lax.axis_index("box"), lax.axis_index("angle")
    core = angle % 2
    mine = jnp.where(core == 0, box // SIDE, box % SIDE)
    other = jnp.where(core == 0, box % SIDE, box // SIDE)
    where = jnp.stack([core, mine, other]).astype(I32)

    whole = swap(child_field, "angle").reshape(8, 8, 2, 8, 128)
    parents = swap(lift(whole, tuple(map(hold, (theta_up, phi_up, cos_t, sin_t)))), "angle")
    wanted, child_code, parent_code = plan(
        where, child_list, child_op, child_home, parent_list, parent_op, parent_home
    )
    own = jnp.concatenate([child_field.reshape(128, 8, 128), parents.reshape(128, 8, 128)])
    up2, down2 = hop(own, 2), hop(own, -2)
    up1, down1 = hop(own, 1), hop(own, -1)
    onward = jnp.where(mine % 2 == 0, up2, down2)
    pairs = [(g[i], g[(i + 2 - 4 * (i % 2)) % SIDE]) for g in SPREAD for i in range(SIDE)]
    up4 = lax.ppermute(onward, BOTH, pairs)
    up3, down3 = hop(up2, 1), hop(down2, -1)
    blocks = [own, down1, down2, down3, up4, up3, up2, up1]
    asked = swap(wanted.reshape(SIDE, 1, 128), BOTH, axis_index_groups=TRADE).reshape(SIDE, 128)
    parents_out, *children_out = select(where, asked, blocks)
    parents_in = swap(parents_out, BOTH, axis_index_groups=TRADE)
    children_in = {0: children_out[0]}
    for d in (4, 3, 5, 2, 6, 1, 7):
        children_in[d] = hop(children_out[d], d, TRADE)
    sums = far_parents(hold(parent_code), parents_in.reshape(128, 8, 8, 128), parent_ops)
    turned = swap(sums, "angle").reshape(8, 2, 8, 8, 128)
    term = lower(turned, (theta_down, hold(phi_down), cos_t, sin_t))
    term = swap(term, "angle").reshape(64, 2, 8, 128)
    child_far = far_children(hold(child_code), [children_in[d] for d in range(SIDE)], child_ops)
    return (child_far + term.astype(F32)).astype(BF16)


def solution(mesh):
    return jax.shard_map(
        local,
        mesh=mesh,
        in_specs=(
            P("box", None, "angle", None),
            P("box", None),
            P("box", None),
            P(),
            P(None, None, "angle", None),
            P("box", None),
            P("box", None),
            P(),
            P(None, None, "angle", None),
        ),
        out_specs=P("box", None, "angle", None),
        check_vma=False,
    )
```

```python
import math

import jax
import jax.numpy as jnp
import numpy as np
from jax import lax
from jax.experimental import pallas as pl
from jax.experimental.pallas import tpu as pltpu
from jax.sharding import PartitionSpec as P


CT = 64
SUBBOX_HEADINGS = 128
PT = 128
PP = 256
WAVE_NUMBER = 6.0
SIDE = 8
BOTH = ("box", "angle")
F32, BF16, I32 = jnp.float32, jnp.bfloat16, jnp.int32
VM = pltpu.VMEM
ANY = pl.ANY
GRANT = 12 << 20


def fourier_table(fine_count, coarse_count, offset):
    f32 = np.float32
    fine = (np.arange(fine_count, dtype=f32) + f32(offset)) / f32(fine_count)
    coarse = (np.arange(coarse_count, dtype=f32) + f32(offset)) / f32(coarse_count)
    x = fine[:, None] - coarse[None, :]
    harmonic = np.arange(1, coarse_count // 2, dtype=f32)
    cosines = np.cos(f32(2.0 * math.pi) * harmonic * x[:, :, None])
    summed = f32(1.0) + f32(2.0) * cosines.sum(2, dtype=np.float64) + np.cos(f32(math.pi * coarse_count) * x)
    return (summed / coarse_count).astype(f32)


def shift_tables():
    f32 = np.float32
    polar = (f32(math.pi) * (np.arange(PT, dtype=f32) + f32(0.5)) / f32(PT)).astype(f32)
    heading = (f32(2.0 * math.pi / PP) * np.arange(PP, dtype=f32)).astype(f32)
    cos_h, sin_h = np.cos(heading), np.sin(heading)
    across = np.stack([-cos_h - sin_h, cos_h - sin_h])
    arg = (f32(WAVE_NUMBER) * np.sin(polar))[None, :, None] * across[:, None, :]
    return np.cos(arg).astype(f32), np.sin(arg).astype(f32)


def hold(x):
    return pltpu.with_memory_space_constraint(x, pltpu.HBM)


def bmm(a, b):
    return lax.dot_general(a, b, (((1,), (0,)), ((), ())), preferred_element_type=F32)


def iota(shape, dim):
    return lax.broadcasted_iota(I32, shape, dim)


def plan_level(ids_ref, op_ref, home_ref, core, mine, other, rows_device, cap, empty_op, code_ref):
    slots, rows = ids_ref.shape
    home = home_ref[...]
    owner = home // rows_device
    table = jnp.concatenate([owner, home - owner * rows_device], axis=0).astype(F32).astype(BF16)
    highs = home.shape[0]
    before = (iota((rows, rows), 0) < iota((rows, rows), 1)).astype(F32).astype(BF16)
    carry = jnp.zeros((SIDE, 1), F32)
    wanted = jnp.zeros((2 * SIDE, cap), F32)
    for j in range(slots):
        ids = ids_ref[pl.ds(j, 1), :]
        usable = ids >= 0
        safe = jnp.maximum(ids, 0)
        high, low = safe >> 7, safe & 127
        low_hot = (iota((128, rows), 0) == low).astype(F32).astype(BF16)
        picked = bmm(table, low_hot)
        high_hot = (iota((highs, rows), 0) == high).astype(F32)
        own = jnp.sum(picked[:highs] * high_hot, axis=0, keepdims=True).astype(I32)
        loc = jnp.sum(picked[highs:] * high_hot, axis=0, keepdims=True)
        along_y, along_z = own >> 3, own & 7
        column = jnp.where(core == 0, along_z, along_y)
        place = (jnp.where(core == 0, along_y, along_z) - mine) & 7
        hot = jnp.where((iota((SIDE, rows), 0) == column) & usable, 1.0, 0.0)
        hot_b = hot.astype(BF16)
        prefix = bmm(hot_b, before) + carry
        carry = carry + jnp.sum(hot, axis=1, keepdims=True)
        rank = jnp.sum(hot * prefix, axis=0, keepdims=True).astype(I32)
        lane = column if other is None else (other - column) & 7
        position = lane * cap + rank
        code_ref[pl.ds(j, 1), pl.ds(0, rows)] = jnp.where(
            usable, position * 64 + op_ref[pl.ds(j, 1), :], empty_op
        )
        rank_hot = (iota((cap, rows), 0) == rank).astype(F32).astype(BF16)
        both = jnp.concatenate([hot * place.astype(F32), hot * loc], axis=0).astype(BF16)
        wanted = wanted + lax.dot_general(
            both, rank_hot, (((1,), (1,)), ((), ())), preferred_element_type=F32
        )
    return (wanted[:SIDE] * rows_device + wanted[SIDE:]).astype(I32)


def plan_body(where, cl, co, ch, plist, po, ph, want_ref, ccode_ref, pcode_ref):
    core, mine, other = where[0], where[1], where[2]
    want_ref[...] = jnp.zeros(want_ref.shape, I32)
    want_ref[:, pl.ds(0, 64)] = plan_level(cl, co, ch, core, mine, other, 64, 64, 40, ccode_ref)
    want_ref[:, pl.ds(64, 16)] = plan_level(plist, po, ph, core, mine, None, 16, 16, 40, pcode_ref)


def plan(where, child_list, child_op, child_home, parent_list, parent_op, parent_home):
    args = (
        where,
        *map(
            hold,
            (
                child_list.T,
                child_op.T,
                child_home.reshape(-1, 128),
                parent_list.T,
                parent_op.T,
                parent_home.reshape(-1, 128),
            ),
        ),
    )
    return pl.pallas_call(
        plan_body,
        out_shape=(
            jax.ShapeDtypeStruct((SIDE, 128), I32),
            pltpu.HBM((8, 64), I32),
            pltpu.HBM((8, 16), I32),
        ),
        in_specs=[pl.BlockSpec(memory_space=pltpu.SMEM)] + [pl.BlockSpec(memory_space=VM)] * 6,
        out_specs=(pl.BlockSpec(memory_space=VM),) * 3,
        compiler_params=pltpu.CompilerParams(vmem_limit_bytes=GRANT),
        name="plan",
    )(*args)


def up_body(field, theta_h, phi_h, cos_h, sin_h, out, theta, phi, cos_t, sin_t, wide, sems):
    copies = fetch((theta_h, phi_h, cos_h, sin_h), (theta, phi, cos_t, sin_t), sems)
    copies[0].wait()
    copies[1].wait()
    for i in range(4):
        rows = jnp.concatenate(
            [
                jnp.concatenate([field[s, (i * 4 + k) // 2, k % 2] for s in range(8)], axis=0)
                for k in range(4)
            ],
            axis=1,
        )
        stretched = bmm(theta[...], rows).astype(BF16)
        tall = jnp.concatenate([stretched[:, k * 128 : k * 128 + 128] for k in range(4)], axis=0)
        spread = bmm(tall, phi[...])
        for k in range(4):
            wide[i * 4 + k] = spread[k * PT : (k + 1) * PT]
    copies[2].wait()
    copies[3].wait()
    for q in range(2):
        for u in range(PT // 8):
            at = pl.ds(u * 8, 8)
            w = [[wide[(q * 4 + k) * 2 + c, at, :] for c in range(2)] for k in range(4)]
            real = jnp.zeros((8, PP), F32)
            imag = jnp.zeros((8, PP), F32)
            for t, (k, m) in enumerate(((0, 3), (1, 2))):
                cs, sn = cos_t[t, at, :], sin_t[t, at, :]
                real = real + cs * (w[k][0] + w[m][0]) - sn * (w[k][1] - w[m][1])
                imag = imag + cs * (w[k][1] + w[m][1]) + sn * (w[k][0] - w[m][0])
            for c, part in enumerate((real, imag)):
                part = part.astype(BF16)
                for v in range(2):
                    out[u // 2, q, c * 4 + (u % 2) * 2 + v] = part[:, v * 128 : (v + 1) * 128]


def fetch(sources, targets, sems):
    copies = [pltpu.make_async_copy(a, b, sems.at[i]) for i, (a, b) in enumerate(zip(sources, targets))]
    for copy in copies:
        copy.start()
    return copies


def lift(field, tables):
    return pl.pallas_call(
        up_body,
        out_shape=jax.ShapeDtypeStruct((8, 2, 8, 8, 128), BF16),
        in_specs=[pl.BlockSpec(memory_space=VM)] + [pl.BlockSpec(memory_space=pltpu.HBM)] * 4,
        out_specs=pl.BlockSpec(memory_space=VM),
        scratch_shapes=[pltpu.VMEM(t.shape, t.dtype) for t in tables]
        + [pltpu.VMEM((16, PT, PP), F32), pltpu.SemaphoreType.DMA((4,))],
        compiler_params=pltpu.CompilerParams(vmem_limit_bytes=GRANT),
        name="lift",
    )(field, *tables)


def select_body(where, asked, *refs):
    blocks, parents, children = refs[:8], refs[8], refs[9:17]
    pool, parent_buf, child_buf, sems, parent_sems, child_sems = refs[17:]
    copies = [
        pltpu.make_async_copy(
            b.at[pl.ds(128 * half, 128)], pool.at[half, i], sems.at[half, i]
        )
        for half in (1, 0)
        for i, b in enumerate(blocks)
    ]
    for copy in copies:
        copy.start()

    def child_out(d):
        return pltpu.make_async_copy(child_buf.at[d], children[d], child_sems.at[d])

    def parent_out(h):
        return pltpu.make_async_copy(parent_buf.at[h], parents.at[h], parent_sems.at[h])

    for copy in copies[:8]:
        copy.wait()

    def peer(h, carry):
        for k in range(16):
            row = asked[h, 64 + k]
            at = pl.multiple_of((row & 15) * 8, 8)
            parent_buf[h, k] = pool[1, row >> 4, pl.ds(at, 8)]
        parent_out(h).start()
        return carry

    lax.fori_loop(0, SIDE, peer, 0)
    for copy in copies[8:]:
        copy.wait()
    for d in range(SIDE):
        h = (where[2] + d) & 7

        def some(i, carry):
            for j in range(16):
                k = i * 16 + j
                row = asked[h, k]
                at = pl.multiple_of((row & 63) * 2, 2)
                child_buf[d, k] = pool[0, row >> 6, pl.ds(at, 2)]
            return carry

        lax.fori_loop(0, 4, some, 0)
        child_out(d).start()
    for h in range(SIDE):
        parent_out(h).wait()
    for d in range(SIDE):
        child_out(d).wait()


def select(where, asked, blocks):
    hbm = pl.BlockSpec(memory_space=pltpu.HBM)
    return pl.pallas_call(
        select_body,
        out_shape=(pltpu.HBM((SIDE, 16, 8, 8, 128), BF16),) + (pltpu.HBM((64, 2, 8, 128), BF16),) * SIDE,
        in_specs=[pl.BlockSpec(memory_space=pltpu.SMEM)] * 2 + [pl.BlockSpec(memory_space=ANY)] * 8,
        out_specs=(hbm,) * 9,
        scratch_shapes=[
            pltpu.VMEM((2, 8, 128, 8, 128), BF16),
            pltpu.VMEM((SIDE, 16, 8, 8, 128), BF16),
            pltpu.VMEM((SIDE, 64, 2, 8, 128), BF16),
            pltpu.SemaphoreType.DMA((2, 8)),
            pltpu.SemaphoreType.DMA((8,)),
            pltpu.SemaphoreType.DMA((8,)),
        ],
        compiler_params=pltpu.CompilerParams(vmem_limit_bytes=GRANT),
        name="select",
    )(where, asked, *blocks)


def parent_far_body(code, recv, ops_hbm, out, ops, sem):
    copy = pltpu.make_async_copy(ops_hbm, ops.at[pl.ds(0, 40)], sem)
    copy.start()
    ops[40] = jnp.zeros(ops.shape[1:], BF16)
    copy.wait()

    def row(r, carry):
        real = [jnp.zeros((8, 128), F32) for _ in range(4)]
        imag = [jnp.zeros((8, 128), F32) for _ in range(4)]
        for j in range(8):
            both = code[j, r]
            at, op = both >> 6, both & 63
            for t in range(4):
                u, v = t // 2, t % 2
                a = ops[op, 0, u * 8 : u * 8 + 8, v * 128 : v * 128 + 128].astype(F32)
                b = ops[op, 1, u * 8 : u * 8 + 8, v * 128 : v * 128 + 128].astype(F32)
                c = recv[at, t].astype(F32)
                d = recv[at, 4 + t].astype(F32)
                real[t] = real[t] + (a * c - b * d)
                imag[t] = imag[t] + (a * d + b * c)
        for t in range(4):
            out[r, t] = real[t].astype(BF16)
            out[r, 4 + t] = imag[t].astype(BF16)
        return carry

    lax.fori_loop(0, 16, row, 0)


def far_parents(code, recv, ops):
    return pl.pallas_call(
        parent_far_body,
        out_shape=jax.ShapeDtypeStruct((16, 8, 8, 128), BF16),
        in_specs=[
            pl.BlockSpec(memory_space=pltpu.SMEM),
            pl.BlockSpec(memory_space=VM),
            pl.BlockSpec(memory_space=ANY),
        ],
        out_specs=pl.BlockSpec(memory_space=VM),
        scratch_shapes=[pltpu.VMEM((41, 2, 16, PP), BF16), pltpu.SemaphoreType.DMA],
        compiler_params=pltpu.CompilerParams(vmem_limit_bytes=GRANT),
        name="far_parents",
    )(code, recv, ops)


def child_far_body(code, *refs):
    blocks, ops_hbm, out, recv, ops, sems = refs[:8], *refs[8:]
    copies = fetch((ops_hbm, *blocks), (ops.at[pl.ds(0, 40)], *(recv.at[i] for i in range(8))), sems)
    ops[40] = jnp.zeros(ops.shape[1:], BF16)
    for copy in copies:
        copy.wait()

    def row(r, carry):
        real = jnp.zeros((8, 128), F32)
        imag = jnp.zeros((8, 128), F32)
        for j in range(8):
            both = code[j, r]
            lane, at, op = both >> 12, (both >> 6) & 63, both & 63
            a, b = ops[op, 0].astype(F32), ops[op, 1].astype(F32)
            c, d = recv[lane, at, 0].astype(F32), recv[lane, at, 1].astype(F32)
            real = real + (a * c - b * d)
            imag = imag + (a * d + b * c)
        out[r, 0] = real
        out[r, 1] = imag
        return carry

    lax.fori_loop(0, 64, row, 0, unroll=2)


def far_children(code, blocks, ops):
    return pl.pallas_call(
        child_far_body,
        out_shape=jax.ShapeDtypeStruct((64, 2, 8, 128), F32),
        in_specs=[pl.BlockSpec(memory_space=pltpu.SMEM)] + [pl.BlockSpec(memory_space=ANY)] * 9,
        out_specs=pl.BlockSpec(memory_space=VM),
        scratch_shapes=[
            pltpu.VMEM((SIDE, 64, 2, 8, 128), BF16),
            pltpu.VMEM((41, 2, 8, 128), BF16),
            pltpu.SemaphoreType.DMA((9,)),
        ],
        compiler_params=pltpu.CompilerParams(vmem_limit_bytes=GRANT),
        name="far_children",
    )(code, *blocks, ops)


def down_body(far, theta, phi_h, cos_t, sin_t, out, phi, turned, thin, sem):
    copy = pltpu.make_async_copy(phi_h, phi, sem)
    copy.start()
    for q in range(2):
        for u in range(PT // 8):
            at = pl.ds(u * 8, 8)
            re, im = (
                jnp.concatenate(
                    [far[u // 2, q, c * 4 + (u % 2) * 2 + v].astype(F32) for v in range(2)], axis=1
                )
                for c in range(2)
            )
            for t, (k, m) in enumerate(((0, 3), (1, 2))):
                cs, sn = cos_t[t, at, :], sin_t[t, at, :]
                cr, si, ci, sr = cs * re, sn * im, cs * im, sn * re
                turned[(q * 4 + k) * 2, at, :] = (cr + si).astype(BF16)
                turned[(q * 4 + k) * 2 + 1, at, :] = (ci - sr).astype(BF16)
                turned[(q * 4 + m) * 2, at, :] = (cr - si).astype(BF16)
                turned[(q * 4 + m) * 2 + 1, at, :] = (ci + sr).astype(BF16)
    copy.wait()
    for i in range(4):
        tall = jnp.concatenate([turned[i * 4 + k] for k in range(4)], axis=0)
        narrowed = bmm(tall, phi[...]).astype(BF16)
        for k in range(4):
            at = (i * 4 + k) * SUBBOX_HEADINGS
            thin[:, at : at + SUBBOX_HEADINGS] = narrowed[k * PT : (k + 1) * PT]
    for i in range(4):
        term = bmm(theta[...], thin[:, i * 512 : i * 512 + 512]).astype(BF16)
        for k in range(4):
            for s in range(8):
                out[s, (i * 4 + k) // 2, k % 2] = term[s * 8 : s * 8 + 8, k * 128 : k * 128 + 128]


def lower(far, tables):
    return pl.pallas_call(
        down_body,
        out_shape=jax.ShapeDtypeStruct((8, 8, 2, 8, 128), BF16),
        in_specs=[pl.BlockSpec(memory_space=ANY if i == 2 else VM) for i in range(5)],
        out_specs=pl.BlockSpec(memory_space=VM),
        scratch_shapes=[
            pltpu.VMEM(tables[1].shape, BF16),
            pltpu.VMEM((16, PT, PP), BF16),
            pltpu.VMEM((PT, 16 * SUBBOX_HEADINGS), BF16),
            pltpu.SemaphoreType.DMA,
        ],
        compiler_params=pltpu.CompilerParams(vmem_limit_bytes=GRANT),
        name="lower",
    )(far, *tables)


def groups(straight):
    found = []
    for angle in range(8):
        for o in range(SIDE):
            line = [(o, i) if (angle % 2) == straight else (i, o) for i in range(SIDE)]
            found.append([(y * SIDE + z) * 8 + angle for y, z in line])
    return found


SPREAD, TRADE = groups(1), groups(0)


def hop(x, step, lines=SPREAD):
    pairs = [(g[i], g[(i + step) % SIDE]) for g in lines for i in range(SIDE)]
    return lax.ppermute(x, BOTH, pairs)


def swap(x, axis, **kw):
    return lax.all_to_all(x, axis, split_axis=0, concat_axis=0, tiled=True, **kw)


def local(
    child_field,
    child_list,
    child_op,
    child_home,
    child_ops,
    parent_list,
    parent_op,
    parent_home,
    parent_ops,
):
    theta_up = jnp.asarray(fourier_table(PT, CT, 0.5)).astype(BF16)
    phi_up = jnp.asarray(np.ascontiguousarray(fourier_table(PP, SUBBOX_HEADINGS, 0.0).T)).astype(BF16)
    theta_down = jnp.asarray(np.ascontiguousarray(fourier_table(PT, CT, 0.5).T) * np.float32(CT / PT)).astype(BF16)
    phi_down = jnp.asarray(
        fourier_table(PP, SUBBOX_HEADINGS, 0.0) * np.float32(SUBBOX_HEADINGS / PP)
    ).astype(BF16)
    cos_np, sin_np = shift_tables()
    cos_t, sin_t = jnp.asarray(cos_np), jnp.asarray(sin_np)

    box, angle = lax.axis_index("box"), lax.axis_index("angle")
    core = angle % 2
    mine = jnp.where(core == 0, box // SIDE, box % SIDE)
    other = jnp.where(core == 0, box % SIDE, box // SIDE)
    where = jnp.stack([core, mine, other]).astype(I32)

    whole = swap(child_field, "angle").reshape(8, 8, 2, 8, 128)
    parents = swap(lift(whole, tuple(map(hold, (theta_up, phi_up, cos_t, sin_t)))), "angle")
    wanted, child_code, parent_code = plan(
        where, child_list, child_op, child_home, parent_list, parent_op, parent_home
    )
    own = jnp.concatenate([child_field.reshape(128, 8, 128), parents.reshape(128, 8, 128)])
    up2, down2 = hop(own, 2), hop(own, -2)
    up1, down1 = hop(own, 1), hop(own, -1)
    onward = jnp.where(mine % 2 == 0, up2, down2)
    pairs = [(g[i], g[(i + 2 - 4 * (i % 2)) % SIDE]) for g in SPREAD for i in range(SIDE)]
    up4 = lax.ppermute(onward, BOTH, pairs)
    up3, down3 = hop(up2, 1), hop(down2, -1)
    blocks = [own, down1, down2, down3, up4, up3, up2, up1]
    asked = swap(wanted.reshape(SIDE, 1, 128), BOTH, axis_index_groups=TRADE).reshape(SIDE, 128)
    parents_out, *children_out = select(where, asked, blocks)
    parents_in = swap(parents_out, BOTH, axis_index_groups=TRADE)
    children_in = {0: children_out[0]}
    for d in (4, 3, 5, 2, 6, 1, 7):
        children_in[d] = hop(children_out[d], d, TRADE)
    sums = far_parents(hold(parent_code), parents_in.reshape(128, 8, 8, 128), parent_ops)
    turned = swap(sums, "angle").reshape(8, 2, 8, 8, 128)
    term = lower(turned, (theta_down, hold(phi_down), cos_t, sin_t))
    term = swap(term, "angle").reshape(64, 2, 8, 128)
    child_far = far_children(hold(child_code), [children_in[d] for d in range(SIDE)], child_ops)
    return (child_far + term.astype(F32)).astype(BF16)


def solution(mesh):
    return jax.shard_map(
        local,
        mesh=mesh,
        in_specs=(
            P("box", None, "angle", None),
            P("box", None),
            P("box", None),
            P(),
            P(None, None, "angle", None),
            P("box", None),
            P("box", None),
            P(),
            P(None, None, "angle", None),
        ),
        out_specs=P("box", None, "angle", None),
        check_vma=False,
    )
```

```python
import math

import jax
import jax.numpy as jnp
import numpy as np
from jax import lax
from jax.experimental import pallas as pl
from jax.experimental.pallas import tpu as pltpu
from jax.sharding import PartitionSpec as P


CT = 64
SUBBOX_HEADINGS = 128
PT = 128
PP = 256
WAVE_NUMBER = 6.0
SIDE = 8
ORDER = (4, 3, 5, 2, 6, 1, 7)
BOTH = ("box", "angle")
F32, BF16, I32 = jnp.float32, jnp.bfloat16, jnp.int32
VM = pltpu.VMEM
ANY = pl.ANY
GRANT = 12 << 20


def fourier_table(fine_count, coarse_count, offset):
    f32 = np.float32
    fine = (np.arange(fine_count, dtype=f32) + f32(offset)) / f32(fine_count)
    coarse = (np.arange(coarse_count, dtype=f32) + f32(offset)) / f32(coarse_count)
    x = fine[:, None] - coarse[None, :]
    harmonic = np.arange(1, coarse_count // 2, dtype=f32)
    cosines = np.cos(f32(2.0 * math.pi) * harmonic * x[:, :, None])
    summed = f32(1.0) + f32(2.0) * cosines.sum(2, dtype=np.float64) + np.cos(f32(math.pi * coarse_count) * x)
    return (summed / coarse_count).astype(f32)


def shift_tables():
    f32 = np.float32
    polar = (f32(math.pi) * (np.arange(PT, dtype=f32) + f32(0.5)) / f32(PT)).astype(f32)
    heading = (f32(2.0 * math.pi / PP) * np.arange(PP, dtype=f32)).astype(f32)
    cos_h, sin_h = np.cos(heading), np.sin(heading)
    across = np.stack([-cos_h - sin_h, cos_h - sin_h])
    arg = (f32(WAVE_NUMBER) * np.sin(polar))[None, :, None] * across[:, None, :]
    return np.cos(arg).astype(f32), np.sin(arg).astype(f32)


def hold(x):
    return pltpu.with_memory_space_constraint(x, pltpu.HBM)


def bmm(a, b):
    return lax.dot_general(a, b, (((1,), (0,)), ((), ())), preferred_element_type=F32)


def iota(shape, dim):
    return lax.broadcasted_iota(I32, shape, dim)


def plan_level(ids_ref, op_ref, home_ref, core, mine, other, rows_device, cap, empty_op, code_ref):
    slots, rows = ids_ref.shape
    home = home_ref[...]
    owner = home // rows_device
    table = jnp.concatenate([owner, home - owner * rows_device], axis=0).astype(F32).astype(BF16)
    highs = home.shape[0]
    before = (iota((rows, rows), 0) < iota((rows, rows), 1)).astype(F32).astype(BF16)
    carry = jnp.zeros((SIDE, 1), F32)
    wanted = jnp.zeros((2 * SIDE, cap), F32)
    for j in range(slots):
        ids = ids_ref[pl.ds(j, 1), :]
        usable = ids >= 0
        safe = jnp.maximum(ids, 0)
        high, low = safe >> 7, safe & 127
        low_hot = (iota((128, rows), 0) == low).astype(F32).astype(BF16)
        picked = bmm(table, low_hot)
        high_hot = (iota((highs, rows), 0) == high).astype(F32)
        own = jnp.sum(picked[:highs] * high_hot, axis=0, keepdims=True).astype(I32)
        loc = jnp.sum(picked[highs:] * high_hot, axis=0, keepdims=True)
        along_y, along_z = own >> 3, own & 7
        column = jnp.where(core == 0, along_z, along_y)
        place = (jnp.where(core == 0, along_y, along_z) - mine) & 7
        hot = jnp.where((iota((SIDE, rows), 0) == column) & usable, 1.0, 0.0)
        hot_b = hot.astype(BF16)
        prefix = bmm(hot_b, before) + carry
        carry = carry + jnp.sum(hot, axis=1, keepdims=True)
        rank = jnp.sum(hot * prefix, axis=0, keepdims=True).astype(I32)
        lane = column if other is None else (other - column) & 7
        position = lane * cap + rank
        code_ref[pl.ds(j, 1), pl.ds(0, rows)] = jnp.where(
            usable, position * 64 + op_ref[pl.ds(j, 1), :], empty_op
        )
        rank_hot = (iota((cap, rows), 0) == rank).astype(F32).astype(BF16)
        both = jnp.concatenate([hot * place.astype(F32), hot * loc], axis=0).astype(BF16)
        wanted = wanted + lax.dot_general(
            both, rank_hot, (((1,), (1,)), ((), ())), preferred_element_type=F32
        )
    return (wanted[:SIDE] * rows_device + wanted[SIDE:]).astype(I32)


def plan_body(where, cl, co, ch, plist, po, ph, want_ref, ccode_ref, pcode_ref):
    core, mine, other = where[0], where[1], where[2]
    want_ref[...] = jnp.zeros(want_ref.shape, I32)
    want_ref[:, pl.ds(0, 64)] = plan_level(cl, co, ch, core, mine, other, 64, 64, 40, ccode_ref)
    want_ref[:, pl.ds(64, 16)] = plan_level(plist, po, ph, core, mine, None, 16, 16, 40, pcode_ref)


def plan(where, child_list, child_op, child_home, parent_list, parent_op, parent_home):
    args = (
        where,
        *map(
            hold,
            (
                child_list.T,
                child_op.T,
                child_home.reshape(-1, 128),
                parent_list.T,
                parent_op.T,
                parent_home.reshape(-1, 128),
            ),
        ),
    )
    return pl.pallas_call(
        plan_body,
        out_shape=(
            jax.ShapeDtypeStruct((SIDE, 128), I32),
            pltpu.HBM((8, 64), I32),
            pltpu.HBM((8, 16), I32),
        ),
        in_specs=[pl.BlockSpec(memory_space=pltpu.SMEM)] + [pl.BlockSpec(memory_space=VM)] * 6,
        out_specs=(pl.BlockSpec(memory_space=VM),) * 3,
        compiler_params=pltpu.CompilerParams(vmem_limit_bytes=GRANT),
        name="plan",
    )(*args)


def up_body(field, theta_h, phi_h, cos_h, sin_h, out, theta, phi, cos_t, sin_t, wide, sems):
    copies = fetch((theta_h, phi_h, cos_h, sin_h), (theta, phi, cos_t, sin_t), sems)
    copies[0].wait()
    copies[1].wait()
    for i in range(4):
        rows = jnp.concatenate(
            [
                jnp.concatenate([field[s, (i * 4 + k) // 2, k % 2] for s in range(8)], axis=0)
                for k in range(4)
            ],
            axis=1,
        )
        stretched = bmm(theta[...], rows).astype(BF16)
        tall = jnp.concatenate([stretched[:, k * 128 : k * 128 + 128] for k in range(4)], axis=0)
        spread = bmm(tall, phi[...])
        for k in range(4):
            wide[i * 4 + k] = spread[k * PT : (k + 1) * PT]
    copies[2].wait()
    copies[3].wait()
    for q in range(2):
        for u in range(PT // 8):
            at = pl.ds(u * 8, 8)
            w = [[wide[(q * 4 + k) * 2 + c, at, :] for c in range(2)] for k in range(4)]
            real = jnp.zeros((8, PP), F32)
            imag = jnp.zeros((8, PP), F32)
            for t, (k, m) in enumerate(((0, 3), (1, 2))):
                cs, sn = cos_t[t, at, :], sin_t[t, at, :]
                real = real + cs * (w[k][0] + w[m][0]) - sn * (w[k][1] - w[m][1])
                imag = imag + cs * (w[k][1] + w[m][1]) + sn * (w[k][0] - w[m][0])
            for c, part in enumerate((real, imag)):
                part = part.astype(BF16)
                for v in range(2):
                    out[u // 2, q, c * 4 + (u % 2) * 2 + v] = part[:, v * 128 : (v + 1) * 128]


def fetch(sources, targets, sems):
    copies = [pltpu.make_async_copy(a, b, sems.at[i]) for i, (a, b) in enumerate(zip(sources, targets))]
    for copy in copies:
        copy.start()
    return copies


def lift(field, tables):
    return pl.pallas_call(
        up_body,
        out_shape=jax.ShapeDtypeStruct((8, 2, 8, 8, 128), BF16),
        in_specs=[pl.BlockSpec(memory_space=VM)] + [pl.BlockSpec(memory_space=pltpu.HBM)] * 4,
        out_specs=pl.BlockSpec(memory_space=VM),
        scratch_shapes=[pltpu.VMEM(t.shape, t.dtype) for t in tables]
        + [pltpu.VMEM((16, PT, PP), F32), pltpu.SemaphoreType.DMA((4,))],
        compiler_params=pltpu.CompilerParams(vmem_limit_bytes=GRANT),
        name="lift",
    )(field, *tables)


def select_body(where, asked, *refs):
    blocks, parents, children = refs[:8], refs[8], refs[9:17]
    pool, parent_buf, child_buf, sems, parent_sems, child_sems = refs[17:]
    copies = [
        pltpu.make_async_copy(
            b.at[pl.ds(128 * half, 128)], pool.at[half, pl.ds(128 * i, 128)], sems.at[half, i]
        )
        for half in (1, 0)
        for i, b in enumerate(blocks)
    ]
    for copy in copies:
        copy.start()

    def child_out(d):
        return pltpu.make_async_copy(child_buf.at[d], children[d], child_sems.at[d])

    def parent_out(h):
        return pltpu.make_async_copy(parent_buf.at[h], parents.at[h], parent_sems.at[h])

    for copy in copies[:8]:
        copy.wait()

    def peer(h, carry):
        for k in range(16):
            at = pl.multiple_of(asked[h, 64 + k] * 8, 8)
            parent_buf[h, k] = pool[1, pl.ds(at, 8)]
        parent_out(h).start()
        return carry

    lax.fori_loop(0, SIDE, peer, 0)
    for copy in copies[8:]:
        copy.wait()
    for d in range(SIDE):
        h = (where[2] + d) & 7

        def some(i, carry):
            for j in range(16):
                k = i * 16 + j
                at = pl.multiple_of(asked[h, k] * 2, 2)
                child_buf[d, k] = pool[0, pl.ds(at, 2)]
            return carry

        lax.fori_loop(0, 4, some, 0)
        child_out(d).start()
    for h in range(SIDE):
        parent_out(h).wait()
    for d in range(SIDE):
        child_out(d).wait()


def select(where, asked, blocks):
    hbm = pl.BlockSpec(memory_space=pltpu.HBM)
    return pl.pallas_call(
        select_body,
        out_shape=(pltpu.HBM((SIDE, 16, 8, 8, 128), BF16),) + (pltpu.HBM((64, 2, 8, 128), BF16),) * SIDE,
        in_specs=[pl.BlockSpec(memory_space=pltpu.SMEM)] * 2 + [pl.BlockSpec(memory_space=ANY)] * 8,
        out_specs=(hbm,) * 9,
        scratch_shapes=[
            pltpu.VMEM((2, 8 * 128, 8, 128), BF16),
            pltpu.VMEM((SIDE, 16, 8, 8, 128), BF16),
            pltpu.VMEM((SIDE, 64, 2, 8, 128), BF16),
            pltpu.SemaphoreType.DMA((2, 8)),
            pltpu.SemaphoreType.DMA((8,)),
            pltpu.SemaphoreType.DMA((8,)),
        ],
        compiler_params=pltpu.CompilerParams(vmem_limit_bytes=GRANT),
        name="select",
    )(where, asked, *blocks)


def parent_far_body(code, recv, ops_hbm, out, ops, sem):
    copy = pltpu.make_async_copy(ops_hbm, ops.at[pl.ds(0, 40)], sem)
    copy.start()
    ops[40] = jnp.zeros(ops.shape[1:], BF16)
    copy.wait()

    def row(r, carry):
        real = [jnp.zeros((8, 128), F32) for _ in range(4)]
        imag = [jnp.zeros((8, 128), F32) for _ in range(4)]
        for j in range(8):
            both = code[j, r]
            at, op = both >> 6, both & 63
            for t in range(4):
                u, v = t // 2, t % 2
                a = ops[op, 0, u * 8 : u * 8 + 8, v * 128 : v * 128 + 128].astype(F32)
                b = ops[op, 1, u * 8 : u * 8 + 8, v * 128 : v * 128 + 128].astype(F32)
                c = recv[at, t].astype(F32)
                d = recv[at, 4 + t].astype(F32)
                real[t] = real[t] + (a * c - b * d)
                imag[t] = imag[t] + (a * d + b * c)
        for t in range(4):
            out[r, t] = real[t].astype(BF16)
            out[r, 4 + t] = imag[t].astype(BF16)
        return carry

    lax.fori_loop(0, 16, row, 0)


def far_parents(code, recv, ops):
    return pl.pallas_call(
        parent_far_body,
        out_shape=jax.ShapeDtypeStruct((16, 8, 8, 128), BF16),
        in_specs=[
            pl.BlockSpec(memory_space=pltpu.SMEM),
            pl.BlockSpec(memory_space=VM),
            pl.BlockSpec(memory_space=ANY),
        ],
        out_specs=pl.BlockSpec(memory_space=VM),
        scratch_shapes=[pltpu.VMEM((41, 2, 16, PP), BF16), pltpu.SemaphoreType.DMA],
        compiler_params=pltpu.CompilerParams(vmem_limit_bytes=GRANT),
        name="far_parents",
    )(code, recv, ops)


def child_far_body(code, *refs):
    blocks, ops_hbm, out, recv, ops, wide, sems = refs[:8], *refs[8:]
    copies = fetch((ops_hbm, *blocks), (ops, *(recv.at[pl.ds(64 * i, 64)] for i in range(8))), sems)
    copies[0].wait()
    for i in range(40):
        wide[i] = ops[i].astype(F32)
    wide[40] = jnp.zeros(wide.shape[1:], F32)
    for copy in copies[1:]:
        copy.wait()

    def row(r, carry):
        real = jnp.zeros((8, 128), F32)
        imag = jnp.zeros((8, 128), F32)
        for j in range(8):
            both = code[j, r]
            at, op = both >> 6, both & 63
            a, b = wide[op, 0], wide[op, 1]
            c, d = recv[at, 0].astype(F32), recv[at, 1].astype(F32)
            real = real + (a * c - b * d)
            imag = imag + (a * d + b * c)
        out[r, 0] = real
        out[r, 1] = imag
        return carry

    lax.fori_loop(0, 64, row, 0, unroll=2)


def far_children(code, blocks, ops):
    return pl.pallas_call(
        child_far_body,
        out_shape=jax.ShapeDtypeStruct((64, 2, 8, 128), F32),
        in_specs=[pl.BlockSpec(memory_space=pltpu.SMEM)] + [pl.BlockSpec(memory_space=ANY)] * 9,
        out_specs=pl.BlockSpec(memory_space=VM),
        scratch_shapes=[
            pltpu.VMEM((SIDE * 64, 2, 8, 128), BF16),
            pltpu.VMEM((40, 2, 8, 128), BF16),
            pltpu.VMEM((41, 2, 8, 128), F32),
            pltpu.SemaphoreType.DMA((9,)),
        ],
        compiler_params=pltpu.CompilerParams(vmem_limit_bytes=GRANT),
        name="far_children",
    )(code, *blocks, ops)


def down_body(far, theta, phi_h, cos_t, sin_t, out, phi, turned, thin, sem):
    copy = pltpu.make_async_copy(phi_h, phi, sem)
    copy.start()
    for q in range(2):
        for u in range(PT // 8):
            at = pl.ds(u * 8, 8)
            re, im = (
                jnp.concatenate(
                    [far[u // 2, q, c * 4 + (u % 2) * 2 + v].astype(F32) for v in range(2)], axis=1
                )
                for c in range(2)
            )
            for t, (k, m) in enumerate(((0, 3), (1, 2))):
                cs, sn = cos_t[t, at, :], sin_t[t, at, :]
                cr, si, ci, sr = cs * re, sn * im, cs * im, sn * re
                turned[(q * 4 + k) * 2, at, :] = (cr + si).astype(BF16)
                turned[(q * 4 + k) * 2 + 1, at, :] = (ci - sr).astype(BF16)
                turned[(q * 4 + m) * 2, at, :] = (cr - si).astype(BF16)
                turned[(q * 4 + m) * 2 + 1, at, :] = (ci + sr).astype(BF16)
    copy.wait()
    for i in range(4):
        tall = jnp.concatenate([turned[i * 4 + k] for k in range(4)], axis=0)
        narrowed = bmm(tall, phi[...]).astype(BF16)
        for k in range(4):
            at = (i * 4 + k) * SUBBOX_HEADINGS
            thin[:, at : at + SUBBOX_HEADINGS] = narrowed[k * PT : (k + 1) * PT]
    for i in range(4):
        term = bmm(theta[...], thin[:, i * 512 : i * 512 + 512]).astype(BF16)
        for k in range(4):
            for s in range(8):
                out[s, (i * 4 + k) // 2, k % 2] = term[s * 8 : s * 8 + 8, k * 128 : k * 128 + 128]


def lower(far, tables):
    return pl.pallas_call(
        down_body,
        out_shape=jax.ShapeDtypeStruct((8, 8, 2, 8, 128), BF16),
        in_specs=[pl.BlockSpec(memory_space=ANY if i == 2 else VM) for i in range(5)],
        out_specs=pl.BlockSpec(memory_space=VM),
        scratch_shapes=[
            pltpu.VMEM(tables[1].shape, BF16),
            pltpu.VMEM((16, PT, PP), BF16),
            pltpu.VMEM((PT, 16 * SUBBOX_HEADINGS), BF16),
            pltpu.SemaphoreType.DMA,
        ],
        compiler_params=pltpu.CompilerParams(vmem_limit_bytes=GRANT),
        name="lower",
    )(far, *tables)


def groups(straight):
    found = []
    for angle in range(8):
        for o in range(SIDE):
            line = [(o, i) if (angle % 2) == straight else (i, o) for i in range(SIDE)]
            found.append([(y * SIDE + z) * 8 + angle for y, z in line])
    return found


SPREAD, TRADE = groups(1), groups(0)


def hop(x, step, lines=SPREAD):
    pairs = [(g[i], g[(i + step) % SIDE]) for g in lines for i in range(SIDE)]
    return lax.ppermute(x, BOTH, pairs)


def swap(x, axis, **kw):
    return lax.all_to_all(x, axis, split_axis=0, concat_axis=0, tiled=True, **kw)


def local(
    child_field,
    child_list,
    child_op,
    child_home,
    child_ops,
    parent_list,
    parent_op,
    parent_home,
    parent_ops,
):
    theta_up = jnp.asarray(fourier_table(PT, CT, 0.5)).astype(BF16)
    phi_up = jnp.asarray(np.ascontiguousarray(fourier_table(PP, SUBBOX_HEADINGS, 0.0).T)).astype(BF16)
    theta_down = jnp.asarray(np.ascontiguousarray(fourier_table(PT, CT, 0.5).T) * np.float32(CT / PT)).astype(BF16)
    phi_down = jnp.asarray(
        fourier_table(PP, SUBBOX_HEADINGS, 0.0) * np.float32(SUBBOX_HEADINGS / PP)
    ).astype(BF16)
    cos_np, sin_np = shift_tables()
    cos_t, sin_t = jnp.asarray(cos_np), jnp.asarray(sin_np)

    box, angle = lax.axis_index("box"), lax.axis_index("angle")
    core = angle % 2
    mine = jnp.where(core == 0, box // SIDE, box % SIDE)
    other = jnp.where(core == 0, box % SIDE, box // SIDE)
    where = jnp.stack([core, mine, other]).astype(I32)

    whole = swap(child_field, "angle").reshape(8, 8, 2, 8, 128)
    parents = swap(lift(whole, tuple(map(hold, (theta_up, phi_up, cos_t, sin_t)))), "angle")
    wanted, child_code, parent_code = plan(
        where, child_list, child_op, child_home, parent_list, parent_op, parent_home
    )
    own = jnp.concatenate([child_field.reshape(128, 8, 128), parents.reshape(128, 8, 128)])
    up2, down2 = hop(own, 2), hop(own, -2)
    up1, down1 = hop(own, 1), hop(own, -1)
    onward = jnp.where(mine % 2 == 0, up2, down2)
    pairs = [(g[i], g[(i + 2 - 4 * (i % 2)) % SIDE]) for g in SPREAD for i in range(SIDE)]
    up4 = lax.ppermute(onward, BOTH, pairs)
    up3, down3 = hop(up2, 1), hop(down2, -1)
    blocks = [own, down1, down2, down3, up4, up3, up2, up1]
    asked = swap(wanted.reshape(SIDE, 1, 128), BOTH, axis_index_groups=TRADE).reshape(SIDE, 128)
    parents_out, *children_out = select(where, asked, blocks)
    parents_in = swap(parents_out, BOTH, axis_index_groups=TRADE)
    children_in = {0: children_out[0]}
    for d in ORDER:
        children_in[d] = hop(children_out[d], d, TRADE)
    sums = far_parents(hold(parent_code), parents_in.reshape(128, 8, 8, 128), parent_ops)
    turned = swap(sums, "angle").reshape(8, 2, 8, 8, 128)
    term = lower(turned, (theta_down, hold(phi_down), cos_t, sin_t))
    term = swap(term, "angle").reshape(64, 2, 8, 128)
    child_far = far_children(hold(child_code), [children_in[d] for d in range(SIDE)], child_ops)
    return (child_far + term.astype(F32)).astype(BF16)


def solution(mesh):
    return jax.shard_map(
        local,
        mesh=mesh,
        in_specs=(
            P("box", None, "angle", None),
            P("box", None),
            P("box", None),
            P(),
            P(None, None, "angle", None),
            P("box", None),
            P("box", None),
            P(),
            P(None, None, "angle", None),
        ),
        out_specs=P("box", None, "angle", None),
        check_vma=False,
    )
```

```python
import math

import jax
import jax.numpy as jnp
import numpy as np
from jax import lax
from jax.experimental import pallas as pl
from jax.experimental.pallas import tpu as pltpu
from jax.sharding import PartitionSpec as P


CT = 64
SUBBOX_HEADINGS = 128
PT = 128
PP = 256
WAVE_NUMBER = 6.0
SIDE = 8
BOTH = ("box", "angle")
F32, BF16, I32 = jnp.float32, jnp.bfloat16, jnp.int32
VM = pltpu.VMEM
ANY = pl.ANY
GRANT = 12 << 20


def fourier_table(fine_count, coarse_count, offset):
    f32 = np.float32
    fine = (np.arange(fine_count, dtype=f32) + f32(offset)) / f32(fine_count)
    coarse = (np.arange(coarse_count, dtype=f32) + f32(offset)) / f32(coarse_count)
    x = fine[:, None] - coarse[None, :]
    harmonic = np.arange(1, coarse_count // 2, dtype=f32)
    cosines = np.cos(f32(2.0 * math.pi) * harmonic * x[:, :, None])
    summed = f32(1.0) + f32(2.0) * cosines.sum(2, dtype=np.float64) + np.cos(f32(math.pi * coarse_count) * x)
    return (summed / coarse_count).astype(f32)


def shift_tables():
    f32 = np.float32
    polar = (f32(math.pi) * (np.arange(PT, dtype=f32) + f32(0.5)) / f32(PT)).astype(f32)
    heading = (f32(2.0 * math.pi / PP) * np.arange(PP, dtype=f32)).astype(f32)
    cos_h, sin_h = np.cos(heading), np.sin(heading)
    across = np.stack([-cos_h - sin_h, cos_h - sin_h])
    arg = (f32(WAVE_NUMBER) * np.sin(polar))[None, :, None] * across[:, None, :]
    return np.cos(arg).astype(f32), np.sin(arg).astype(f32)


def hold(x):
    return pltpu.with_memory_space_constraint(x, pltpu.HBM)


def bmm(a, b):
    return lax.dot_general(a, b, (((1,), (0,)), ((), ())), preferred_element_type=F32)


def iota(shape, dim):
    return lax.broadcasted_iota(I32, shape, dim)


def plan_level(ids_ref, op_ref, home_ref, core, mine, other, rows_device, cap, empty_op, code_ref):
    slots, rows = ids_ref.shape
    home = home_ref[...]
    owner = home // rows_device
    table = jnp.concatenate([owner, home - owner * rows_device], axis=0).astype(F32).astype(BF16)
    highs = home.shape[0]
    before = (iota((rows, rows), 0) < iota((rows, rows), 1)).astype(F32).astype(BF16)
    share = cap // SIDE
    carry = jnp.zeros((SIDE * SIDE, 1), F32)
    wanted = jnp.zeros((SIDE, cap), F32)
    for j in range(slots):
        ids = ids_ref[pl.ds(j, 1), :]
        usable = ids >= 0
        safe = jnp.maximum(ids, 0)
        high, low = safe >> 7, safe & 127
        low_hot = (iota((128, rows), 0) == low).astype(F32).astype(BF16)
        picked = bmm(table, low_hot)
        high_hot = (iota((highs, rows), 0) == high).astype(F32)
        own = jnp.sum(picked[:highs] * high_hot, axis=0, keepdims=True).astype(I32)
        loc = jnp.sum(picked[highs:] * high_hot, axis=0, keepdims=True)
        along_y, along_z = own >> 3, own & 7
        column = jnp.where(core == 0, along_z, along_y)
        place = (jnp.where(core == 0, along_y, along_z) - mine) & 7
        hot = jnp.where((iota((SIDE, rows), 0) == column) & usable, 1.0, 0.0)
        holder = column * SIDE + place
        fine = jnp.where((iota((SIDE * SIDE, rows), 0) == holder) & usable, 1.0, 0.0)
        prefix = bmm(fine.astype(BF16), before) + carry
        carry = carry + jnp.sum(fine, axis=1, keepdims=True)
        rank = jnp.sum(fine * prefix, axis=0, keepdims=True).astype(I32)
        slot = place * share + rank
        lane = column if other is None else (other - column) & 7
        position = lane * cap + slot
        code_ref[pl.ds(j, 1), pl.ds(0, rows)] = jnp.where(
            usable, position * 64 + op_ref[pl.ds(j, 1), :], empty_op
        )
        slot_hot = (iota((cap, rows), 0) == slot).astype(F32).astype(BF16)
        wanted = wanted + lax.dot_general(
            (hot * loc).astype(BF16), slot_hot, (((1,), (1,)), ((), ())), preferred_element_type=F32
        )
    return wanted.astype(I32)


def plan_body(where, cl, co, ch, plist, po, ph, want_ref, ccode_ref, pcode_ref):
    core, mine, other = where[0], where[1], where[2]
    want_ref[...] = jnp.zeros(want_ref.shape, I32)
    want_ref[:, pl.ds(0, 64)] = plan_level(cl, co, ch, core, mine, other, 64, 64, 40, ccode_ref)
    want_ref[:, pl.ds(64, 16)] = plan_level(plist, po, ph, core, mine, None, 16, 16, 40, pcode_ref)


def plan(where, child_list, child_op, child_home, parent_list, parent_op, parent_home):
    args = (
        where,
        *map(
            hold,
            (
                child_list.T,
                child_op.T,
                child_home.reshape(-1, 128),
                parent_list.T,
                parent_op.T,
                parent_home.reshape(-1, 128),
            ),
        ),
    )
    return pl.pallas_call(
        plan_body,
        out_shape=(
            jax.ShapeDtypeStruct((SIDE, 128), I32),
            pltpu.HBM((8, 64), I32),
            pltpu.HBM((8, 16), I32),
        ),
        in_specs=[pl.BlockSpec(memory_space=pltpu.SMEM)] + [pl.BlockSpec(memory_space=VM)] * 6,
        out_specs=(pl.BlockSpec(memory_space=VM),) * 3,
        compiler_params=pltpu.CompilerParams(vmem_limit_bytes=GRANT),
        name="plan",
    )(*args)


def up_body(field, theta_h, phi_h, cos_h, sin_h, out, theta, phi, cos_t, sin_t, wide, sems):
    copies = fetch((theta_h, phi_h, cos_h, sin_h), (theta, phi, cos_t, sin_t), sems)
    copies[0].wait()
    copies[1].wait()
    for i in range(4):
        rows = jnp.concatenate(
            [
                jnp.concatenate([field[s, (i * 4 + k) // 2, k % 2] for s in range(8)], axis=0)
                for k in range(4)
            ],
            axis=1,
        )
        stretched = bmm(theta[...], rows).astype(BF16)
        tall = jnp.concatenate([stretched[:, k * 128 : k * 128 + 128] for k in range(4)], axis=0)
        spread = bmm(tall, phi[...])
        for k in range(4):
            wide[i * 4 + k] = spread[k * PT : (k + 1) * PT]
    copies[2].wait()
    copies[3].wait()
    for q in range(2):
        for u in range(PT // 8):
            at = pl.ds(u * 8, 8)
            w = [[wide[(q * 4 + k) * 2 + c, at, :] for c in range(2)] for k in range(4)]
            real = jnp.zeros((8, PP), F32)
            imag = jnp.zeros((8, PP), F32)
            for t, (k, m) in enumerate(((0, 3), (1, 2))):
                cs, sn = cos_t[t, at, :], sin_t[t, at, :]
                real = real + cs * (w[k][0] + w[m][0]) - sn * (w[k][1] - w[m][1])
                imag = imag + cs * (w[k][1] + w[m][1]) + sn * (w[k][0] - w[m][0])
            for c, part in enumerate((real, imag)):
                part = part.astype(BF16)
                for v in range(2):
                    out[u // 2, q, c * 4 + (u % 2) * 2 + v] = part[:, v * 128 : (v + 1) * 128]


def fetch(sources, targets, sems):
    copies = [pltpu.make_async_copy(a, b, sems.at[i]) for i, (a, b) in enumerate(zip(sources, targets))]
    for copy in copies:
        copy.start()
    return copies


def lift(field, tables):
    return pl.pallas_call(
        up_body,
        out_shape=jax.ShapeDtypeStruct((8, 2, 8, 8, 128), BF16),
        in_specs=[pl.BlockSpec(memory_space=VM)] + [pl.BlockSpec(memory_space=pltpu.HBM)] * 4,
        out_specs=pl.BlockSpec(memory_space=VM),
        scratch_shapes=[pltpu.VMEM(t.shape, t.dtype) for t in tables]
        + [pltpu.VMEM((16, PT, PP), F32), pltpu.SemaphoreType.DMA((4,))],
        compiler_params=pltpu.CompilerParams(vmem_limit_bytes=GRANT),
        name="lift",
    )(field, *tables)


def select_body(where, asked, *refs):
    blocks, parents, children = refs[:8], refs[8], refs[9:17]
    parent_buf, child_buf, parent_sems, child_sems = refs[17:]

    def child_out(d):
        return pltpu.make_async_copy(child_buf.at[d], children[d], child_sems.at[d])

    def parent_out(h):
        return pltpu.make_async_copy(parent_buf.at[h], parents.at[h], parent_sems.at[h])

    def peer(h, carry):
        for k in range(16):
            at = pl.multiple_of(128 + asked[h, 64 + k] * 8, 8)
            parent_buf[h, k] = blocks[k // 2][pl.ds(at, 8)]
        parent_out(h).start()
        return carry

    lax.fori_loop(0, SIDE, peer, 0)
    for d in range(SIDE):
        h = (where[2] + d) & 7
        for k in range(64):
            at = pl.multiple_of(asked[h, k] * 2, 2)
            child_buf[d, k] = blocks[k // 8][pl.ds(at, 2)]
        child_out(d).start()
    for h in range(SIDE):
        parent_out(h).wait()
    for d in range(SIDE):
        child_out(d).wait()


def select(where, asked, blocks):
    hbm = pl.BlockSpec(memory_space=pltpu.HBM)
    return pl.pallas_call(
        select_body,
        out_shape=(pltpu.HBM((SIDE, 16, 8, 8, 128), BF16),) + (pltpu.HBM((64, 2, 8, 128), BF16),) * SIDE,
        in_specs=[pl.BlockSpec(memory_space=pltpu.SMEM)] * 2 + [pl.BlockSpec(memory_space=VM)] * 8,
        out_specs=(hbm,) * 9,
        scratch_shapes=[
            pltpu.VMEM((SIDE, 16, 8, 8, 128), BF16),
            pltpu.VMEM((SIDE, 64, 2, 8, 128), BF16),
            pltpu.SemaphoreType.DMA((8,)),
            pltpu.SemaphoreType.DMA((8,)),
        ],
        compiler_params=pltpu.CompilerParams(vmem_limit_bytes=GRANT),
        name="select",
    )(where, asked, *blocks)


def parent_far_body(code, recv, ops_hbm, out, ops, sem):
    copy = pltpu.make_async_copy(ops_hbm, ops.at[pl.ds(0, 40)], sem)
    copy.start()
    ops[40] = jnp.zeros(ops.shape[1:], BF16)
    copy.wait()

    def row(r, carry):
        real = [jnp.zeros((8, 128), F32) for _ in range(4)]
        imag = [jnp.zeros((8, 128), F32) for _ in range(4)]
        for j in range(8):
            both = code[j, r]
            at, op = both >> 6, both & 63
            for t in range(4):
                u, v = t // 2, t % 2
                a = ops[op, 0, u * 8 : u * 8 + 8, v * 128 : v * 128 + 128].astype(F32)
                b = ops[op, 1, u * 8 : u * 8 + 8, v * 128 : v * 128 + 128].astype(F32)
                c = recv[at, t].astype(F32)
                d = recv[at, 4 + t].astype(F32)
                real[t] = real[t] + (a * c - b * d)
                imag[t] = imag[t] + (a * d + b * c)
        for t in range(4):
            out[r, t] = real[t].astype(BF16)
            out[r, 4 + t] = imag[t].astype(BF16)
        return carry

    lax.fori_loop(0, 16, row, 0)


def far_parents(code, recv, ops):
    return pl.pallas_call(
        parent_far_body,
        out_shape=jax.ShapeDtypeStruct((16, 8, 8, 128), BF16),
        in_specs=[
            pl.BlockSpec(memory_space=pltpu.SMEM),
            pl.BlockSpec(memory_space=VM),
            pl.BlockSpec(memory_space=ANY),
        ],
        out_specs=pl.BlockSpec(memory_space=VM),
        scratch_shapes=[pltpu.VMEM((41, 2, 16, PP), BF16), pltpu.SemaphoreType.DMA],
        compiler_params=pltpu.CompilerParams(vmem_limit_bytes=GRANT),
        name="far_parents",
    )(code, recv, ops)


def child_far_body(code, *refs):
    blocks, ops_hbm, out, recv, ops, wide, sems = refs[:8], *refs[8:]
    copies = fetch((ops_hbm, *blocks), (ops, *(recv.at[pl.ds(64 * i, 64)] for i in range(8))), sems)
    copies[0].wait()
    for i in range(40):
        wide[i] = ops[i].astype(F32)
    wide[40] = jnp.zeros(wide.shape[1:], F32)
    for copy in copies[1:]:
        copy.wait()

    def row(r, carry):
        real = jnp.zeros((8, 128), F32)
        imag = jnp.zeros((8, 128), F32)
        for j in range(8):
            both = code[j, r]
            at, op = both >> 6, both & 63
            a, b = wide[op, 0], wide[op, 1]
            c, d = recv[at, 0].astype(F32), recv[at, 1].astype(F32)
            real = real + (a * c - b * d)
            imag = imag + (a * d + b * c)
        out[r, 0] = real
        out[r, 1] = imag
        return carry

    lax.fori_loop(0, 64, row, 0, unroll=2)


def far_children(code, blocks, ops):
    return pl.pallas_call(
        child_far_body,
        out_shape=jax.ShapeDtypeStruct((64, 2, 8, 128), F32),
        in_specs=[pl.BlockSpec(memory_space=pltpu.SMEM)] + [pl.BlockSpec(memory_space=ANY)] * 9,
        out_specs=pl.BlockSpec(memory_space=VM),
        scratch_shapes=[
            pltpu.VMEM((SIDE * 64, 2, 8, 128), BF16),
            pltpu.VMEM((40, 2, 8, 128), BF16),
            pltpu.VMEM((41, 2, 8, 128), F32),
            pltpu.SemaphoreType.DMA((9,)),
        ],
        compiler_params=pltpu.CompilerParams(vmem_limit_bytes=GRANT),
        name="far_children",
    )(code, *blocks, ops)


def down_body(far, theta, phi_h, cos_t, sin_t, out, phi, turned, thin, sem):
    copy = pltpu.make_async_copy(phi_h, phi, sem)
    copy.start()
    for q in range(2):
        for u in range(PT // 8):
            at = pl.ds(u * 8, 8)
            re, im = (
                jnp.concatenate(
                    [far[u // 2, q, c * 4 + (u % 2) * 2 + v].astype(F32) for v in range(2)], axis=1
                )
                for c in range(2)
            )
            for t, (k, m) in enumerate(((0, 3), (1, 2))):
                cs, sn = cos_t[t, at, :], sin_t[t, at, :]
                cr, si, ci, sr = cs * re, sn * im, cs * im, sn * re
                turned[(q * 4 + k) * 2, at, :] = (cr + si).astype(BF16)
                turned[(q * 4 + k) * 2 + 1, at, :] = (ci - sr).astype(BF16)
                turned[(q * 4 + m) * 2, at, :] = (cr - si).astype(BF16)
                turned[(q * 4 + m) * 2 + 1, at, :] = (ci + sr).astype(BF16)
    copy.wait()
    for i in range(4):
        tall = jnp.concatenate([turned[i * 4 + k] for k in range(4)], axis=0)
        narrowed = bmm(tall, phi[...]).astype(BF16)
        for k in range(4):
            at = (i * 4 + k) * SUBBOX_HEADINGS
            thin[:, at : at + SUBBOX_HEADINGS] = narrowed[k * PT : (k + 1) * PT]
    for i in range(4):
        term = bmm(theta[...], thin[:, i * 512 : i * 512 + 512]).astype(BF16)
        for k in range(4):
            for s in range(8):
                out[s, (i * 4 + k) // 2, k % 2] = term[s * 8 : s * 8 + 8, k * 128 : k * 128 + 128]


def lower(far, tables):
    return pl.pallas_call(
        down_body,
        out_shape=jax.ShapeDtypeStruct((8, 8, 2, 8, 128), BF16),
        in_specs=[pl.BlockSpec(memory_space=ANY if i == 2 else VM) for i in range(5)],
        out_specs=pl.BlockSpec(memory_space=VM),
        scratch_shapes=[
            pltpu.VMEM(tables[1].shape, BF16),
            pltpu.VMEM((16, PT, PP), BF16),
            pltpu.VMEM((PT, 16 * SUBBOX_HEADINGS), BF16),
            pltpu.SemaphoreType.DMA,
        ],
        compiler_params=pltpu.CompilerParams(vmem_limit_bytes=GRANT),
        name="lower",
    )(far, *tables)


def groups(straight):
    found = []
    for angle in range(8):
        for o in range(SIDE):
            line = [(o, i) if (angle % 2) == straight else (i, o) for i in range(SIDE)]
            found.append([(y * SIDE + z) * 8 + angle for y, z in line])
    return found


SPREAD, TRADE = groups(1), groups(0)


def hop(x, step, lines=SPREAD):
    pairs = [(g[i], g[(i + step) % SIDE]) for g in lines for i in range(SIDE)]
    return lax.ppermute(x, BOTH, pairs)


def swap(x, axis, **kw):
    return lax.all_to_all(x, axis, split_axis=0, concat_axis=0, tiled=True, **kw)


def local(
    child_field,
    child_list,
    child_op,
    child_home,
    child_ops,
    parent_list,
    parent_op,
    parent_home,
    parent_ops,
):
    theta_up = jnp.asarray(fourier_table(PT, CT, 0.5)).astype(BF16)
    phi_up = jnp.asarray(np.ascontiguousarray(fourier_table(PP, SUBBOX_HEADINGS, 0.0).T)).astype(BF16)
    theta_down = jnp.asarray(np.ascontiguousarray(fourier_table(PT, CT, 0.5).T) * np.float32(CT / PT)).astype(BF16)
    phi_down = jnp.asarray(
        fourier_table(PP, SUBBOX_HEADINGS, 0.0) * np.float32(SUBBOX_HEADINGS / PP)
    ).astype(BF16)
    cos_np, sin_np = shift_tables()
    cos_t, sin_t = jnp.asarray(cos_np), jnp.asarray(sin_np)

    box, angle = lax.axis_index("box"), lax.axis_index("angle")
    core = angle % 2
    mine = jnp.where(core == 0, box // SIDE, box % SIDE)
    other = jnp.where(core == 0, box % SIDE, box // SIDE)
    where = jnp.stack([core, mine, other]).astype(I32)

    whole = swap(child_field, "angle").reshape(8, 8, 2, 8, 128)
    parents = swap(lift(whole, tuple(map(hold, (theta_up, phi_up, cos_t, sin_t)))), "angle")
    wanted, child_code, parent_code = plan(
        where, child_list, child_op, child_home, parent_list, parent_op, parent_home
    )
    own = jnp.concatenate([child_field.reshape(128, 8, 128), parents.reshape(128, 8, 128)])
    up2, down2 = hop(own, 2), hop(own, -2)
    up1, down1 = hop(own, 1), hop(own, -1)
    onward = jnp.where(mine % 2 == 0, up2, down2)
    pairs = [(g[i], g[(i + 2 - 4 * (i % 2)) % SIDE]) for g in SPREAD for i in range(SIDE)]
    up4 = lax.ppermute(onward, BOTH, pairs)
    up3, down3 = hop(up2, 1), hop(down2, -1)
    blocks = [own, down1, down2, down3, up4, up3, up2, up1]
    asked = swap(wanted.reshape(SIDE, 1, 128), BOTH, axis_index_groups=TRADE).reshape(SIDE, 128)
    parents_out, *children_out = select(where, asked, blocks)
    parents_in = swap(parents_out, BOTH, axis_index_groups=TRADE)
    children_in = {0: children_out[0]}
    for d in (4, 3, 5, 2, 6, 1, 7):
        children_in[d] = hop(children_out[d], d, TRADE)
    sums = far_parents(hold(parent_code), parents_in.reshape(128, 8, 8, 128), parent_ops)
    turned = swap(sums, "angle").reshape(8, 2, 8, 8, 128)
    term = lower(turned, (theta_down, hold(phi_down), cos_t, sin_t))
    term = swap(term, "angle").reshape(64, 2, 8, 128)
    child_far = far_children(hold(child_code), [children_in[d] for d in range(SIDE)], child_ops)
    return (child_far + term.astype(F32)).astype(BF16)


def solution(mesh):
    return jax.shard_map(
        local,
        mesh=mesh,
        in_specs=(
            P("box", None, "angle", None),
            P("box", None),
            P("box", None),
            P(),
            P(None, None, "angle", None),
            P("box", None),
            P("box", None),
            P(),
            P(None, None, "angle", None),
        ),
        out_specs=P("box", None, "angle", None),
        check_vma=False,
    )
```
